32 devices in a mesh: dp: 2 (over core), fsdp: 16 (over z, y, x).
Axes of the slice: x: 2, y: 2, z: 4, core: 2. Of those that a mesh axis runs over, the one named last changes fastest.
Arguments:
- hidden: bfloat16 [32768, 768], P(('dp', 'fsdp')), may hold values from -6 to 6
- gain_attn: bfloat16 [768], P('fsdp'), may hold values from 0.5 to 1.5
- rel_table: bfloat16 [384], P('fsdp'), may hold values from -4 to 4
- query_weight: bfloat16 [768, 768], P('fsdp'), may hold values from -0.0546875 to 0.0546875
- key_weight: bfloat16 [768, 768], P('fsdp'), may hold values from -0.21875 to 0.21875
- value_weight: bfloat16 [768, 768], P('fsdp'), may hold values from -0.21875 to 0.21875
- output_weight: bfloat16 [768, 768], P('fsdp'), may hold values from -0.625 to 0.625
- gain_ffn: bfloat16 [768], P('fsdp'), may hold values from 0.5 to 1.5
- inner_weight: bfloat16 [768, 3072], P('fsdp'), may hold values from -0.21875 to 0.21875
- outer_weight: bfloat16 [3072, 768], P('fsdp'), may hold values from -0.109375 to 0.109375
- lengths: int32 [160], P(('dp', 'fsdp')), may hold values from 33 to 512, as said below
- cotangent: bfloat16 [32768, 768], P(('dp', 'fsdp')), may hold values from -6 to 6
Outputs:
- result: float32 [32768, 768], P(('dp', 'fsdp'))
- grad_hidden: float32 [32768, 768], P(('dp', 'fsdp'))
- grad_gain_attn: float32 [768], P('fsdp')
- grad_rel_table: float32 [384], P('fsdp')
- grad_query_weight: float32 [768, 768], P('fsdp')
- grad_key_weight: float32 [768, 768], P('fsdp')
- grad_value_weight: float32 [768, 768], P('fsdp')
- grad_output_weight: float32 [768, 768], P('fsdp')
- grad_gain_ffn: float32 [768], P('fsdp')
- grad_inner_weight: float32 [768, 3072], P('fsdp')
- grad_outer_weight: float32 [3072, 768], P('fsdp')
The draws below stay inside these ranges and needn't reach their ends.
Inputs may be any that keep to these rules, and one draw needn't show every extreme that they name: `lengths`: the document of slot s = index % 5 of a pair of blocks has more than half and at most all of its slot's rows, the slots holding 512, 256, 128, 64 and 64 rows.
All inputs are finite; a program needn't handle non-finite values.
Results may differ from the reference program's by a relative error of at most 0.015.
Values may be sent and summed in bfloat16 or wider, within the bound.
No kernel may reach another device: no remote copies, remote signals or barrier semaphores. Data moves between devices by JAX's collectives and lax.ppermute only.
A program may use at most 256 MiB of HBM per device.

```python
import jax
import jax.numpy as jnp
from jax import lax

D = 768
H = 12
DK = 64
FF = 3072
BUCKETS = 32
BLOCK = 512
TOKENS = 32768
DOCS = 160


def draw_lengths(key, part):
    slot_id = jnp.arange(DOCS, dtype=jnp.int32) % 5
    capacity = jnp.where(slot_id == 0, BLOCK, jnp.where(slot_id == 1, BLOCK // 2, jnp.where(slot_id == 2, BLOCK // 4, BLOCK // 8))).astype(jnp.int32)
    drawn = jax.random.randint(key, (DOCS,), capacity // 2 + 1, capacity + 1, dtype=jnp.int32)
    return drawn.at[0].set(BLOCK).at[3].set(BLOCK // 16 + 1)


def levels(key, extent, shards, least, top_value):
    gain = 1.0
    for position, blocks in shards:
        draws = jax.random.uniform(jax.random.fold_in(jax.random.fold_in(key, 6), position), (blocks,), jnp.float32, least / len(shards), top_value / len(shards))
        gain = gain * jnp.repeat(jnp.exp(draws), extent[position] // blocks).reshape((-1,) + (1,) * (len(extent) - 1 - position))
    return gain


def gaussian(rng, shape, spread, most, split=(), kind=jnp.bfloat16):
    values = jax.random.normal(rng, shape, jnp.float32) * spread
    if len(split) > 0:
        values = levels(rng, shape, split, -0.22, 0.18) * values
    return jnp.clip(values, min=-most, max=most).astype(kind)


def setup_inputs(seed: int = 0) -> dict:
    splits = jax.random.split(jax.random.key(seed), 13)
    return {
        "hidden": gaussian(splits[0], (TOKENS, D), 1.0, 6.0, ((0, 32),)),
        "gain_attn": jnp.clip(1.0 + 0.1 * jax.random.normal(splits[1], (D,), jnp.float32), 0.5, 1.5).astype(jnp.bfloat16),
        "rel_table": gaussian(splits[2], (BUCKETS * H,), 1.0, 4.0, ((0, 16),)),
        "query_weight": gaussian(splits[3], (D, H * DK), (16 * D) ** -0.5, 0.0546875, ((0, 16),)),
        "key_weight": gaussian(splits[4], (D, H * DK), D ** -0.5, 0.21875, ((0, 16),)),
        "value_weight": gaussian(splits[5], (D, H * DK), D ** -0.5, 0.21875, ((0, 16),)),
        "output_weight": gaussian(splits[6], (H * DK, D), (H * DK // 8) ** -0.5, 0.625, ((0, 16),)),
        "gain_ffn": jnp.clip(1.0 + 0.1 * jax.random.normal(splits[7], (D,), jnp.float32), 0.5, 1.5).astype(jnp.bfloat16),
        "inner_weight": gaussian(splits[8], (D, FF), D ** -0.5, 0.21875, ((0, 16),)),
        "outer_weight": gaussian(splits[9], (FF, D), FF ** -0.5, 0.109375, ((0, 16),)),
        "lengths": draw_lengths(jax.random.fold_in(splits[12], 71), 0),
        "cotangent": gaussian(splits[11], (TOKENS, D), 1.0, 6.0, ((0, 32),)),
    }


@jax.custom_vjp
def low(v):
    return lax.optimization_barrier(v.astype(jnp.bfloat16)).astype(jnp.float32)

@jax.custom_vjp
def low_back(v):
    return v

def low_keep(v):
    return (low(v), None)

def low_pass(kept, grad):
    return (grad,)

def back_keep(v):
    return (v, None)

def back_low(kept, grad):
    return (low(grad),)
low.defvjp(low_keep, low_pass)
low_back.defvjp(back_keep, back_low)
norm_eps = 1e-06
bucket_edges = (12, 16, 23, 32, 46, 64, 91)

def low_both(values):
    return low(low_back(values))

def matmul(left, right):
    return jnp.dot(left, right, precision=lax.Precision.HIGHEST, preferred_element_type=jnp.float32)

def rms_scale(values, gain_vec):
    return values * lax.rsqrt(lax.optimization_barrier(jnp.mean(values * values, axis=-1, keepdims=True)) + norm_eps) * gain_vec

def bucket_of(relative):
    distance = jnp.abs(relative)
    passed = sum(((distance >= edge_value).astype(jnp.int32) for edge_value in bucket_edges))
    return jnp.where(relative > 0, BUCKETS // 2, 0) + jnp.where(distance < BUCKETS // 4, distance, BUCKETS // 4 + passed)

def row_layout(row_count, lengths):
    row_index = jnp.arange(row_count, dtype=jnp.int32)
    block_id = row_index // BLOCK
    within = row_index % BLOCK
    odd_block = block_id % 2
    part_id = (within >= BLOCK // 2).astype(jnp.int32) + (within >= 3 * BLOCK // 4).astype(jnp.int32) + (within >= 7 * BLOCK // 8).astype(jnp.int32)
    offset = jnp.where(part_id == 0, 0, jnp.where(part_id == 1, BLOCK // 2, jnp.where(part_id == 2, 3 * BLOCK // 4, 7 * BLOCK // 8)))
    slot_id = jnp.where(odd_block == 1, part_id + 1, 0)
    offset = jnp.where(odd_block == 1, offset, 0)
    document = (block_id // 2 * 5 + slot_id).astype(jnp.int32)
    return (document, within - offset < lengths[document])

def forward(hidden_f, gain_attn, rel_table, query_weight, key_weight, value_weight, output_weight, gain_ffn, inner_weight, outer_weight, document, in_use):
    blocks = hidden_f.shape[0] // BLOCK
    normed = low(rms_scale(hidden_f, gain_attn))
    query = low_both(matmul(normed, query_weight))
    keyset = low_both(matmul(normed, key_weight))
    values = low_both(matmul(normed, value_weight))
    places = jnp.arange(BLOCK, dtype=jnp.int32)
    bucket_grid = bucket_of(places[None, :] - places[:, None])
    pos_bias = jnp.transpose(rel_table.reshape(BUCKETS, H)[bucket_grid], (2, 0, 1))

    def attend(pieces):
        block_query, block_key, block_value, block_doc, block_live = pieces
        scores = jnp.einsum('ihd,jhd->hij', block_query, block_key, precision=lax.Precision.HIGHEST) + pos_bias
        scores = low_back(scores)
        allowed = (block_doc[:, None] == block_doc[None, :]) & block_live[None, :]
        scores = jnp.where(allowed[None], scores, -1e+30)
        row_max = lax.optimization_barrier(jnp.max(scores, axis=-1, keepdims=True))
        expo_terms = jnp.exp(scores - row_max)
        attn_probs = low(expo_terms / lax.optimization_barrier(jnp.sum(expo_terms, axis=-1, keepdims=True)))
        mixture = jnp.einsum('hij,jhd->ihd', attn_probs, block_value, precision=lax.Precision.HIGHEST)
        return low_both(mixture.reshape(BLOCK, H * DK))
    context = lax.map(jax.checkpoint(attend), (query.reshape(blocks, BLOCK, H, DK), keyset.reshape(blocks, BLOCK, H, DK), values.reshape(blocks, BLOCK, H, DK), document.reshape(blocks, BLOCK), in_use.reshape(blocks, BLOCK)))
    attended = low_back(matmul(context.reshape(-1, H * DK), output_weight))
    middle = hidden_f + attended
    normed2 = low(rms_scale(middle, gain_ffn))
    inner_pre = low_back(matmul(normed2, inner_weight))
    active = low(jax.nn.gelu(inner_pre, approximate=True))
    ffn_out = low_back(matmul(active, outer_weight))
    return middle + ffn_out

def reference(hidden, gain_attn, rel_table, query_weight, key_weight, value_weight, output_weight, gain_ffn, inner_weight, outer_weight, lengths, cotangent):
    document, in_use = row_layout(hidden.shape[0], lengths)
    params = tuple((item.astype(jnp.float32) for item in (hidden, gain_attn, rel_table, query_weight, key_weight, value_weight, output_weight, gain_ffn, inner_weight, outer_weight)))

    def apply_layer(*inputs):
        return forward(*inputs, document, in_use)
    result, pullback = jax.vjp(apply_layer, *params)
    seed_grad = cotangent.astype(jnp.float32) * in_use[:, None].astype(jnp.float32)
    grads = pullback(seed_grad)
    return (result, grads[0], grads[1], grads[2], grads[3], grads[4], grads[5], grads[6], grads[7], grads[8], grads[9])
```

```python
import functools

import jax
import jax.numpy as jnp
import numpy as np
from jax import lax
from jax.experimental import pallas as pl
from jax.experimental.pallas import tpu as pltpu
from jax.sharding import PartitionSpec as P

H = 12
DK = 64
BUCKETS = 32
BLOCK = 512
norm_eps = 1e-06
bucket_edges = (12, 16, 23, 32, 46, 64, 91)
MASKED = -1e30
F32 = jnp.float32
BF16 = jnp.bfloat16
PAIR = 2 * BLOCK
GROUPS = ((0, 512), (512, 256), (768, 128), (896, 128))
SPAN = 1024
VMEM_BIG = 58 * 1024 * 1024


def bucket_of(relative):
    distance = jnp.abs(relative)
    passed = sum(((distance >= edge_value).astype(jnp.int32) for edge_value in bucket_edges))
    return jnp.where(relative > 0, BUCKETS // 2, 0) + jnp.where(
        distance < BUCKETS // 4, distance, BUCKETS // 4 + passed
    )


class Ring:
    def __init__(self, mesh):
        self.cores = mesh.shape["dp"]
        self.n = mesh.shape["fsdp"]
        bits = self.n.bit_length() - 1
        base = list(range(bits - 1, -1, -1))
        other = base[:-2] + base[-2:][::-1]
        self.order = (base, other)
        self.bits = bits

    def offsets(self, which):
        out = np.zeros(self.n, np.int32)
        for j in range(self.n):
            for k, b in enumerate(self.order[which]):
                out[j] |= ((j >> k) & 1) << b
        return out

    def inverse(self, which):
        off = self.offsets(which)
        inv = np.zeros(self.n, np.int32)
        inv[off] = np.arange(self.n)
        return inv

    def swap_phase(self, k):
        n = self.n
        return [
            (c * n + f, c * n + (f ^ (1 << self.order[c][k])))
            for c in range(2)
            for f in range(n)
        ]

    def swap_core(self):
        n = self.n
        return [(c * n + f, (1 - c) * n + f) for c in range(2) for f in range(n)]

    def meta(self):
        me = lax.axis_index("fsdp").astype(jnp.int32)
        core = lax.axis_index("dp").astype(jnp.int32)
        spots = jnp.arange(self.n, dtype=jnp.int32)

        def off(which):
            out = jnp.zeros_like(spots)
            for k, b in enumerate(self.order[which]):
                out = out | (((spots >> k) & 1) << b)
            return out

        def inv(which, m):
            out = jnp.zeros_like(spots)
            for k, b in enumerate(self.order[which]):
                out = out | (((m >> b) & 1) << k)
            return out

        first = core == 0
        mixed = me ^ spots
        return jnp.concatenate(
            [
                core[None],
                me ^ jnp.where(first, off(0), off(1)),
                me ^ jnp.where(first, off(1), off(0)),
                jnp.where(first, inv(0, mixed), inv(1, mixed)),
                jnp.where(first, inv(1, mixed), inv(0, mixed)),
            ]
        )


    def flip_origin(self, pieces):
        me = lax.axis_index("fsdp")
        shape = pieces.shape
        pieces = pieces.reshape((2,) * self.bits + shape[1:])
        for b in range(self.bits):
            axis = self.bits - 1 - b
            pieces = jnp.where((me >> b) & 1 == 1, jnp.flip(pieces, axis), pieces)
        return pieces.reshape(shape)

    def reorder(self, pieces, first, back):
        shape = pieces.shape
        split = pieces.reshape((2,) * self.bits + shape[1:])
        tail = list(range(self.bits, self.bits + len(shape) - 1))
        found = []
        for order in self.order:
            axes = [self.bits - 1 - order.index(self.bits - 1 - a) for a in range(self.bits)]
            if back:
                axes = list(np.argsort(axes))
            found.append(jnp.transpose(split, [int(a) for a in axes] + tail).reshape(shape))
        return jnp.where(first, found[0], found[1])

    def to_origin(self, pieces, first):
        return self.flip_origin(self.reorder(pieces, first, False))

    def from_origin(self, pieces, first):
        return self.reorder(self.flip_origin(pieces), first, True)


def shift(value, pairs):
    return lax.ppermute(value, ("dp", "fsdp"), pairs)


def gather_pieces(ring, shard):
    held = shard[None]
    for k in range(ring.bits - 1):
        held = jnp.concatenate([held, shift(held, ring.swap_phase(k))], axis=0)
    last = shift(held, ring.swap_phase(ring.bits - 1))
    return (held, last), (shift(held, ring.swap_core()), shift(last, ring.swap_core()))


def reduce_pieces(ring, keep, send):
    got = shift(send, ring.swap_core())
    count = ring.n
    for k in range(ring.bits - 1, -1, -1):
        half = count // 2
        away = (keep[half:count].astype(F32) + got[half:count].astype(F32)).astype(BF16)
        stay = (keep[:half].astype(F32) + got[:half].astype(F32)).astype(BF16)
        if k == 0:
            stay = keep[:half].astype(F32) + got[:half].astype(F32)
        got = shift(away, ring.swap_phase(k))
        keep = stay
        count = half
    return keep[0].astype(F32) + got[0].astype(F32)


def any_spec():
    return pl.BlockSpec(memory_space=pl.ANY)


def params(vmem=VMEM_BIG):
    return pltpu.CompilerParams(vmem_limit_bytes=vmem)


def cost(flops, bytes_accessed, trans=0):
    return pl.CostEstimate(flops=flops, bytes_accessed=bytes_accessed, transcendentals=trans)


def dot(a, b):
    return jnp.dot(a, b, preferred_element_type=F32)


def dot_nt(a, b):
    return lax.dot_general(a, b, (((1,), (1,)), ((), ())), preferred_element_type=F32)


def dot_tn(a, b):
    return lax.dot_general(a, b, (((0,), (0,)), ((), ())), preferred_element_type=F32)


class Pieces:
    def __init__(self, own, rec, n):
        self.arrays = [own[0], own[1], rec[0], rec[1]]
        self.n = n
        self.count = 4
        self.whole = False


class Whole:
    def __init__(self, array):
        self.arrays = [array]
        self.count = 1
        self.whole = True
        self.n = 0


def column_copies(chunk, meta, refs, lo, width, dst, sems, base=0):
    copies = []
    if chunk.whole:
        for h in range(2):
            src = refs[0].at[h, :, pl.ds(lo, width)]
            copies.append(
                pltpu.make_async_copy(src, dst.at[:, pl.ds(h * width, width)], sems.at[base + h])
            )
        return copies
    n = chunk.n
    half = n // 2
    rows = refs[0].shape[1]
    core = meta[0]
    for h in range(2):
        col = pl.multiple_of((core if h == 0 else 1 - core) * width, 128)
        for j in range(n):
            ref = refs[2 * h + j // half]
            row = pl.multiple_of(meta[1 + h * n + j] * rows, 16)
            copies.append(
                pltpu.make_async_copy(
                    ref.at[j % half, :, pl.ds(lo, width)],
                    dst.at[pl.ds(row, rows), pl.ds(col, width)],
                    sems.at[base + h * n + j],
                )
            )
    return copies


def row_copies(chunk, meta, refs, dst, sems, base=0):
    if chunk.whole:
        return [pltpu.make_async_copy(refs[0], dst, sems.at[base])]
    n = chunk.n
    half = n // 2
    rows = refs[0].shape[1]
    core = meta[0]
    copies = []
    for h in range(2):
        for j in range(n):
            ref = refs[2 * h + j // half]
            row = pl.multiple_of(
                meta[1 + h * n + j] * (2 * rows) + (core if h == 0 else 1 - core) * rows, 16
            )
            copies.append(
                pltpu.make_async_copy(
                    ref.at[j % half], dst.at[pl.ds(row, rows), :], sems.at[base + h * n + j]
                )
            )
    return copies


def run_copies(copies):
    for c in copies:
        c.start()
    for c in copies:
        c.wait()


def copy_count(chunk):
    return 2 if chunk.whole else 2 * chunk.n


def norm_tile(x, ext_ref, first):
    d = x.shape[1]
    scale = lax.rsqrt(jnp.mean(x * x, axis=-1, keepdims=True) + norm_eps)
    out = []
    for c in range(d // 128):
        out.append(
            (x[:, c * 128 : (c + 1) * 128] * scale * ext_ref[first + c : first + c + 1, :]).astype(
                BF16
            )
        )
    return jnp.concatenate(out, axis=1), scale


def qkv_kernel(chunk, meta, x_ref, ext_ref, *rest):
    refs = rest[: chunk.count]
    qkv_ref, n_ref, dist_ref, w, sems = rest[chunk.count :]
    width = w.shape[1] // 2

    @pl.when(pl.program_id(0) == 0)
    def _():
        copies = column_copies(chunk, meta, refs, 0, width, w, sems)
        for c in copies:
            c.start()
        place = lax.broadcasted_iota(jnp.int32, (BUCKETS, SPAN), 1)
        row = lax.broadcasted_iota(jnp.int32, (BUCKETS, SPAN), 0)
        chosen = (bucket_of(BLOCK - 1 - place) == row).astype(F32).astype(BF16)
        dist_ref[...] = dot(ext_ref[16:32, 0:BUCKETS].astype(BF16), chosen)
        for c in copies:
            c.wait()

    normed, _ = norm_tile(x_ref[...].astype(F32), ext_ref, 0)
    n_ref[...] = normed
    qkv_ref[...] = dot(normed, w[...]).astype(BF16)


def qkv_call(meta, x, ext, chunk, tile=256):
    rows, d = x.shape
    grid_spec = pltpu.PrefetchScalarGridSpec(
        num_scalar_prefetch=1,
        grid=(rows // tile,),
        in_specs=[
            pl.BlockSpec((tile, d), lambda i, m: (i, 0)),
            pl.BlockSpec(ext.shape, lambda i, m: (0, 0)),
        ]
        + [any_spec()] * chunk.count,
        out_specs=[
            pl.BlockSpec((tile, 3 * d), lambda i, m: (i, 0)),
            pl.BlockSpec((tile, d), lambda i, m: (i, 0)),
            pl.BlockSpec((16, SPAN), lambda i, m: (0, 0)),
        ],
        scratch_shapes=[
            pltpu.VMEM((d, 3 * d), BF16),
            pltpu.SemaphoreType.DMA((copy_count(chunk),)),
        ],
    )
    return pl.pallas_call(
        functools.partial(qkv_kernel, chunk),
        grid_spec=grid_spec,
        out_shape=[
            jax.ShapeDtypeStruct((rows, 3 * d), BF16),
            jax.ShapeDtypeStruct((rows, d), BF16),
            jax.ShapeDtypeStruct((16, SPAN), F32),
        ],
        compiler_params=params(),
        cost_estimate=cost(6 * rows * d * d, 14 * rows * d + 6 * d * d),
        name="qkv",
    )(meta, x, ext, *chunk.arrays)


def bias_strip(dist_row):
    spread = jnp.broadcast_to(dist_row, (128, SPAN))
    return pltpu.roll(spread, SPAN - 127, 1, stride=1, stride_axis=0)


def attend_kernel(q_ref, k_ref, v_ref, qaug_ref, kaug_ref, dist_ref, ctx_ref, lse_ref):
    pair = pl.program_id(1)
    lane = lax.broadcasted_iota(jnp.int32, (PAIR, 128), 1)
    q, k = q_ref[...], k_ref[...]
    qaug, kaug = qaug_ref[...], kaug_ref[...]
    v_turned = v_ref[...].T
    heads = []
    for hh in range(2):
        mine = (lane // 64) == hh
        heads.append(
            (
                jnp.where(mine, q, qaug),
                jnp.where(mine, k, kaug),
                v_turned[hh * 64 : (hh + 1) * 64, :],
                bias_strip(dist_ref[pl.ds(2 * pair + hh, 1), :]),
            )
        )
    for off, size in GROUPS:
        step = min(256, size)
        for i0 in range(0, size, step):
            parts = []
            for hh in range(2):
                qa, ka, vt, strip = heads[hh]
                scores = dot_nt(ka[off : off + size], qa[off + i0 : off + i0 + step])
                bias = jnp.concatenate(
                    [
                        strip[:, (3 - t) * 128 + i0 : (3 - t) * 128 + i0 + step]
                        for t in range(size // 128)
                    ],
                    axis=0,
                )
                scores = scores + bias
                top = jnp.max(scores, axis=0, keepdims=True)
                expo = jnp.exp(scores - top)
                total = jnp.sum(expo, axis=0, keepdims=True)
                mixed = dot(vt[:, off : off + size], expo.astype(BF16))
                parts.append(mixed * (1.0 / total))
                lse_ref[0, hh : hh + 1, off + i0 : off + i0 + step] = top + jnp.log(total)
            both = jnp.concatenate(parts, axis=0)
            ctx_ref[off + i0 : off + i0 + step, :] = both.T.astype(BF16)


def head_block(part):
    return lambda p, h: (p, (h // 3) * 9 + part * 3 + h % 3)


def attend_call(qkv, qaug, kaug, dist):
    rows = qkv.shape[0]
    d = qkv.shape[1] // 3
    pairs = rows // PAIR
    return pl.pallas_call(
        attend_kernel,
        grid=(pairs, H // 2),
        in_specs=[
            pl.BlockSpec((PAIR, 128), head_block(0)),
            pl.BlockSpec((PAIR, 128), head_block(1)),
            pl.BlockSpec((PAIR, 128), head_block(2)),
            pl.BlockSpec((PAIR, 128), lambda p, h: (p, 0)),
            pl.BlockSpec((PAIR, 128), lambda p, h: (p, 0)),
            pl.BlockSpec((16, SPAN), lambda p, h: (0, 0)),
        ],
        out_specs=[
            pl.BlockSpec((PAIR, 128), lambda p, h: (p, h)),
            pl.BlockSpec((1, 2, PAIR), lambda p, h: (h, 0, p)),
        ],
        out_shape=[
            jax.ShapeDtypeStruct((rows, d), BF16),
            jax.ShapeDtypeStruct((H // 2, 2, rows), F32),
        ],
        compiler_params=params(),
        cost_estimate=cost(4 * pairs * H * 350000 * 128, 8 * rows * d, pairs * H * 350000),
        name="attend",
    )(qkv, qkv, qkv, qaug, kaug, dist)


def mid_kernel(chunk, meta, ctx_ref, x_ref, ext_ref, *rest):
    refs = rest[: chunk.count]
    mid_ref, n2_ref, act_ref, slope_ref, wo, w1, sems = rest[chunk.count :]
    d = wo.shape[0]

    @pl.when(pl.program_id(0) == 0)
    def _():
        n = copy_count(chunk)
        run_copies(
            column_copies(chunk, meta, refs, 0, d // 2, wo, sems)
            + column_copies(chunk, meta, refs, d // 2, w1.shape[1] // 2, w1, sems, n)
        )

    middle = x_ref[...].astype(F32) + dot(ctx_ref[...], wo[...])
    mid_ref[...] = middle
    normed, _ = norm_tile(middle, ext_ref, 6)
    n2_ref[...] = normed
    c0 = 0.7978845608028654
    c1 = c0 * 0.044715
    step = 512
    for f in range(0, w1.shape[1], step):
        v = dot(normed, w1[:, f : f + step])
        v2 = v * v
        t = jnp.tanh(v * (c0 + c1 * v2))
        half = 0.5 + 0.5 * t
        act_ref[:, f : f + step] = (v * half).astype(BF16)
        slope_ref[:, f : f + step] = (
            half + (0.5 * v) * (1.0 - t * t) * (c0 + (3.0 * c1) * v2)
        ).astype(BF16)


def mid_call(meta, ctx, x, ext, chunk, ff, tile=256):
    rows, d = x.shape
    grid_spec = pltpu.PrefetchScalarGridSpec(
        num_scalar_prefetch=1,
        grid=(rows // tile,),
        in_specs=[
            pl.BlockSpec((tile, d), lambda i, m: (i, 0)),
            pl.BlockSpec((tile, d), lambda i, m: (i, 0)),
            pl.BlockSpec(ext.shape, lambda i, m: (0, 0)),
        ]
        + [any_spec()] * chunk.count,
        out_specs=[
            pl.BlockSpec((tile, d), lambda i, m: (i, 0)),
            pl.BlockSpec((tile, d), lambda i, m: (i, 0)),
            pl.BlockSpec((tile, ff), lambda i, m: (i, 0)),
            pl.BlockSpec((tile, ff), lambda i, m: (i, 0)),
        ],
        scratch_shapes=[
            pltpu.VMEM((d, d), BF16),
            pltpu.VMEM((d, ff), BF16),
            pltpu.SemaphoreType.DMA((2 * copy_count(chunk),)),
        ],
    )
    return pl.pallas_call(
        functools.partial(mid_kernel, chunk),
        grid_spec=grid_spec,
        out_shape=[
            jax.ShapeDtypeStruct((rows, d), F32),
            jax.ShapeDtypeStruct((rows, d), BF16),
            jax.ShapeDtypeStruct((rows, ff), BF16),
            jax.ShapeDtypeStruct((rows, ff), BF16),
        ],
        compiler_params=params(),
        cost_estimate=cost(2 * rows * d * (d + ff), 10 * rows * d + 4 * rows * ff, rows * ff),
        name="mid",
    )(meta, ctx, x, ext, *chunk.arrays)


def outer_grad_kernel(n, meta, act_ref, g_ref, keep_ref, send_ref):
    per = keep_ref.shape[1]
    first = meta[0] == 0
    total = dot_tn(act_ref[...], g_ref[...]).astype(BF16)
    count = act_ref.shape[1] // (2 * per)
    for f in range(count):
        low = total[2 * f * per : (2 * f + 1) * per]
        high = total[(2 * f + 1) * per : (2 * f + 2) * per]
        spot = pl.program_id(0) * count + f
        keep_ref[meta[1 + 2 * n + spot]] = jnp.where(first, low, high)
        send_ref[meta[1 + 3 * n + spot]] = jnp.where(first, high, low)


def outer_grad_call(meta, act, g, n):
    rows, ff = act.shape
    d = g.shape[1]
    per = ff // n // 2
    shape = jax.ShapeDtypeStruct((n, per, d), BF16)
    return pl.pallas_call(
        functools.partial(outer_grad_kernel, n),
        grid_spec=pltpu.PrefetchScalarGridSpec(
            num_scalar_prefetch=1,
            grid=(ff // 768,),
            in_specs=[
                pl.BlockSpec((rows, 768), lambda i, m: (0, i)),
                pl.BlockSpec((rows, d), lambda i, m: (0, 0)),
            ],
            out_specs=[pl.BlockSpec((n, per, d), lambda i, m: (0, 0, 0))] * 2,
        ),
        out_shape=[shape, shape],
        compiler_params=params(),
        cost_estimate=cost(2 * rows * d * ff, 2 * rows * (d + ff) + 2 * d * ff),
        name="outer_grad",
    )(meta, act, g)


def out_kernel(chunk, meta, act_ref, mid_ref, g_ref, slope_ref, *rest):
    refs = rest[: chunk.count]
    result_ref, din_ref, w2, sems = rest[chunk.count :]

    @pl.when(pl.program_id(0) == 0)
    def _():
        run_copies(row_copies(chunk, meta, refs, w2, sems))

    result_ref[...] = mid_ref[...] + dot(act_ref[...], w2[...])
    step = 512
    g = g_ref[...]
    for f in range(0, w2.shape[0], step):
        d_act = dot_nt(g, w2[f : f + step, :])
        din_ref[:, f : f + step] = (d_act * slope_ref[:, f : f + step].astype(F32)).astype(BF16)


def out_call(meta, act, middle, g, slope, chunk, tile=256):
    rows, ff = act.shape
    d = middle.shape[1]
    row = lambda w: pl.BlockSpec((tile, w), lambda i, m: (i, 0))
    return pl.pallas_call(
        functools.partial(out_kernel, chunk),
        grid_spec=pltpu.PrefetchScalarGridSpec(
            num_scalar_prefetch=1,
            grid=(rows // tile,),
            in_specs=[row(ff), row(d), row(d), row(ff)] + [any_spec()] * chunk.count,
            out_specs=[row(d), row(ff)],
            scratch_shapes=[
                pltpu.VMEM((ff, d), BF16),
                pltpu.SemaphoreType.DMA((copy_count(chunk),)),
            ],
        ),
        out_shape=[
            jax.ShapeDtypeStruct((rows, d), F32),
            jax.ShapeDtypeStruct((rows, ff), BF16),
        ],
        compiler_params=params(),
        cost_estimate=cost(4 * rows * d * ff, 10 * rows * d + 6 * rows * ff),
        name="out",
    )(meta, act, middle, g, slope, *chunk.arrays)


def column_grad_kernel(n, steps, extra, meta, a_ref, *rest):
    b_refs = rest[: len(rest) - 3 - (1 if extra else 0)]
    rest = rest[len(b_refs) :]
    e_ref = rest[0] if extra else None
    keep_ref, send_ref, turned = rest[1:] if extra else rest
    half = pl.program_id(0)

    @pl.when((half == 0) & (pl.program_id(1) == 0))
    def _():
        turned[...] = a_ref[...].T

    per = turned.shape[0] // n

    def fill(out, table):
        col = 0
        for b_ref in b_refs:
            w = b_ref.shape[1]
            total = dot(turned[...], b_ref[...]).astype(BF16)
            for f in range(n):
                out[meta[1 + table * n + f], :, col : col + w] = total[f * per : (f + 1) * per]
            col += w
        if extra:
            for f in range(n):
                out[f, :, col : col + 128] = e_ref[...]

    @pl.when(half == 0)
    def _():
        fill(send_ref, 3)

    @pl.when(half == 1)
    def _():
        fill(keep_ref, 2)


def column_grad_call(meta, a, bs, n, steps, name, extra=None):
    rows, d = a.shape
    per = d // n
    widths = [b.shape[1] // 2 // steps for b in bs]
    block = sum(widths) + (128 if extra is not None else 0)
    shape = jax.ShapeDtypeStruct((n, per, block * steps), BF16)

    def pick(i, j, m):
        half = jnp.where(i == 0, 1 - m[0], m[0])
        return (0, half * steps + j)

    in_specs = [pl.BlockSpec((rows, d), lambda i, j, m: (0, 0))]
    in_specs += [pl.BlockSpec((rows, w), pick) for w in widths]
    args = [a, *bs]
    if extra is not None:
        assert steps == 1
        in_specs.append(pl.BlockSpec(extra.shape, lambda i, j, m: (0, 0)))
        args.append(extra)
    return pl.pallas_call(
        functools.partial(column_grad_kernel, n, steps, extra is not None),
        grid_spec=pltpu.PrefetchScalarGridSpec(
            num_scalar_prefetch=1,
            grid=(2, steps),
            in_specs=in_specs,
            out_specs=[
                pl.BlockSpec((n, per, block), lambda i, j, m: (0, 0, jnp.where(i == 0, 0, j))),
                pl.BlockSpec(
                    (n, per, block), lambda i, j, m: (0, 0, jnp.where(i == 0, j, steps - 1))
                ),
            ],
            scratch_shapes=[pltpu.VMEM((d, rows), BF16)],
        ),
        out_shape=[shape, shape],
        compiler_params=params(),
        cost_estimate=cost(
            2 * rows * d * sum(b.shape[1] for b in bs),
            2 * rows * (d + sum(b.shape[1] for b in bs)) + 2 * d * sum(b.shape[1] for b in bs),
        ),
        name=name,
    )(meta, *args)


def norm_back(dn, x, gain_ref, first, scale):
    d = x.shape[1]
    z = jnp.concatenate(
        [
            dn[:, c * 128 : (c + 1) * 128] * gain_ref[first + c : first + c + 1, :]
            for c in range(d // 128)
        ],
        axis=1,
    )
    inner = jnp.mean(z * x, axis=-1, keepdims=True)
    back = scale * z - x * (scale * scale * scale * inner)
    return back, jnp.sum(dn * (x * scale), axis=0, keepdims=True)


def mid_back_kernel(chunk, meta, din_ref, mid_ref, g_ref, ext_ref, *rest):
    refs = rest[: chunk.count]
    dmid_ref, datt_ref, dctx_ref, gain_ref, wo, w1, sems = rest[chunk.count :]
    d = wo.shape[0]

    @pl.when(pl.program_id(0) == 0)
    def _():
        n = copy_count(chunk)
        run_copies(
            column_copies(chunk, meta, refs, 0, d // 2, wo, sems)
            + column_copies(chunk, meta, refs, d // 2, w1.shape[1] // 2, w1, sems, n)
        )
        gain_ref[...] = jnp.zeros_like(gain_ref)

    dn = dot_nt(din_ref[...], w1[...])
    middle = mid_ref[...]
    scale = lax.rsqrt(jnp.mean(middle * middle, axis=-1, keepdims=True) + norm_eps)
    back, gain = norm_back(dn, middle, ext_ref, 6, scale)
    gain_ref[...] += gain
    dmid = g_ref[...].astype(F32) + back
    dmid_ref[...] = dmid
    low = dmid.astype(BF16)
    datt_ref[...] = low
    dctx_ref[...] = dot_nt(low, wo[...]).astype(BF16)


def mid_back_call(meta, din, middle, g, ext, chunk, tile=256):
    rows, ff = din.shape
    d = middle.shape[1]
    row = lambda w: pl.BlockSpec((tile, w), lambda i, m: (i, 0))
    return pl.pallas_call(
        functools.partial(mid_back_kernel, chunk),
        grid_spec=pltpu.PrefetchScalarGridSpec(
            num_scalar_prefetch=1,
            grid=(rows // tile,),
            in_specs=[row(ff), row(d), row(d), pl.BlockSpec(ext.shape, lambda i, m: (0, 0))]
            + [any_spec()] * chunk.count,
            out_specs=[row(d), row(d), row(d), pl.BlockSpec((1, d), lambda i, m: (0, 0))],
            scratch_shapes=[
                pltpu.VMEM((d, d), BF16),
                pltpu.VMEM((d, ff), BF16),
                pltpu.SemaphoreType.DMA((2 * copy_count(chunk),)),
            ],
        ),
        out_shape=[
            jax.ShapeDtypeStruct((rows, d), F32),
            jax.ShapeDtypeStruct((rows, d), BF16),
            jax.ShapeDtypeStruct((rows, d), BF16),
            jax.ShapeDtypeStruct((1, d), F32),
        ],
        compiler_params=params(),
        cost_estimate=cost(2 * rows * d * (d + ff), 14 * rows * d + 2 * rows * ff),
        name="mid_back",
    )(meta, din, middle, g, ext, *chunk.arrays)


def diagonal_sums(strip):
    for s in (64, 32, 16, 8):
        strip = strip[:s] + pltpu.roll(strip[s:], SPAN - s, 1)
    for s in (4, 2, 1):
        strip = strip + pltpu.roll(pltpu.roll(strip, 8 - s, 0), SPAN - s, 1)
    return strip[:1]


def attend_back_kernel(
    q_ref,
    k_ref,
    v_ref,
    do_ref,
    qaug_ref,
    kaug_ref,
    dist_ref,
    lse_ref,
    dq_ref,
    dk_ref,
    dv_ref,
    table_ref,
    strip_acc,
):
    pair = pl.program_id(0)
    lane = lax.broadcasted_iota(jnp.int32, (PAIR, 128), 1)
    q, k, v, do = q_ref[...], k_ref[...], v_ref[...], do_ref[...]
    qaug, kaug = qaug_ref[...], kaug_ref[...]
    k_turned = k.T
    strip_acc[...] = jnp.zeros_like(strip_acc)
    heads = []
    for hh in range(2):
        mine = (lane // 64) == hh
        heads.append(
            (
                jnp.where(mine, q, qaug),
                jnp.where(mine, k, kaug),
                jnp.where(mine, v, jnp.zeros_like(v)),
                k_turned[hh * 64 : (hh + 1) * 64, :],
                bias_strip(dist_ref[pl.ds(2 * pair + hh, 1), :]),
            )
        )
    for off, size in GROUPS:
        step = min(256, size)
        low = lax.broadcasted_iota(jnp.int32, (size, 128), 1) < 64
        dks, dvs = [None, None], [None, None]
        for i0 in range(0, size, step):
            lo, hi = off + i0, off + i0 + step
            dqs = []
            for hh in range(2):
                qa, ka, va, kt, strip = heads[hh]
                scores = dot_nt(ka[off : off + size], qa[lo:hi])
                bias = jnp.concatenate(
                    [
                        strip[:, (3 - t) * 128 + i0 : (3 - t) * 128 + i0 + step]
                        for t in range(size // 128)
                    ],
                    axis=0,
                )
                probs = jnp.exp(scores + bias - lse_ref[0, hh : hh + 1, lo:hi])
                d_probs = dot_nt(va[off : off + size], do[lo:hi])
                dv = dot(probs.astype(BF16), do[lo:hi])
                center = jnp.sum(probs * d_probs, axis=0, keepdims=True)
                d_scores = probs * (d_probs - center)
                for t in range(size // 128):
                    at = (3 - t) * 128 + i0
                    strip_acc[hh, :, at : at + step] += d_scores[t * 128 : (t + 1) * 128]
                ds_low = d_scores.astype(BF16)
                dk = dot(ds_low, q[lo:hi])
                dqs.append(dot(kt[:, off : off + size], ds_low))
                dks[hh] = dk if dks[hh] is None else dks[hh] + dk
                dvs[hh] = dv if dvs[hh] is None else dvs[hh] + dv
            dq_ref[lo:hi, :] = jnp.concatenate(dqs, axis=0).T.astype(BF16)
        dk_ref[off : off + size, :] = jnp.where(low, dks[0], dks[1]).astype(BF16)
        dv_ref[off : off + size, :] = jnp.where(low, dvs[0], dvs[1]).astype(BF16)

    place = (lax.broadcasted_iota(jnp.int32, (128, SPAN), 1) + 127) % SPAN
    row = lax.broadcasted_iota(jnp.int32, (128, SPAN), 0)
    chosen = (bucket_of(BLOCK - 1 - place) == row).astype(F32)
    sums = [diagonal_sums(strip_acc[hh]) for hh in range(2)]
    sums.append(jnp.zeros((6, SPAN), F32))
    found = lax.dot_general(
        jnp.concatenate(sums, axis=0),
        chosen,
        (((1,), (1,)), ((), ())),
        precision=lax.Precision.HIGHEST,
        preferred_element_type=F32,
    )

    @pl.when(pl.program_id(1) == 0)
    def _():
        table_ref[0] = found

    @pl.when(pl.program_id(1) > 0)
    def _():
        table_ref[0] += found


def attend_back_call(qkv, dctx, qaug, kaug, dist, lse):
    rows, d = dctx.shape
    pairs = rows // PAIR

    def part(t):
        return lambda h, p: (p, (h // 3) * 9 + t * 3 + h % 3)

    head = pl.BlockSpec((PAIR, 128), lambda h, p: (p, h))
    same = pl.BlockSpec((PAIR, 128), lambda h, p: (p, 0))
    grad = jax.ShapeDtypeStruct((rows, d), BF16)
    return pl.pallas_call(
        attend_back_kernel,
        grid=(H // 2, pairs),
        in_specs=[
            pl.BlockSpec((PAIR, 128), part(0)),
            pl.BlockSpec((PAIR, 128), part(1)),
            pl.BlockSpec((PAIR, 128), part(2)),
            head,
            same,
            same,
            pl.BlockSpec((16, SPAN), lambda h, p: (0, 0)),
            pl.BlockSpec((1, 2, PAIR), lambda h, p: (h, 0, p)),
        ],
        out_specs=[head, head, head, pl.BlockSpec((1, 8, 128), lambda h, p: (h, 0, 0))],
        out_shape=[grad, grad, grad, jax.ShapeDtypeStruct((H // 2, 8, 128), F32)],
        scratch_shapes=[pltpu.VMEM((2, 128, SPAN), F32)],
        compiler_params=params(),
        cost_estimate=cost(10 * pairs * H * 350000 * 128, 14 * rows * d, pairs * H * 350000),
        name="attend_back",
    )(qkv, qkv, qkv, dctx, qaug, kaug, dist, lse)


def in_back_kernel(chunk, meta, dq_ref, dk_ref, dv_ref, x_ref, dmid_ref, ext_ref, *rest):
    refs = rest[: chunk.count]
    dx_ref, gain_ref, w, sems = rest[chunk.count :]
    d = w.shape[0]

    @pl.when(pl.program_id(0) == 0)
    def _():
        run_copies(column_copies(chunk, meta, refs, 0, w.shape[1] // 2, w, sems))
        gain_ref[...] = jnp.zeros_like(gain_ref)

    h = d // 2
    parts = [r[:, s * h : (s + 1) * h] for s in range(2) for r in (dq_ref, dk_ref, dv_ref)]
    dn = dot_nt(jnp.concatenate(parts, axis=1), w[...])
    x = x_ref[...].astype(F32)
    scale = lax.rsqrt(jnp.mean(x * x, axis=-1, keepdims=True) + norm_eps)
    back, gain = norm_back(dn, x, ext_ref, 0, scale)
    gain_ref[...] += gain
    dx_ref[...] = dmid_ref[...] + back


def in_back_call(meta, dq, dk, dv, x, dmid, ext, chunk, tile=256):
    rows, d = x.shape
    row = lambda w: pl.BlockSpec((tile, w), lambda i, m: (i, 0))
    return pl.pallas_call(
        functools.partial(in_back_kernel, chunk),
        grid_spec=pltpu.PrefetchScalarGridSpec(
            num_scalar_prefetch=1,
            grid=(rows // tile,),
            in_specs=[row(d)] * 5
            + [pl.BlockSpec(ext.shape, lambda i, m: (0, 0))]
            + [any_spec()] * chunk.count,
            out_specs=[row(d), pl.BlockSpec((1, d), lambda i, m: (0, 0))],
            scratch_shapes=[
                pltpu.VMEM((d, 3 * d), BF16),
                pltpu.SemaphoreType.DMA((copy_count(chunk),)),
            ],
        ),
        out_shape=[
            jax.ShapeDtypeStruct((rows, d), F32),
            jax.ShapeDtypeStruct((1, d), F32),
        ],
        compiler_params=params(),
        cost_estimate=cost(6 * rows * d * d, 16 * rows * d + 6 * d * d),
        name="in_back",
    )(meta, dq, dk, dv, x, dmid, ext, *chunk.arrays)


def mask_lanes(lengths, rows):
    spot = jnp.arange(rows, dtype=jnp.int32)
    within = spot % PAIR
    first = jnp.array([0, 512, 768, 896, 960], jnp.int32)
    slot = jnp.sum((within[:, None] >= first[None, 1:]).astype(jnp.int32), axis=1)
    start = jnp.sum(jnp.where(slot[:, None] == jnp.arange(5)[None], first[None], 0), axis=1)
    docs = jnp.arange(lengths.shape[0], dtype=jnp.int32)
    document = spot // PAIR * 5 + slot
    own = jnp.sum(jnp.where(document[:, None] == docs[None], lengths[None], 0), axis=1)
    live = within - start < own
    late = slot == 4
    lane = jnp.arange(128, dtype=jnp.int32) % 64
    shown = [live & ~late, live & late]
    kaug = jnp.where(
        lane[None] == 0,
        jnp.where(shown[0], 0.0, MASKED)[:, None],
        jnp.where(lane[None] == 1, jnp.where(shown[1], 0.0, MASKED)[:, None], 0.0),
    ).astype(BF16)
    qaug = jnp.where(
        lane[None] == 0,
        jnp.where(late, 0.0, 1.0)[:, None],
        jnp.where(lane[None] == 1, jnp.where(late, 1.0, 0.0)[:, None], 0.0),
    ).astype(BF16)
    return qaug, kaug, live


def placed_rows(vector, me, rows):
    count = vector.shape[0]
    spot = jnp.arange(rows * 128, dtype=jnp.int32)[None] - me * count
    hit = spot == jnp.arange(count, dtype=jnp.int32)[:, None]
    flat = jnp.sum(jnp.where(hit, vector.astype(F32)[:, None], 0.0), axis=0)
    return flat.reshape(rows, 128)


def placed_table(vector, me):
    count = vector.shape[0]
    head = jnp.arange(16, dtype=jnp.int32)[:, None]
    bucket = jnp.arange(128, dtype=jnp.int32)[None]
    entry = jnp.where((head < H) & (bucket < BUCKETS), bucket * H + head, -1) - me * count
    hit = entry[None] == jnp.arange(count, dtype=jnp.int32)[:, None, None]
    return jnp.sum(jnp.where(hit, vector.astype(F32)[:, None, None], 0.0), axis=0)


def local(
    ring,
    hidden,
    gain_attn,
    rel_table,
    query_weight,
    key_weight,
    value_weight,
    output_weight,
    gain_ffn,
    inner_weight,
    outer_weight,
    lengths,
    cotangent,
):
    rows, d = hidden.shape
    ff = inner_weight.shape[1]
    n = ring.n
    shard_rows = query_weight.shape[0]
    outer_rows = outer_weight.shape[0]
    direct = shard_rows % 16 == 0 and shard_rows >= 32 and outer_rows % 32 == 0
    me = lax.axis_index("fsdp")
    core = lax.axis_index("dp")
    meta = ring.meta()
    h = d // 2

    def half(w, which):
        width = w.shape[1] // 2
        return lax.dynamic_slice_in_dim(w, which * width, width, 1)

    small = jnp.concatenate(
        [
            placed_rows(gain_attn, me, d // 128),
            placed_rows(gain_ffn, me, d // 128),
            jnp.zeros((16 - 2 * (d // 128), 128), F32),
            placed_table(rel_table, me),
        ],
        axis=0,
    ).astype(BF16)
    pack_a = [half(w, core) for w in (query_weight, key_weight, value_weight)]
    if direct:
        pack_a.append(jnp.pad(small, ((0, shard_rows - 32), (0, 0))))
    pack_a = jnp.concatenate(pack_a, axis=1)
    pack_b = jnp.concatenate([half(output_weight, core), half(inner_weight, core)], axis=1)
    pack_c = lax.dynamic_slice_in_dim(
        outer_weight, core * (outer_rows // 2), outer_rows // 2, 0
    )

    def whole_columns(own, rec):
        both = []
        for parts, first in ((own, core == 0), (rec, core == 1)):
            pieces = ring.to_origin(jnp.concatenate(parts, axis=0), first)
            both.append(pieces.reshape(-1, pieces.shape[2]))
        first = jnp.where(core == 0, both[0], both[1])
        second = jnp.where(core == 0, both[1], both[0])
        return jnp.stack([first, second])

    got_a = gather_pieces(ring, pack_a)
    got_b = gather_pieces(ring, pack_b)
    got_c = gather_pieces(ring, pack_c)
    if direct:
        chunk_a, chunk_b, chunk_c = (Pieces(*g, n) for g in (got_a, got_b, got_c))
        ext = sum(jnp.sum(p[:, :32, 3 * h :].astype(F32), axis=0) for p in got_a[0])
    else:
        chunk_a = Whole(whole_columns(*got_a))
        chunk_b = Whole(whole_columns(*got_b))
        both = [
            ring.to_origin(jnp.concatenate(parts, axis=0), first)
            for parts, first in zip(got_c, (core == 0, core == 1))
        ]
        first = jnp.where(core == 0, both[0], both[1])
        second = jnp.where(core == 0, both[1], both[0])
        chunk_c = Whole(jnp.stack([first, second], axis=1).reshape(ff, d))
        ext = lax.psum(small.astype(F32), "fsdp")

    qaug, kaug, live = mask_lanes(lengths, rows)
    g = jnp.where(live[:, None], cotangent, jnp.zeros_like(cotangent))

    qkv, normed, dist = qkv_call(meta, hidden, ext, chunk_a)
    ctx, lse = attend_call(qkv, qaug, kaug, dist)
    middle, normed2, act, slope = mid_call(meta, ctx, hidden, ext, chunk_b, ff)

    def split_columns(a, bs, steps, name, extra=None):
        if direct:
            return column_grad_call(meta, a, bs, n, steps, name, extra)
        full = [jnp.einsum("td,tf->df", a, b, preferred_element_type=F32) for b in bs]
        out = []
        for which in (core, 1 - core):
            part = jnp.concatenate([half(w, which) for w in full], axis=1).astype(BF16)
            part = part.reshape(n, d // n, part.shape[1])
            out.append(ring.from_origin(part, which == 0))
        return out

    def split_rows(a, b):
        if direct:
            return outer_grad_call(meta, a, b, n)
        full = jnp.einsum("tf,td->fd", a, b, preferred_element_type=F32).astype(BF16)
        full = full.reshape(n, 2, outer_rows // 2, d)
        return [
            ring.from_origin(
                lax.dynamic_index_in_dim(full, which, 1, keepdims=False), which == 0
            )
            for which in (core, 1 - core)
        ]

    sum_c = reduce_pieces(ring, *split_rows(act, g))
    result, d_inner = out_call(meta, act, middle, g, slope, chunk_c)
    sum_b = reduce_pieces(ring, *split_columns(normed2, [d_inner], 3, "inner_grad"))
    d_middle, d_att, d_ctx, grad_gain_f = mid_back_call(meta, d_inner, middle, g, ext, chunk_b)
    sum_o = reduce_pieces(ring, *split_columns(ctx, [d_att], 1, "output_grad"))
    dq, dk, dv, found = attend_back_call(qkv, d_ctx, qaug, kaug, dist, lse)
    grad_hidden, grad_gain_a = in_back_call(meta, dq, dk, dv, hidden, d_middle, ext, chunk_a)
    extra = jnp.concatenate(
        [
            grad_gain_a.reshape(d // 128, 128),
            grad_gain_f.reshape(d // 128, 128),
            jnp.zeros((16 - 2 * (d // 128), 128), F32),
            found[:, :2].reshape(H, 128),
            jnp.zeros((4, 128), F32),
        ],
        axis=0,
    )
    if direct:
        block = jnp.pad(extra, ((0, shard_rows - 32), (0, 0))).astype(BF16)
        sum_a = reduce_pieces(ring, *split_columns(normed, [dq, dk, dv], 1, "qkv_grad", block))
        extra = sum_a[:32, 3 * h :]
    else:
        sum_a = reduce_pieces(ring, *split_columns(normed, [dq, dk, dv], 1, "qkv_grad"))
        extra = lax.psum(extra, ("dp", "fsdp"))

    own = [sum_a[:, : 3 * h], sum_o, sum_b, sum_c]
    other = [shift(s, ring.swap_core()) for s in own]
    low = [jnp.where(core == 0, a, b) for a, b in zip(own, other)]
    high = [jnp.where(core == 0, b, a) for a, b in zip(own, other)]
    grads = [
        jnp.concatenate([low[0][:, t * h : (t + 1) * h], high[0][:, t * h : (t + 1) * h]], axis=1)
        for t in range(3)
    ]
    grad_output = jnp.concatenate([low[1], high[1]], axis=1)
    grad_inner = jnp.concatenate([low[2], high[2]], axis=1)
    grad_outer = jnp.concatenate([low[3], high[3]], axis=0)
    per = d // n
    gain_a = lax.dynamic_slice_in_dim(extra[: d // 128].reshape(-1), me * per, per, 0)
    gain_f = lax.dynamic_slice_in_dim(
        extra[d // 128 : 2 * (d // 128)].reshape(-1), me * per, per, 0
    )
    table = extra[16 : 16 + H, :BUCKETS].T.reshape(-1)
    table = lax.dynamic_slice_in_dim(table, me * rel_table.shape[0], rel_table.shape[0], 0)
    return (
        result,
        grad_hidden,
        gain_a,
        table,
        grads[0],
        grads[1],
        grads[2],
        grad_output,
        gain_f,
        grad_inner,
        grad_outer,
    )


def solution(mesh):
    both = P(("dp", "fsdp"), None)
    line = P("fsdp")
    wide = P("fsdp", None)
    in_specs = (both, line, line, wide, wide, wide, wide, line, wide, wide, P(("dp", "fsdp")), both)
    out_specs = (both, both, line, line, wide, wide, wide, wide, line, wide, wide)
    return jax.shard_map(
        functools.partial(local, Ring(mesh)),
        mesh=mesh,
        in_specs=in_specs,
        out_specs=out_specs,
        check_vma=False,
    )
```

```python
import functools

import jax
import jax.numpy as jnp
import numpy as np
from jax import lax
from jax.experimental import pallas as pl
from jax.experimental.pallas import tpu as pltpu
from jax.sharding import PartitionSpec as P

H = 12
DK = 64
BUCKETS = 32
BLOCK = 512
norm_eps = 1e-06
bucket_edges = (12, 16, 23, 32, 46, 64, 91)
MASKED = -1e30
F32 = jnp.float32
BF16 = jnp.bfloat16
PAIR = 2 * BLOCK
GROUPS = ((0, 512), (512, 256), (768, 128), (896, 128))
SPAN = 1024
SCOPED = {
    "qkv": 7,
    "attend": 5,
    "mid": 8,
    "outer_grad": 4,
    "out": 10,
    "mid_back": 10,
    "mid_grad": 3,
    "attend_back": 9,
    "qkv_grad": 3,
    "in_back": 13,
}


def bucket_of(relative):
    distance = jnp.abs(relative)
    passed = sum(((distance >= edge_value).astype(jnp.int32) for edge_value in bucket_edges))
    return jnp.where(relative > 0, BUCKETS // 2, 0) + jnp.where(
        distance < BUCKETS // 4, distance, BUCKETS // 4 + passed
    )


class Ring:
    def __init__(self, mesh, split=False):
        self.n = mesh.shape["fsdp"]
        self.bits = self.n.bit_length() - 1
        high = list(range(self.bits - 1, 1, -1))
        if split:
            self.order = ([0] + high + [1], [1] + high + [0])
        else:
            self.order = (high + [1, 0], high + [0, 1])

    def swap_phase(self, k):
        n = self.n
        return [
            (c * n + f, c * n + (f ^ (1 << self.order[c][k])))
            for c in range(2)
            for f in range(n)
        ]

    def swap_core(self):
        n = self.n
        return [(c * n + f, (1 - c) * n + f) for c in range(2) for f in range(n)]

    def meta(self):
        me = lax.axis_index("fsdp").astype(jnp.int32)
        core = lax.axis_index("dp").astype(jnp.int32)
        spots = jnp.arange(self.n, dtype=jnp.int32)

        def off(which):
            out = jnp.zeros_like(spots)
            for k, b in enumerate(self.order[which]):
                out = out | (((spots >> k) & 1) << b)
            return out

        def inv(which, m):
            out = jnp.zeros_like(spots)
            for k, b in enumerate(self.order[which]):
                out = out | (((m >> b) & 1) << k)
            return out

        first = core == 0
        mixed = me ^ spots
        return jnp.concatenate(
            [
                core[None],
                me ^ jnp.where(first, off(0), off(1)),
                me ^ jnp.where(first, off(1), off(0)),
                jnp.where(first, inv(0, mixed), inv(1, mixed)),
                jnp.where(first, inv(1, mixed), inv(0, mixed)),
            ]
        )


    def flip_origin(self, pieces):
        me = lax.axis_index("fsdp")
        shape = pieces.shape
        pieces = pieces.reshape((2,) * self.bits + shape[1:])
        for b in range(self.bits):
            axis = self.bits - 1 - b
            pieces = jnp.where((me >> b) & 1 == 1, jnp.flip(pieces, axis), pieces)
        return pieces.reshape(shape)

    def reorder(self, pieces, first, back):
        shape = pieces.shape
        split = pieces.reshape((2,) * self.bits + shape[1:])
        tail = list(range(self.bits, self.bits + len(shape) - 1))
        found = []
        for order in self.order:
            axes = [self.bits - 1 - order.index(self.bits - 1 - a) for a in range(self.bits)]
            if back:
                axes = list(np.argsort(axes))
            found.append(jnp.transpose(split, [int(a) for a in axes] + tail).reshape(shape))
        return jnp.where(first, found[0], found[1])

    def to_origin(self, pieces, first):
        return self.flip_origin(self.reorder(pieces, first, False))

    def from_origin(self, pieces, first):
        return self.reorder(self.flip_origin(pieces), first, True)


def shift(value, pairs):
    return lax.ppermute(value, ("dp", "fsdp"), pairs)


def after(value, *others):
    return lax.optimization_barrier((value, *others))[0]


class Gather:
    def __init__(self, ring, shard):
        self.ring = ring
        self.held = shard[None]
        self.phase = 0
        self.last = None
        self.got = None

    def join(self, *others):
        if self.got is not None:
            got = after(self.got, *others) if others else self.got
            self.held = jnp.concatenate([self.held, got], axis=0)
            self.got = None

    def go(self):
        got = shift(self.held, self.ring.swap_phase(self.phase))
        self.phase += 1
        if self.phase == self.ring.bits:
            self.last = got
        else:
            self.got = got
        return got

    def step(self, *others):
        self.join()
        if others:
            self.held = after(self.held, *others)
        got = self.go()
        return got

    def near(self):
        self.join()
        return self.held

    def finish(self, *others):
        own = (self.held, after(self.last, *others) if others else self.last)
        return own, tuple(shift(p, self.ring.swap_core()) for p in own)


def ready(*moves):
    for move, held in zip(moves, lax.optimization_barrier(tuple(m.held for m in moves))):
        move.held = held


def gather_on(values, *moves):
    values = tuple(values)
    flat = list(values)
    for move in moves:
        move.join(*values)
        flat.append(move.held)
        if move.last is not None:
            flat.append(move.last)
    flat = list(lax.optimization_barrier(tuple(flat)))
    values = [flat.pop(0) for _ in values]
    for move in moves:
        move.held = flat.pop(0)
        if move.last is not None:
            move.last = flat.pop(0)
        else:
            move.go()
    return values


def gather_pieces(ring, shard):
    move = Gather(ring, shard)
    for _ in range(ring.bits):
        move.step()
    return move.finish()


class Reduce:
    def __init__(self, ring, keep, send):
        self.ring = ring
        self.keep = keep
        self.away = send
        self.got = None
        self.phase = ring.bits + 1

    def step(self, *others):
        got = after(self.got, *others) if others else self.got
        self.got = None
        if self.phase == 0:
            return self.keep[0].astype(F32) + got[0].astype(F32)
        half = self.keep.shape[0] // 2

        def add(part):
            return self.keep[part].astype(F32) + got[part].astype(F32)

        self.away = add(slice(half, None)).astype(BF16)
        self.keep = add(slice(0, half))
        if self.phase > 1:
            self.keep = self.keep.astype(BF16)

    def go(self):
        self.phase -= 1
        if self.phase == self.ring.bits:
            pairs = self.ring.swap_core()
        else:
            pairs = self.ring.swap_phase(self.phase)
        self.got = shift(self.away, pairs)

    def finish(self):
        while self.phase > 0:
            if self.got is not None:
                self.step()
            self.go()
        return self.step()


def tick(values, steps=(), fresh=()):
    values = tuple(values)
    for red in steps:
        red.step(*values)
    reds = [*steps, *fresh]
    flat = list(values)
    for red in reds:
        flat += [red.keep, red.away]
    flat = lax.optimization_barrier(tuple(flat))
    for i, red in enumerate(reds):
        red.keep, red.away = flat[len(values) + 2 * i : len(values) + 2 * i + 2]
        red.go()
    return flat[: len(values)]


def sum_all(ring, value):
    value = value + shift(value, ring.swap_core())
    for k in range(ring.bits):
        value = value + shift(value, ring.swap_phase(k))
    return value


def any_spec():
    return pl.BlockSpec(memory_space=pl.ANY)


def params(vmem):
    return pltpu.CompilerParams(vmem_limit_bytes=vmem)


def cost(flops, bytes_accessed, trans=0):
    return pl.CostEstimate(flops=flops, bytes_accessed=bytes_accessed, transcendentals=trans)


def dot(a, b):
    return jnp.dot(a, b, preferred_element_type=F32)


def dot_nt(a, b):
    return lax.dot_general(a, b, (((1,), (1,)), ((), ())), preferred_element_type=F32)


def dot_tn(a, b):
    return lax.dot_general(a, b, (((0,), (0,)), ((), ())), preferred_element_type=F32)


class Pieces:
    def __init__(self, own, rec, n, placed=False):
        self.arrays = [*own, *rec]
        self.n = n
        self.count = len(self.arrays)
        self.part = n // len(own)
        self.whole = False
        self.placed = placed

    def spot(self, meta, h, j):
        place = j if self.placed else meta[1 + h * self.n + j]
        return place, h * (self.count // 2) + j // self.part, j % self.part


class Whole:
    def __init__(self, array):
        self.arrays = [array]
        self.count = 1
        self.whole = True
        self.n = 0


def column_copies(chunk, meta, refs, lo, width, dst, sems, base=0, own_first=False):
    copies = []
    if chunk.whole:
        for h in range(2):
            side = (meta[0] if h == 0 else 1 - meta[0]) if own_first else h
            src = refs[0].at[side, :, pl.ds(lo, width)]
            copies.append(
                pltpu.make_async_copy(src, dst.at[:, pl.ds(h * width, width)], sems.at[base + h])
            )
        return copies
    n = chunk.n
    rows = refs[0].shape[1]
    core = meta[0]
    for h in range(2):
        side = h if own_first else (core if h == 0 else 1 - core)
        col = pl.multiple_of(side * width, 128)
        for j in range(n):
            place, which, index = chunk.spot(meta, h, j)
            row = pl.multiple_of(place * rows, 16)
            copies.append(
                pltpu.make_async_copy(
                    refs[which].at[index, :, pl.ds(lo, width)],
                    dst.at[pl.ds(row, rows), pl.ds(col, width)],
                    sems.at[base + h * n + j],
                )
            )
    return copies


def row_copies(chunk, meta, refs, dst, sems, base=0):
    if chunk.whole:
        return [pltpu.make_async_copy(refs[0], dst, sems.at[base])]
    n = chunk.n
    rows = refs[0].shape[1]
    core = meta[0]
    copies = []
    for h in range(2):
        for j in range(n):
            place, which, index = chunk.spot(meta, h, j)
            row = pl.multiple_of(
                place * (2 * rows) + (core if h == 0 else 1 - core) * rows, 16
            )
            copies.append(
                pltpu.make_async_copy(
                    refs[which].at[index], dst.at[pl.ds(row, rows), :], sems.at[base + h * n + j]
                )
            )
    return copies


def run_copies(copies):
    for c in copies:
        c.start()
    for c in copies:
        c.wait()


def copy_count(chunk):
    return 2 if chunk.whole else 2 * chunk.n


def norm_tile(x, ext_ref, first):
    d = x.shape[1]
    scale = lax.rsqrt(jnp.mean(x * x, axis=-1, keepdims=True) + norm_eps)
    out = []
    for c in range(d // 128):
        out.append(
            (x[:, c * 128 : (c + 1) * 128] * scale * ext_ref[first + c : first + c + 1, :]).astype(
                BF16
            )
        )
    return jnp.concatenate(out, axis=1), scale


def call(body, name, inputs, anys, outs, scratch, flops, trans=0, aliases=None):
    meta, *arrays = inputs
    moved = sum(a.size * a.dtype.itemsize for a in [*arrays, *anys])
    moved += sum(int(np.prod(o.shape)) * jnp.dtype(o.dtype).itemsize for o in outs)
    vmem_spec = pl.BlockSpec(memory_space=pltpu.VMEM)
    return pl.pallas_call(
        body,
        in_specs=[pl.BlockSpec(memory_space=pltpu.SMEM)]
        + [vmem_spec] * len(arrays)
        + [any_spec()] * len(anys),
        out_specs=[vmem_spec] * len(outs),
        out_shape=outs,
        scratch_shapes=scratch,
        input_output_aliases=aliases or {},
        compiler_params=params(SCOPED[name] * 1024 * 1024),
        cost_estimate=cost(flops, moved, trans),
        name=name,
    )(meta, *arrays, *anys)


def array(shape, dtype):
    return jax.ShapeDtypeStruct(shape, dtype)


def qkv_kernel(chunk, tile, meta, x_ref, ext_ref, *rest):
    refs = rest[: chunk.count]
    qkv_ref, n_ref, dist_ref, w, sems = rest[chunk.count :]
    copies = column_copies(chunk, meta, refs, 0, w.shape[1] // 2, w, sems)
    for c in copies:
        c.start()
    place = lax.broadcasted_iota(jnp.int32, (BUCKETS, SPAN), 1)
    row = lax.broadcasted_iota(jnp.int32, (BUCKETS, SPAN), 0)
    chosen = (bucket_of(BLOCK - 1 - place) == row).astype(F32).astype(BF16)
    dist_ref[...] = dot(ext_ref[16:32, 0:BUCKETS].astype(BF16), chosen)
    rows = x_ref.shape[0]
    for r in range(0, rows, tile):
        n_ref[r : r + tile, :] = norm_tile(x_ref[r : r + tile, :].astype(F32), ext_ref, 0)[0]
    for c in copies:
        c.wait()
    for c in range(0, w.shape[1], 256):
        qkv_ref[:, c : c + 256] = dot(n_ref[...], w[:, c : c + 256]).astype(BF16)


def qkv_call(meta, x, ext, chunk):
    rows, d = x.shape
    return call(
        functools.partial(qkv_kernel, chunk, rows // 4),
        "qkv",
        (meta, x, ext),
        chunk.arrays,
        [array((rows, 3 * d), BF16), array((rows, d), BF16), array((16, SPAN), F32)],
        [pltpu.VMEM((d, 3 * d), BF16), pltpu.SemaphoreType.DMA((copy_count(chunk),))],
        6 * rows * d * d,
    )


def bias_strip(dist_row):
    spread = jnp.broadcast_to(dist_row, (128, SPAN))
    return pltpu.roll(spread, SPAN - 127, 1, stride=1, stride_axis=0)


def strip_bias(strip, size, i0, step):
    return jnp.concatenate(
        [
            strip[:, (3 - t) * 128 + i0 : (3 - t) * 128 + i0 + step]
            for t in range(size // 128)
        ],
        axis=0,
    )


def attend_kernel(first, count, meta, qkv_ref, qaug_ref, kaug_ref, dist_ref, ctx_ref, lse_ref):
    rows = qkv_ref.shape[0]
    for base in range(0, rows, PAIR):
        lane = lax.broadcasted_iota(jnp.int32, (PAIR, 128), 1)
        qaug, kaug = qaug_ref[base : base + PAIR, :], kaug_ref[base : base + PAIR, :]
        for pair in range(count):
            at = first + pair
            col = (at // 3) * 9 * 128 + (at % 3) * 128
            q = qkv_ref[base : base + PAIR, col : col + 128]
            k = qkv_ref[base : base + PAIR, col + 384 : col + 512]
            v_turned = qkv_ref[base : base + PAIR, col + 768 : col + 896].T
            heads = []
            for hh in range(2):
                mine = (lane // 64) == hh
                heads.append(
                    (
                        jnp.where(mine, q, qaug),
                        jnp.where(mine, k, kaug),
                        v_turned[hh * 64 : (hh + 1) * 64, :],
                        bias_strip(dist_ref[2 * at + hh : 2 * at + hh + 1, :]),
                    )
                )
            for off, size in GROUPS:
                step = min(256, size)
                for i0 in range(0, size, step):
                    lo, hi = off + i0, off + i0 + step
                    parts = []
                    for hh in range(2):
                        qa, ka, vt, strip = heads[hh]
                        scores = dot_nt(ka[off : off + size], qa[lo:hi])
                        scores = scores + strip_bias(strip, size, i0, step)
                        top = jnp.max(scores, axis=0, keepdims=True)
                        expo = jnp.exp(scores - top)
                        total = jnp.sum(expo, axis=0, keepdims=True)
                        mixed = dot(vt[:, off : off + size], expo.astype(BF16))
                        parts.append(mixed * (1.0 / total))
                        lse_ref[2 * pair + hh : 2 * pair + hh + 1, base + lo : base + hi] = (
                            top + jnp.log(total)
                        )
                    both = jnp.concatenate(parts, axis=0)
                    ctx_ref[base + lo : base + hi, pair * 128 : (pair + 1) * 128] = both.T.astype(
                        BF16
                    )


def attend_call(meta, qkv, qaug, kaug, dist, first, count):
    rows = qkv.shape[0]
    pairs = rows // PAIR
    return call(
        functools.partial(attend_kernel, first, count),
        "attend",
        (meta, qkv, qaug, kaug, dist),
        (),
        [array((rows, count * 128), BF16), array((2 * count, rows), F32)],
        [],
        8 * pairs * count * 350000 * 128,
        trans=2 * pairs * count * 350000,
    )


def mid_kernel(chunk, tile, meta, low_ref, high_ref, x_ref, ext_ref, *rest):
    refs = rest[: chunk.count]
    mid_ref, n2_ref, act_ref, slope_ref, wo, w1, sems = rest[chunk.count :]
    d = wo.shape[0]
    n = copy_count(chunk)
    first = column_copies(chunk, meta, refs, 0, d // 2, wo, sems)
    second = column_copies(chunk, meta, refs, d // 2, w1.shape[1] // 2, w1, sems, n)
    for c in first + second:
        c.start()
    for c in first:
        c.wait()
    rows = x_ref.shape[0]
    for r in range(0, rows, tile):
        span = slice(r, r + tile)
        ctx = jnp.concatenate([low_ref[span, :], high_ref[span, :]], axis=1)
        middle = x_ref[span, :].astype(F32) + dot(ctx, wo[...])
        mid_ref[span, :] = middle
        n2_ref[span, :] = norm_tile(middle, ext_ref, 6)[0]
    for c in second:
        c.wait()
    c0 = 0.7978845608028654
    c1 = c0 * 0.044715
    step = 256
    for f in range(0, w1.shape[1], step):
        for r in range(0, rows, tile):
            span = slice(r, r + tile)
            v = dot(n2_ref[span, :], w1[:, f : f + step])
            v2 = v * v
            half = 0.5 + 0.5 * jnp.tanh(v * (c0 + c1 * v2))
            active = v * half
            act_ref[span, f : f + step] = active.astype(BF16)
            slope_ref[span, f : f + step] = (
                half + (active - active * half) * (2.0 * c0 + (6.0 * c1) * v2)
            ).astype(BF16)


def mid_call(meta, ctxs, x, ext, chunk, ff):
    rows, d = x.shape
    return call(
        functools.partial(mid_kernel, chunk, rows // 4),
        "mid",
        (meta, *ctxs, x, ext),
        chunk.arrays,
        [
            array((rows, d), F32),
            array((rows, d), BF16),
            array((rows, ff), BF16),
            array((rows, ff), BF16),
        ],
        [
            pltpu.VMEM((d, d), BF16),
            pltpu.VMEM((d, ff), BF16),
            pltpu.SemaphoreType.DMA((2 * copy_count(chunk),)),
        ],
        2 * rows * d * (d + ff),
        trans=rows * ff,
    )


def outer_grad_kernel(n, meta, act_ref, g_ref, keep_ref, send_ref):
    per = keep_ref.shape[1]
    first = meta[0] == 0
    width = 4 * per * 2
    for b in range(act_ref.shape[1] // width):
        total = dot_tn(act_ref[:, b * width : (b + 1) * width], g_ref[...]).astype(BF16)
        for f in range(4):
            low = total[2 * f * per : (2 * f + 1) * per]
            high = total[(2 * f + 1) * per : (2 * f + 2) * per]
            spot = b * 4 + f
            keep_ref[meta[1 + 2 * n + spot]] = jnp.where(first, low, high)
            send_ref[meta[1 + 3 * n + spot]] = jnp.where(first, high, low)


def outer_grad_call(meta, act, g, n):
    rows, ff = act.shape
    d = g.shape[1]
    shape = array((n, ff // n // 2, d), BF16)
    return call(
        functools.partial(outer_grad_kernel, n),
        "outer_grad",
        (meta, act, g),
        (),
        [shape, shape],
        [],
        2 * rows * d * ff,
    )


def out_kernel(chunk, tile, meta, act_ref, mid_ref, g_ref, slope_ref, *rest):
    refs = rest[: chunk.count]
    result_ref, din_ref, w2, sems = rest[chunk.count :]
    run_copies(row_copies(chunk, meta, refs, w2, sems))
    rows = g_ref.shape[0]
    step = 256
    for f in range(0, w2.shape[0], step):
        for r in range(0, rows, tile):
            span = slice(r, r + tile)
            d_act = dot_nt(g_ref[span, :], w2[f : f + step, :])
            slope = slope_ref[span, f : f + step].astype(F32)
            din_ref[span, f : f + step] = (d_act * slope).astype(BF16)
    for c in range(0, w2.shape[1], step):
        result_ref[:, c : c + step] = mid_ref[:, c : c + step] + dot(
            act_ref[...], w2[:, c : c + step]
        )


def out_call(meta, act, middle, g, slope, chunk):
    rows, ff = act.shape
    d = middle.shape[1]
    return call(
        functools.partial(out_kernel, chunk, rows // 4),
        "out",
        (meta, act, middle, g, slope),
        chunk.arrays,
        [array((rows, d), F32), array((rows, ff), BF16)],
        [pltpu.VMEM((ff, d), BF16), pltpu.SemaphoreType.DMA((copy_count(chunk),))],
        4 * rows * d * ff,
        aliases={4: 1},
    )


def store_pieces(out, spots, base, total, rows, cols, first=0):
    for f in range(total.shape[0] // rows):
        out[spots[base + first + f], :, cols] = total[f * rows : (f + 1) * rows]


def mid_grad_kernel(n, meta, n2_ref, low_ref, high_ref, din_ref, datt_ref, keep_ref, send_ref):
    per = keep_ref.shape[1]
    h = datt_ref.shape[1] // 2
    ffh = din_ref.shape[1] // 2
    step = 512
    for out, side, table in ((send_ref, 1 - meta[0], 3), (keep_ref, meta[0], 2)):
        base = 1 + table * n
        col = pl.multiple_of(side * h, 128)
        datt = datt_ref[:, pl.ds(col, h)]
        for part, c_ref in enumerate((low_ref, high_ref)):
            total = dot_tn(c_ref[...], datt).astype(BF16)
            store_pieces(out, meta, base, total, per, slice(0, h), part * (n // 2))
        for c in range(0, ffh, step):
            col = pl.multiple_of(side * ffh + c, 128)
            total = dot_tn(n2_ref[...], din_ref[:, pl.ds(col, step)]).astype(BF16)
            store_pieces(out, meta, base, total, per, slice(h + c, h + c + step))


def mid_grad_call(meta, n2, ctxs, d_inner, d_att, n):
    rows, d = n2.shape
    ff = d_inner.shape[1]
    shape = array((n, d // n, (d + ff) // 2), BF16)
    return call(
        functools.partial(mid_grad_kernel, n),
        "mid_grad",
        (meta, n2, *ctxs, d_inner, d_att),
        (),
        [shape, shape],
        [],
        2 * rows * d * (d + ff),
    )


def qkv_grad_kernel(n, table, meta, n_ref, d_ref, out_ref):
    h = d_ref.shape[2]
    for t in range(3):
        total = dot_tn(n_ref[...], d_ref[t]).astype(BF16)
        store_pieces(
            out_ref, meta, 1 + table * n, total, out_ref.shape[1], slice(t * h, (t + 1) * h)
        )


def qkv_grad_call(meta, normed, dqkv, n, table):
    rows, d = normed.shape
    h = dqkv.shape[2]
    return call(
        functools.partial(qkv_grad_kernel, n, table),
        "qkv_grad",
        (meta, normed, dqkv),
        (),
        [array((n, d // n, 3 * h), BF16)],
        [],
        6 * rows * d * h,
    )[0]


def norm_back(dn, x, gain_ref, first, scale):
    d = x.shape[1]
    z = jnp.concatenate(
        [
            dn[:, c * 128 : (c + 1) * 128] * gain_ref[first + c : first + c + 1, :]
            for c in range(d // 128)
        ],
        axis=1,
    )
    inner = jnp.mean(z * x, axis=-1, keepdims=True)
    back = scale * z - x * (scale * scale * scale * inner)
    return back, jnp.sum(dn * (x * scale), axis=0, keepdims=True)


def mid_back_kernel(chunk, tile, meta, din_ref, mid_ref, g_ref, ext_ref, *rest):
    refs = rest[: chunk.count]
    dmid_ref, datt_ref, dctx_ref, gain_ref, wo, w1, sems = rest[chunk.count :]
    d = wo.shape[0]
    n = copy_count(chunk)
    first = column_copies(chunk, meta, refs, d // 2, w1.shape[1] // 2, w1, sems, n)
    second = column_copies(chunk, meta, refs, 0, d // 2, wo, sems)
    for c in first + second:
        c.start()
    for c in first:
        c.wait()
    rows = g_ref.shape[0]
    gains = []
    for r in range(0, rows, tile):
        span = slice(r, r + tile)
        dn = dot_nt(din_ref[span, :], w1[...])
        middle = mid_ref[span, :]
        scale = lax.rsqrt(jnp.mean(middle * middle, axis=-1, keepdims=True) + norm_eps)
        back, gain = norm_back(dn, middle, ext_ref, 6, scale)
        gains.append(gain)
        dmid = g_ref[span, :].astype(F32) + back
        dmid_ref[span, :] = dmid
        datt_ref[span, :] = dmid.astype(BF16)
        if r == 0:
            for c in second:
                c.wait()
        dctx_ref[span, :] = dot_nt(datt_ref[span, :], wo[...]).astype(BF16)
    gain_ref[...] = sum(gains)


def mid_back_call(meta, din, middle, g, ext, chunk):
    rows, ff = din.shape
    d = middle.shape[1]
    return call(
        functools.partial(mid_back_kernel, chunk, rows // 4),
        "mid_back",
        (meta, din, middle, g, ext),
        chunk.arrays,
        [
            array((rows, d), F32),
            array((rows, d), BF16),
            array((rows, d), BF16),
            array((1, d), F32),
        ],
        [
            pltpu.VMEM((d, d), BF16),
            pltpu.VMEM((d, ff), BF16),
            pltpu.SemaphoreType.DMA((2 * copy_count(chunk),)),
        ],
        2 * rows * d * (d + ff),
    )


def diagonal_sums(strip):
    for s in (64, 32, 16, 8):
        strip = strip[:s] + pltpu.roll(strip[s:], SPAN - s, 1)
    for s in (4, 2, 1):
        strip = strip + pltpu.roll(pltpu.roll(strip, 8 - s, 0), SPAN - s, 1)
    return strip[:1]


def attend_back_kernel(
    keep,
    meta,
    qkv_ref,
    dctx_ref,
    qaug_ref,
    kaug_ref,
    dist_ref,
    lse_ref,
    grad_ref,
    table_ref,
    strip_acc,
):
    side = meta[0] if keep else 1 - meta[0]
    count = H // 4
    rows = qkv_ref.shape[0]
    lane = lax.broadcasted_iota(jnp.int32, (PAIR, 128), 1)
    for pair in range(count):
        strip_acc[...] = jnp.zeros_like(strip_acc)
        strips = [
            bias_strip(dist_ref[pl.ds(side * 6 + 2 * pair + hh, 1), :]) for hh in range(2)
        ]
        for base in range(0, rows, PAIR):
            block = slice(base, base + PAIR)

            def part(t):
                col = pl.multiple_of(side * 1152 + (t * 3 + pair) * 128, 128)
                return qkv_ref[block, pl.ds(col, 128)]

            q, k, v = part(0), part(1), part(2)
            do = dctx_ref[block, pl.ds(pl.multiple_of(side * 384 + pair * 128, 128), 128)]
            lse = [lse_ref[pl.ds(side * 6 + 2 * pair + hh, 1), block] for hh in range(2)]
            qaug, kaug = qaug_ref[block, :], kaug_ref[block, :]
            k_turned = k.T
            heads = []
            for hh in range(2):
                mine = (lane // 64) == hh
                heads.append(
                    (
                        jnp.where(mine, q, qaug),
                        jnp.where(mine, k, kaug),
                        jnp.where(mine, v, jnp.zeros_like(v)),
                        k_turned[hh * 64 : (hh + 1) * 64, :],
                        strips[hh],
                    )
                )
            cols = slice(pair * 128, (pair + 1) * 128)
            for off, size in GROUPS:
                step = min(256, size)
                low = lax.broadcasted_iota(jnp.int32, (size, 128), 1) < 64
                dks, dvs = [None, None], [None, None]
                for i0 in range(0, size, step):
                    lo, hi = off + i0, off + i0 + step
                    dqs = []
                    for hh in range(2):
                        qa, ka, va, kt, strip = heads[hh]
                        scores = dot_nt(ka[off : off + size], qa[lo:hi])
                        scores = scores + strip_bias(strip, size, i0, step)
                        probs = jnp.exp(scores - lse[hh][:, lo:hi])
                        d_probs = dot_nt(va[off : off + size], do[lo:hi])
                        dv = dot(probs.astype(BF16), do[lo:hi])
                        center = jnp.sum(probs * d_probs, axis=0, keepdims=True)
                        d_scores = probs * (d_probs - center)
                        for t in range(size // 128):
                            at = (3 - t) * 128 + i0
                            strip_acc[hh, :, at : at + step] += d_scores[t * 128 : (t + 1) * 128]
                        ds_low = d_scores.astype(BF16)
                        dk = dot(ds_low, q[lo:hi])
                        dqs.append(dot(kt[:, off : off + size], ds_low))
                        dks[hh] = dk if dks[hh] is None else dks[hh] + dk
                        dvs[hh] = dv if dvs[hh] is None else dvs[hh] + dv
                    dq = jnp.concatenate(dqs, axis=0).T.astype(BF16)
                    grad_ref[0, base + lo : base + hi, cols] = dq
                out = slice(base + off, base + off + size)
                grad_ref[1, out, cols] = jnp.where(low, dks[0], dks[1]).astype(BF16)
                grad_ref[2, out, cols] = jnp.where(low, dvs[0], dvs[1]).astype(BF16)
        for hh in range(2):
            table_ref[2 * pair + hh : 2 * pair + hh + 1, :] = diagonal_sums(strip_acc[hh])
    table_ref[2 * count :, :] = jnp.zeros((8 - 2 * count, SPAN), F32)


def attend_back_call(meta, qkv, dctx, qaug, kaug, dist, lse, keep):
    rows, d = dctx.shape
    pairs = rows // PAIR
    count = H // 4
    return call(
        functools.partial(attend_back_kernel, keep),
        "attend_back",
        (meta, qkv, dctx, qaug, kaug, dist, lse),
        (),
        [array((3, rows, count * 128), BF16), array((8, SPAN), F32)],
        [pltpu.VMEM((2, 128, SPAN), F32)],
        20 * pairs * count * 350000 * 128,
        trans=2 * pairs * count * 350000,
    )


def in_back_kernel(chunk, tile, meta, own_ref, rec_ref, x_ref, dmid_ref, ext_ref, *rest):
    stay_ref, away_ref, gain_ref, *rest = rest
    refs = rest[: chunk.count]
    dx_ref, extra_ref, w, sems = rest[chunk.count :]
    copies = column_copies(chunk, meta, refs, 0, w.shape[1] // 2, w, sems, own_first=True)
    for c in copies:
        c.start()
    place = (lax.broadcasted_iota(jnp.int32, (128, SPAN), 1) + 127) % SPAN
    row = lax.broadcasted_iota(jnp.int32, (128, SPAN), 0)
    chosen = (bucket_of(BLOCK - 1 - place) == row).astype(F32)
    found = [
        lax.dot_general(
            r[...],
            chosen,
            (((1,), (1,)), ((), ())),
            precision=lax.Precision.HIGHEST,
            preferred_element_type=F32,
        )[: H // 2]
        for r in (stay_ref, away_ref)
    ]
    first = meta[0] == 0
    extra_ref[...] = jnp.zeros_like(extra_ref)
    extra_ref[16 : 16 + H // 2, :] = jnp.where(first, found[0], found[1])
    extra_ref[16 + H // 2 : 16 + H, :] = jnp.where(first, found[1], found[0])
    for c in copies:
        c.wait()
    rows, d = x_ref.shape
    gains = []
    for r in range(0, rows, tile):
        span = slice(r, r + tile)
        parts = [ref[t, span, :] for ref in (own_ref, rec_ref) for t in range(3)]
        dn = dot_nt(jnp.concatenate(parts, axis=1), w[...])
        x = x_ref[span, :].astype(F32)
        scale = lax.rsqrt(jnp.mean(x * x, axis=-1, keepdims=True) + norm_eps)
        back, gain = norm_back(dn, x, ext_ref, 0, scale)
        gains.append(gain)
        dx_ref[span, :] = dmid_ref[span, :] + back
    total = sum(gains)
    for c in range(d // 128):
        extra_ref[c : c + 1, :] = total[:, c * 128 : (c + 1) * 128]
        extra_ref[6 + c : 7 + c, :] = gain_ref[:, c * 128 : (c + 1) * 128]


def in_back_call(meta, own, rec, x, dmid, ext, found, gain, chunk):
    rows, d = x.shape
    return call(
        functools.partial(in_back_kernel, chunk, rows // 4),
        "in_back",
        (meta, own, rec, x, dmid, ext, *found, gain),
        chunk.arrays,
        [array((rows, d), F32), array((32, 128), F32)],
        [pltpu.VMEM((d, 3 * d), BF16), pltpu.SemaphoreType.DMA((copy_count(chunk),))],
        6 * rows * d * d,
    )


def mask_lanes(lengths, rows):
    spot = jnp.arange(rows, dtype=jnp.int32)
    within = spot % PAIR
    first = jnp.array([0, 512, 768, 896, 960], jnp.int32)
    slot = jnp.sum((within[:, None] >= first[None, 1:]).astype(jnp.int32), axis=1)
    start = jnp.sum(jnp.where(slot[:, None] == jnp.arange(5)[None], first[None], 0), axis=1)
    docs = jnp.arange(lengths.shape[0], dtype=jnp.int32)
    document = spot // PAIR * 5 + slot
    own = jnp.sum(jnp.where(document[:, None] == docs[None], lengths[None], 0), axis=1)
    live = within - start < own
    late = slot == 4
    lane = jnp.arange(128, dtype=jnp.int32) % 64
    shown = [live & ~late, live & late]
    kaug = jnp.where(
        lane[None] == 0,
        jnp.where(shown[0], 0.0, MASKED)[:, None],
        jnp.where(lane[None] == 1, jnp.where(shown[1], 0.0, MASKED)[:, None], 0.0),
    ).astype(BF16)
    qaug = jnp.where(
        lane[None] == 0,
        jnp.where(late, 0.0, 1.0)[:, None],
        jnp.where(lane[None] == 1, jnp.where(late, 1.0, 0.0)[:, None], 0.0),
    ).astype(BF16)
    return qaug, kaug, live


def placed_rows(vector, me, rows):
    count = vector.shape[0]
    spot = jnp.arange(rows * 128, dtype=jnp.int32)[None] - me * count
    hit = spot == jnp.arange(count, dtype=jnp.int32)[:, None]
    flat = jnp.sum(jnp.where(hit, vector.astype(F32)[:, None], 0.0), axis=0)
    return flat.reshape(rows, 128)


def placed_table(vector, me):
    count = vector.shape[0]
    head = jnp.arange(16, dtype=jnp.int32)[:, None]
    bucket = jnp.arange(128, dtype=jnp.int32)[None]
    entry = jnp.where((head < H) & (bucket < BUCKETS), bucket * H + head, -1) - me * count
    hit = entry[None] == jnp.arange(count, dtype=jnp.int32)[:, None, None]
    return jnp.sum(jnp.where(hit, vector.astype(F32)[:, None, None], 0.0), axis=0)


def local(
    ring,
    ring_c,
    hidden,
    gain_attn,
    rel_table,
    query_weight,
    key_weight,
    value_weight,
    output_weight,
    gain_ffn,
    inner_weight,
    outer_weight,
    lengths,
    cotangent,
):
    rows, d = hidden.shape
    ff = inner_weight.shape[1]
    n = ring.n
    shard_rows = query_weight.shape[0]
    outer_rows = outer_weight.shape[0]
    direct = shard_rows % 16 == 0 and shard_rows >= 32 and outer_rows % 32 == 0
    me = lax.axis_index("fsdp")
    core = lax.axis_index("dp")
    meta = ring.meta()
    meta_c = ring_c.meta()
    h = d // 2

    def half(w, which):
        width = w.shape[1] // 2
        return lax.dynamic_slice_in_dim(w, which * width, width, 1)

    small = jnp.concatenate(
        [
            placed_rows(gain_attn, me, d // 128),
            placed_rows(gain_ffn, me, d // 128),
            jnp.zeros((16 - 2 * (d // 128), 128), F32),
            placed_table(rel_table, me),
        ],
        axis=0,
    ).astype(BF16)
    pack_a = [half(w, core) for w in (query_weight, key_weight, value_weight)]
    if direct:
        pack_a.append(jnp.pad(small, ((0, shard_rows - 32), (0, 0))))
    pack_a = jnp.concatenate(pack_a, axis=1)
    pack_b = jnp.concatenate([half(output_weight, core), half(inner_weight, core)], axis=1)
    pack_c = lax.dynamic_slice_in_dim(
        outer_weight, core * (outer_rows // 2), outer_rows // 2, 0
    )

    def whole_columns(own, rec):
        both = []
        for parts, first in ((own, core == 0), (rec, core == 1)):
            pieces = ring.to_origin(jnp.concatenate(parts, axis=0), first)
            both.append(pieces.reshape(-1, pieces.shape[2]))
        first = jnp.where(core == 0, both[0], both[1])
        second = jnp.where(core == 0, both[1], both[0])
        return jnp.stack([first, second])

    qaug, kaug, live = mask_lanes(lengths, rows)
    g = jnp.where(live[:, None], cotangent, jnp.zeros_like(cotangent))
    if direct:
        move_a, move_b = Gather(ring, pack_a), Gather(ring, pack_b)
        move_c = Gather(ring_c, pack_c)
        move_a.go()
        move_c.go()
        for _ in range(ring.bits - 3):
            move_a.join(meta, meta_c, qaug, kaug, g)
            move_a.go()
        move_a.join()
        for _ in range(ring.bits - 3):
            ready(move_a, move_b)
            move_a.go()
            move_b.go()
            move_a.join()
            move_b.join()
        ready(move_a, move_b)
        move_a.go()
        move_b.go()
        move_a.last, move_b.got = lax.optimization_barrier((move_a.last, move_b.got))
        move_b.join()
        final = move_a.last
        move_b.held, final = lax.optimization_barrier((move_b.held, final))
        move_b.go()
        chunk_a = Pieces(*move_a.finish(), n)
        got_a = (chunk_a.arrays[:2],)
        move_c.join(final)
        move_c.go()
        ext = sum(jnp.sum(p[:, :32, 3 * h :].astype(F32), axis=0) for p in got_a[0])
    else:
        got_c = gather_pieces(ring, pack_c)
        chunk_a = Whole(whole_columns(*gather_pieces(ring, pack_a)))
        chunk_b = Whole(whole_columns(*gather_pieces(ring, pack_b)))
        both = [
            ring.to_origin(jnp.concatenate(parts, axis=0), first)
            for parts, first in zip(got_c, (core == 0, core == 1))
        ]
        first = jnp.where(core == 0, both[0], both[1])
        second = jnp.where(core == 0, both[1], both[0])
        chunk_c = Whole(jnp.stack([first, second], axis=1).reshape(ff, d))
        ext = lax.psum(small.astype(F32), "fsdp")

    qkv, normed, dist = qkv_call(meta, hidden, ext, chunk_a)
    if direct:
        (qkv,) = gather_on((qkv,), move_b, move_c)
    ctx0, lse0 = attend_call(meta, qkv, qaug, kaug, dist, 0, H // 4)
    if direct:
        dist, ctx0 = lax.optimization_barrier((dist, ctx0))
    ctx1, lse1 = attend_call(meta, qkv, qaug, kaug, dist, H // 4, H // 4)
    if direct:
        (ctx1,) = gather_on((ctx1,), move_b, move_c)
        chunk_b = Pieces(*move_b.finish(), n)
    ctxs = (ctx0, ctx1)
    middle, normed2, act, slope = mid_call(meta, ctxs, hidden, ext, chunk_b, ff)
    if direct:
        chunk_c = Pieces(*move_c.finish(act), n)

    def split_columns(pairs, which):
        full = [jnp.einsum("td,tf->df", a, b, preferred_element_type=F32) for a, b in pairs]
        part = jnp.concatenate(full, axis=1).astype(BF16)
        part = part.reshape(n, d // n, part.shape[1])
        return ring.from_origin(part, which == 0)

    if direct:
        grad_c = outer_grad_call(meta, act, g, n)
    else:
        full = jnp.einsum("tf,td->fd", act, g, preferred_element_type=F32).astype(BF16)
        full = full.reshape(n, 2, outer_rows // 2, d)
        grad_c = [
            ring.from_origin(
                lax.dynamic_index_in_dim(full, which, 1, keepdims=False), which == 0
            )
            for which in (core, 1 - core)
        ]
    red_c = Reduce(ring, *grad_c)
    (act,) = tick((act,), fresh=(red_c,))
    result, d_inner = out_call(meta_c, act, middle, g, slope, chunk_c)
    (d_inner,) = tick((d_inner,), (red_c,))
    d_middle, d_att, d_ctx, grad_gain_f = mid_back_call(meta, d_inner, middle, g, ext, chunk_b)
    (d_att,) = tick((d_att,), (red_c,))
    if direct:
        grad_b = mid_grad_call(meta, normed2, ctxs, d_inner, d_att, n)
    else:
        both = jnp.concatenate(ctxs, axis=1)
        grad_b = [
            split_columns([(both, half(d_att, w)), (normed2, half(d_inner, w))], w)
            for w in (core, 1 - core)
        ]
    red_b = Reduce(ring, *grad_b)
    (d_ctx,) = tick((after(d_ctx, *grad_b),), (red_c,), (red_b,))
    lse = jnp.concatenate([lse0, lse1], axis=0)
    away, found_away = attend_back_call(meta, qkv, d_ctx, qaug, kaug, dist, lse, False)
    (away,) = tick((away,), (red_c, red_b))
    if direct:
        send_a = qkv_grad_call(meta, normed, away, n, 3)
    else:
        send_a = split_columns([(normed, away[t]) for t in range(3)], 1 - core)
    d_ctx, send_a = lax.optimization_barrier((d_ctx, send_a))
    red_a = Reduce(ring, None, send_a)
    red_a.go()
    stay, found_stay = attend_back_call(meta, qkv, d_ctx, qaug, kaug, dist, lse, True)
    (stay,) = tick((stay,), (red_b,))
    if direct:
        keep_a = qkv_grad_call(meta, normed, stay, n, 2)
    else:
        keep_a = split_columns([(normed, stay[t]) for t in range(3)], core)
    red_a.keep = keep_a
    (stay,) = tick((after(stay, keep_a),), (red_a,))
    grad_hidden, extra = in_back_call(
        meta,
        stay,
        away,
        hidden,
        d_middle,
        ext,
        (found_stay, found_away),
        grad_gain_f,
        chunk_a,
    )
    (extra,) = tick((extra,), (red_b, red_a))
    extra = sum_all(ring, extra)
    sum_c = red_c.finish()
    sum_b = red_b.finish()
    sum_a = red_a.finish()
    sum_o, sum_b = sum_b[:, :h], sum_b[:, h:]
    own = [sum_a, sum_o, sum_b, sum_c]
    other = [shift(s, ring.swap_core()) for s in own]
    low = [jnp.where(core == 0, a, b) for a, b in zip(own, other)]
    high = [jnp.where(core == 0, b, a) for a, b in zip(own, other)]
    grads = [
        jnp.concatenate([low[0][:, t * h : (t + 1) * h], high[0][:, t * h : (t + 1) * h]], axis=1)
        for t in range(3)
    ]
    grad_output = jnp.concatenate([low[1], high[1]], axis=1)
    grad_inner = jnp.concatenate([low[2], high[2]], axis=1)
    grad_outer = jnp.concatenate([low[3], high[3]], axis=0)
    per = d // n
    gain_a = lax.dynamic_slice_in_dim(extra[: d // 128].reshape(-1), me * per, per, 0)
    gain_f = lax.dynamic_slice_in_dim(
        extra[d // 128 : 2 * (d // 128)].reshape(-1), me * per, per, 0
    )
    table = extra[16 : 16 + H, :BUCKETS].T.reshape(-1)
    table = lax.dynamic_slice_in_dim(table, me * rel_table.shape[0], rel_table.shape[0], 0)
    return (
        result,
        grad_hidden,
        gain_a,
        table,
        grads[0],
        grads[1],
        grads[2],
        grad_output,
        gain_f,
        grad_inner,
        grad_outer,
    )


def solution(mesh):
    both = P(("dp", "fsdp"), None)
    line = P("fsdp")
    wide = P("fsdp", None)
    in_specs = (both, line, line, wide, wide, wide, wide, line, wide, wide, P(("dp", "fsdp")), both)
    out_specs = (both, both, line, line, wide, wide, wide, wide, line, wide, wide)
    return jax.shard_map(
        functools.partial(local, Ring(mesh), Ring(mesh, split=True)),
        mesh=mesh,
        in_specs=in_specs,
        out_specs=out_specs,
        check_vma=False,
    )
```

```python
import functools

import jax
import jax.numpy as jnp
import numpy as np
from jax import lax
from jax.experimental import pallas as pl
from jax.experimental.pallas import tpu as pltpu
from jax.sharding import PartitionSpec as P

H = 12
DK = 64
BUCKETS = 32
BLOCK = 512
norm_eps = 1e-06
bucket_edges = (12, 16, 23, 32, 46, 64, 91)
MASKED = -1e30
F32 = jnp.float32
BF16 = jnp.bfloat16
PAIR = 2 * BLOCK
GROUPS = ((0, 512), (512, 256), (768, 128), (896, 128))
SPAN = 1024
SCOPED = {
    "qkv": 10,
    "attend": 5,
    "mid": 8,
    "outer_grad": 4,
    "out": 10,
    "mid_back": 12,
    "mid_grad": 3,
    "attend_back": 8,
    "qkv_grad": 3,
    "in_back": 18,
}


def bucket_of(relative):
    distance = jnp.abs(relative)
    passed = sum(((distance >= edge_value).astype(jnp.int32) for edge_value in bucket_edges))
    return jnp.where(relative > 0, BUCKETS // 2, 0) + jnp.where(
        distance < BUCKETS // 4, distance, BUCKETS // 4 + passed
    )


class Ring:
    def __init__(self, mesh, split=False):
        self.n = mesh.shape["fsdp"]
        self.bits = self.n.bit_length() - 1
        high = list(range(self.bits - 1, 1, -1))
        if split:
            self.order = ([0] + high + [1], [1] + high + [0])
        else:
            self.order = (high + [1, 0], high + [0, 1])

    def swap_phase(self, k):
        n = self.n
        return [
            (c * n + f, c * n + (f ^ (1 << self.order[c][k])))
            for c in range(2)
            for f in range(n)
        ]

    def swap_core(self):
        n = self.n
        return [(c * n + f, (1 - c) * n + f) for c in range(2) for f in range(n)]

    def meta(self):
        me = lax.axis_index("fsdp").astype(jnp.int32)
        core = lax.axis_index("dp").astype(jnp.int32)
        spots = jnp.arange(self.n, dtype=jnp.int32)

        def off(which):
            out = jnp.zeros_like(spots)
            for k, b in enumerate(self.order[which]):
                out = out | (((spots >> k) & 1) << b)
            return out

        def inv(which, m):
            out = jnp.zeros_like(spots)
            for k, b in enumerate(self.order[which]):
                out = out | (((m >> b) & 1) << k)
            return out

        first = core == 0
        mixed = me ^ spots
        return jnp.concatenate(
            [
                core[None],
                me ^ jnp.where(first, off(0), off(1)),
                me ^ jnp.where(first, off(1), off(0)),
                jnp.where(first, inv(0, mixed), inv(1, mixed)),
                jnp.where(first, inv(1, mixed), inv(0, mixed)),
            ]
        )


    def flip_origin(self, pieces):
        me = lax.axis_index("fsdp")
        shape = pieces.shape
        pieces = pieces.reshape((2,) * self.bits + shape[1:])
        for b in range(self.bits):
            axis = self.bits - 1 - b
            pieces = jnp.where((me >> b) & 1 == 1, jnp.flip(pieces, axis), pieces)
        return pieces.reshape(shape)

    def reorder(self, pieces, first, back):
        shape = pieces.shape
        split = pieces.reshape((2,) * self.bits + shape[1:])
        tail = list(range(self.bits, self.bits + len(shape) - 1))
        found = []
        for order in self.order:
            axes = [self.bits - 1 - order.index(self.bits - 1 - a) for a in range(self.bits)]
            if back:
                axes = list(np.argsort(axes))
            found.append(jnp.transpose(split, [int(a) for a in axes] + tail).reshape(shape))
        return jnp.where(first, found[0], found[1])

    def to_origin(self, pieces, first):
        return self.flip_origin(self.reorder(pieces, first, False))

    def from_origin(self, pieces, first):
        return self.reorder(self.flip_origin(pieces), first, True)


def shift(value, pairs):
    return lax.ppermute(value, ("dp", "fsdp"), pairs)


def after(value, *others):
    return lax.optimization_barrier((value, *others))[0]


class Gather:
    def __init__(self, ring, shard):
        self.ring = ring
        self.held = shard[None]
        self.phase = 0
        self.last = None
        self.got = None

    def join(self, *others):
        if self.got is not None:
            got = after(self.got, *others) if others else self.got
            self.held = jnp.concatenate([self.held, got], axis=0)
            self.got = None

    def go(self):
        got = shift(self.held, self.ring.swap_phase(self.phase))
        self.phase += 1
        if self.phase == self.ring.bits:
            self.last = got
        else:
            self.got = got
        return got

    def step(self, *others):
        self.join()
        if others:
            self.held = after(self.held, *others)
        got = self.go()
        return got

    def near(self):
        self.join()
        return self.held

    def finish(self, *others):
        own = (self.held, after(self.last, *others) if others else self.last)
        return own, tuple(shift(p, self.ring.swap_core()) for p in own)


def ready(*moves):
    for move, held in zip(moves, lax.optimization_barrier(tuple(m.held for m in moves))):
        move.held = held


def gather_on(values, *moves):
    values = tuple(values)
    flat = list(values)
    for move in moves:
        move.join(*values)
        flat.append(move.held)
        if move.last is not None:
            flat.append(move.last)
    flat = list(lax.optimization_barrier(tuple(flat)))
    values = [flat.pop(0) for _ in values]
    for move in moves:
        move.held = flat.pop(0)
        if move.last is not None:
            move.last = flat.pop(0)
        else:
            move.go()
    return values


def gather_pieces(ring, shard):
    move = Gather(ring, shard)
    for _ in range(ring.bits):
        move.step()
    return move.finish()


class Reduce:
    def __init__(self, ring, keep, send):
        self.ring = ring
        self.keep = keep
        self.away = send
        self.got = None
        self.phase = ring.bits + 1

    def step(self, *others):
        got = after(self.got, *others) if others else self.got
        self.got = None
        if self.phase == 0:
            return self.keep[0].astype(F32) + got[0].astype(F32)
        half = self.keep.shape[0] // 2

        def add(part):
            return self.keep[part].astype(F32) + got[part].astype(F32)

        self.away = add(slice(half, None)).astype(BF16)
        self.keep = add(slice(0, half))
        if self.phase > 1:
            self.keep = self.keep.astype(BF16)

    def go(self):
        self.phase -= 1
        if self.phase == self.ring.bits:
            pairs = self.ring.swap_core()
        else:
            pairs = self.ring.swap_phase(self.phase)
        self.got = shift(self.away, pairs)

    def finish(self):
        while self.phase > 0:
            if self.got is not None:
                self.step()
            self.go()
        return self.step()


def tick(values, steps=(), fresh=()):
    values = tuple(values)
    for red in steps:
        red.step(*values)
    reds = [*steps, *fresh]
    flat = list(values)
    for red in reds:
        flat += [red.keep, red.away]
    flat = lax.optimization_barrier(tuple(flat))
    for i, red in enumerate(reds):
        red.keep, red.away = flat[len(values) + 2 * i : len(values) + 2 * i + 2]
        red.go()
    return flat[: len(values)]


def params(vmem):
    return pltpu.CompilerParams(vmem_limit_bytes=vmem)


def cost(flops, bytes_accessed, trans=0):
    return pl.CostEstimate(flops=flops, bytes_accessed=bytes_accessed, transcendentals=trans)


def dot(a, b):
    return jnp.dot(a, b, preferred_element_type=F32)


def dot_nt(a, b):
    return lax.dot_general(a, b, (((1,), (1,)), ((), ())), preferred_element_type=F32)


def dot_tn(a, b):
    return lax.dot_general(a, b, (((0,), (0,)), ((), ())), preferred_element_type=F32)


class Pieces:
    def __init__(self, own, rec, n, placed=False):
        self.arrays = [*own, *rec]
        self.n = n
        self.count = len(self.arrays)
        self.part = n // len(own)
        self.whole = False
        self.placed = placed

    def spot(self, meta, h, j):
        place = j if self.placed else meta[1 + h * self.n + j]
        return place, h * (self.count // 2) + j // self.part, j % self.part


class Whole:
    def __init__(self, array):
        self.arrays = [array]
        self.count = 1
        self.whole = True
        self.n = 0


def load_columns(chunk, meta, refs, lo, width, dst, own_first=False):
    core = meta[0]
    if chunk.whole:
        for h in range(2):
            side = (core if h == 0 else 1 - core) if own_first else h
            dst[:, h * width : (h + 1) * width] = refs[0][side, :, lo : lo + width]
        return
    rows = refs[0].shape[1]
    for h in range(2):
        side = h if own_first else (core if h == 0 else 1 - core)
        col = pl.multiple_of(side * width, 128)
        for j in range(chunk.n):
            place, which, index = chunk.spot(meta, h, j)
            row = pl.multiple_of(place * rows, 16)
            dst[pl.ds(row, rows), pl.ds(col, width)] = refs[which][index, :, lo : lo + width]


def load_rows(chunk, meta, refs, dst):
    if chunk.whole:
        dst[...] = refs[0][...]
        return
    rows = refs[0].shape[1]
    core = meta[0]
    for h in range(2):
        for j in range(chunk.n):
            place, which, index = chunk.spot(meta, h, j)
            row = pl.multiple_of(place * (2 * rows) + (core if h == 0 else 1 - core) * rows, 16)
            dst[pl.ds(row, rows), :] = refs[which][index]


def norm_tile(x, ext_ref, first):
    d = x.shape[1]
    scale = lax.rsqrt(jnp.mean(x * x, axis=-1, keepdims=True) + norm_eps)
    out = []
    for c in range(d // 128):
        out.append(
            (x[:, c * 128 : (c + 1) * 128] * scale * ext_ref[first + c : first + c + 1, :]).astype(
                BF16
            )
        )
    return jnp.concatenate(out, axis=1), scale


def call(body, name, inputs, parts, outs, scratch, flops, trans=0, aliases=None):
    meta, *arrays = inputs
    moved = sum(a.size * a.dtype.itemsize for a in [*arrays, *parts])
    moved += sum(int(np.prod(o.shape)) * jnp.dtype(o.dtype).itemsize for o in outs)
    vmem_spec = pl.BlockSpec(memory_space=pltpu.VMEM)
    return pl.pallas_call(
        body,
        in_specs=[pl.BlockSpec(memory_space=pltpu.SMEM)]
        + [vmem_spec] * (len(arrays) + len(parts)),
        out_specs=[vmem_spec] * len(outs),
        out_shape=outs,
        scratch_shapes=scratch,
        input_output_aliases=aliases or {},
        compiler_params=params(SCOPED[name] * 1024 * 1024),
        cost_estimate=cost(flops, moved, trans),
        name=name,
    )(meta, *arrays, *parts)


def array(shape, dtype):
    return jax.ShapeDtypeStruct(shape, dtype)


def qkv_kernel(chunk, tile, meta, x_ref, *rest):
    refs = rest[: chunk.count]
    *given, qkv_ref, n_ref, dist_ref, ext_ref, w = rest[chunk.count :]
    if given:
        ext_ref[...] = given[0][...]
    else:
        lo = w.shape[1] // 2
        ext_ref[...] = sum(
            ref[j, 0:32, lo : lo + 128].astype(F32)
            for ref in refs[: chunk.count // 2]
            for j in range(chunk.part)
        )
    load_columns(chunk, meta, refs, 0, w.shape[1] // 2, w)
    place = lax.broadcasted_iota(jnp.int32, (BUCKETS, SPAN), 1)
    row = lax.broadcasted_iota(jnp.int32, (BUCKETS, SPAN), 0)
    chosen = (bucket_of(BLOCK - 1 - place) == row).astype(F32).astype(BF16)
    dist_ref[...] = dot(ext_ref[16:32, 0:BUCKETS].astype(BF16), chosen)
    rows = x_ref.shape[0]
    for r in range(0, rows, tile):
        n_ref[r : r + tile, :] = norm_tile(x_ref[r : r + tile, :].astype(F32), ext_ref, 0)[0]
    for c in range(0, w.shape[1], 256):
        qkv_ref[:, c : c + 256] = dot(n_ref[...], w[:, c : c + 256]).astype(BF16)


def qkv_call(meta, x, ext, chunk):
    rows, d = x.shape
    return call(
        functools.partial(qkv_kernel, chunk, rows // 4),
        "qkv",
        (meta, x),
        chunk.arrays + ([] if ext is None else [ext]),
        [
            array((rows, 3 * d), BF16),
            array((rows, d), BF16),
            array((16, SPAN), F32),
            array((32, 128), F32),
        ],
        [pltpu.VMEM((d, 3 * d), BF16)],
        6 * rows * d * d,
    )


def bias_strip(dist_row):
    spread = jnp.broadcast_to(dist_row, (128, SPAN))
    return pltpu.roll(spread, SPAN - 127, 1, stride=1, stride_axis=0)


def strip_bias(strip, size, i0, step):
    return jnp.concatenate(
        [
            strip[:, (3 - t) * 128 + i0 : (3 - t) * 128 + i0 + step]
            for t in range(size // 128)
        ],
        axis=0,
    )


def attend_kernel(first, count, meta, qkv_ref, qaug_ref, kaug_ref, dist_ref, ctx_ref, lse_ref):
    rows = qkv_ref.shape[0]
    for base in range(0, rows, PAIR):
        lane = lax.broadcasted_iota(jnp.int32, (PAIR, 128), 1)
        qaug, kaug = qaug_ref[base : base + PAIR, :], kaug_ref[base : base + PAIR, :]
        for pair in range(count):
            at = first + pair
            col = (at // 3) * 9 * 128 + (at % 3) * 128
            q = qkv_ref[base : base + PAIR, col : col + 128]
            k = qkv_ref[base : base + PAIR, col + 384 : col + 512]
            v_turned = qkv_ref[base : base + PAIR, col + 768 : col + 896].T
            heads = []
            for hh in range(2):
                mine = (lane // 64) == hh
                heads.append(
                    (
                        jnp.where(mine, q, qaug),
                        jnp.where(mine, k, kaug),
                        v_turned[hh * 64 : (hh + 1) * 64, :],
                        bias_strip(dist_ref[2 * at + hh : 2 * at + hh + 1, :]),
                    )
                )
            for off, size in GROUPS:
                step = size
                for i0 in range(0, size, step):
                    lo, hi = off + i0, off + i0 + step
                    parts = []
                    for hh in range(2):
                        qa, ka, vt, strip = heads[hh]
                        scores = dot_nt(ka[off : off + size], qa[lo:hi])
                        scores = scores + strip_bias(strip, size, i0, step)
                        top = jnp.max(scores, axis=0, keepdims=True)
                        expo = jnp.exp(scores - top)
                        total = jnp.sum(expo, axis=0, keepdims=True)
                        mixed = dot(vt[:, off : off + size], expo.astype(BF16))
                        parts.append(mixed * (1.0 / total))
                        lse_ref[2 * pair + hh : 2 * pair + hh + 1, base + lo : base + hi] = (
                            top + jnp.log(total)
                        )
                    both = jnp.concatenate(parts, axis=0)
                    ctx_ref[base + lo : base + hi, pair * 128 : (pair + 1) * 128] = both.T.astype(
                        BF16
                    )


def attend_call(meta, qkv, qaug, kaug, dist, first, count):
    rows = qkv.shape[0]
    pairs = rows // PAIR
    return call(
        functools.partial(attend_kernel, first, count),
        "attend",
        (meta, qkv, qaug, kaug, dist),
        (),
        [array((rows, count * 128), BF16), array((2 * count, rows), F32)],
        [],
        8 * pairs * count * 350000 * 128,
        trans=2 * pairs * count * 350000,
    )


def mid_kernel(chunk, tile, meta, low_ref, high_ref, x_ref, ext_ref, *rest):
    refs = rest[: chunk.count]
    mid_ref, n2_ref, act_ref, slope_ref, wo, w1 = rest[chunk.count :]
    d = wo.shape[0]
    load_columns(chunk, meta, refs, 0, d // 2, wo)
    load_columns(chunk, meta, refs, d // 2, w1.shape[1] // 2, w1)
    rows = x_ref.shape[0]
    for r in range(0, rows, tile):
        span = slice(r, r + tile)
        ctx = jnp.concatenate([low_ref[span, :], high_ref[span, :]], axis=1)
        middle = x_ref[span, :].astype(F32) + dot(ctx, wo[...])
        mid_ref[span, :] = middle
        n2_ref[span, :] = norm_tile(middle, ext_ref, 6)[0]
    c0 = 0.7978845608028654
    c1 = c0 * 0.044715
    step = 256
    for f in range(0, w1.shape[1], step):
        for r in range(0, rows, tile):
            span = slice(r, r + tile)
            v = dot(n2_ref[span, :], w1[:, f : f + step])
            v2 = v * v
            half = 0.5 + 0.5 * jnp.tanh(v * (c0 + c1 * v2))
            active = v * half
            act_ref[span, f : f + step] = active.astype(BF16)
            slope_ref[span, f : f + step] = (
                half + (active - active * half) * (2.0 * c0 + (6.0 * c1) * v2)
            ).astype(BF16)


def mid_call(meta, ctxs, x, ext, chunk, ff):
    rows, d = x.shape
    return call(
        functools.partial(mid_kernel, chunk, rows),
        "mid",
        (meta, *ctxs, x, ext),
        chunk.arrays,
        [
            array((rows, d), F32),
            array((rows, d), BF16),
            array((rows, ff), BF16),
            array((rows, ff), BF16),
        ],
        [
            pltpu.VMEM((d, d), BF16),
            pltpu.VMEM((d, ff), BF16),
        ],
        2 * rows * d * (d + ff),
        trans=rows * ff,
    )


def outer_grad_kernel(n, meta, act_ref, g_ref, keep_ref, send_ref):
    per = keep_ref.shape[1]
    first = meta[0] == 0
    width = 4 * per * 2
    for b in range(act_ref.shape[1] // width):
        total = dot_tn(act_ref[:, b * width : (b + 1) * width], g_ref[...]).astype(BF16)
        for f in range(4):
            low = total[2 * f * per : (2 * f + 1) * per]
            high = total[(2 * f + 1) * per : (2 * f + 2) * per]
            spot = b * 4 + f
            keep_ref[meta[1 + 2 * n + spot]] = jnp.where(first, low, high)
            send_ref[meta[1 + 3 * n + spot]] = jnp.where(first, high, low)


def outer_grad_call(meta, act, g, n):
    rows, ff = act.shape
    d = g.shape[1]
    shape = array((n, ff // n // 2, d), BF16)
    return call(
        functools.partial(outer_grad_kernel, n),
        "outer_grad",
        (meta, act, g),
        (),
        [shape, shape],
        [],
        2 * rows * d * ff,
    )


def out_kernel(chunk, tile, meta, act_ref, mid_ref, g_ref, slope_ref, *rest):
    refs = rest[: chunk.count]
    result_ref, din_ref, w2 = rest[chunk.count :]
    load_rows(chunk, meta, refs, w2)
    rows = g_ref.shape[0]
    step = 256
    for f in range(0, w2.shape[0], step):
        for r in range(0, rows, tile):
            span = slice(r, r + tile)
            d_act = dot_nt(g_ref[span, :], w2[f : f + step, :])
            slope = slope_ref[span, f : f + step].astype(F32)
            din_ref[span, f : f + step] = (d_act * slope).astype(BF16)
    for c in range(0, w2.shape[1], step):
        result_ref[:, c : c + step] = mid_ref[:, c : c + step] + dot(
            act_ref[...], w2[:, c : c + step]
        )


def out_call(meta, act, middle, g, slope, chunk):
    rows, ff = act.shape
    d = middle.shape[1]
    return call(
        functools.partial(out_kernel, chunk, rows // 4),
        "out",
        (meta, act, middle, g, slope),
        chunk.arrays,
        [array((rows, d), F32), array((rows, ff), BF16)],
        [pltpu.VMEM((ff, d), BF16)],
        4 * rows * d * ff,
        aliases={4: 1},
    )


def store_pieces(out, spots, base, total, rows, cols, first=0):
    for f in range(total.shape[0] // rows):
        out[spots[base + first + f], :, cols] = total[f * rows : (f + 1) * rows]


def mid_grad_kernel(n, meta, n2_ref, low_ref, high_ref, din_ref, datt_ref, keep_ref, send_ref):
    per = keep_ref.shape[1]
    h = datt_ref.shape[1] // 2
    ffh = din_ref.shape[1] // 2
    step = 512
    for out, side, table in ((send_ref, 1 - meta[0], 3), (keep_ref, meta[0], 2)):
        base = 1 + table * n
        col = pl.multiple_of(side * h, 128)
        datt = datt_ref[:, pl.ds(col, h)]
        for part, c_ref in enumerate((low_ref, high_ref)):
            total = dot_tn(c_ref[...], datt).astype(BF16)
            store_pieces(out, meta, base, total, per, slice(0, h), part * (n // 2))
        for c in range(0, ffh, step):
            col = pl.multiple_of(side * ffh + c, 128)
            total = dot_tn(n2_ref[...], din_ref[:, pl.ds(col, step)]).astype(BF16)
            store_pieces(out, meta, base, total, per, slice(h + c, h + c + step))


def mid_grad_call(meta, n2, ctxs, d_inner, d_att, n):
    rows, d = n2.shape
    ff = d_inner.shape[1]
    shape = array((n, d // n, (d + ff) // 2), BF16)
    return call(
        functools.partial(mid_grad_kernel, n),
        "mid_grad",
        (meta, n2, *ctxs, d_inner, d_att),
        (),
        [shape, shape],
        [],
        2 * rows * d * (d + ff),
    )


def qkv_grad_kernel(n, table, meta, n_ref, d_ref, out_ref):
    width = d_ref.shape[1]
    for c in range(0, width, 256):
        cols = slice(c, min(c + 256, width))
        total = dot_tn(n_ref[...], d_ref[:, cols]).astype(BF16)
        store_pieces(out_ref, meta, 1 + table * n, total, out_ref.shape[1], cols)


def qkv_grad_call(meta, normed, dqkv, n, table):
    rows, d = normed.shape
    h = dqkv.shape[1] // 3
    return call(
        functools.partial(qkv_grad_kernel, n, table),
        "qkv_grad",
        (meta, normed, dqkv),
        (),
        [array((n, d // n, 3 * h), BF16)],
        [],
        6 * rows * d * h,
    )[0]


def norm_back(dn, x, gain_ref, first, scale):
    d = x.shape[1]
    z = jnp.concatenate(
        [
            dn[:, c * 128 : (c + 1) * 128] * gain_ref[first + c : first + c + 1, :]
            for c in range(d // 128)
        ],
        axis=1,
    )
    inner = jnp.mean(z * x, axis=-1, keepdims=True)
    back = scale * z - x * (scale * scale * scale * inner)
    return back, jnp.sum(dn * (x * scale), axis=0, keepdims=True)


def mid_back_kernel(chunk, tile, meta, din_ref, mid_ref, g_ref, ext_ref, *rest):
    refs = rest[: chunk.count]
    dmid_ref, datt_ref, dctx_ref, gain_ref, wo, w1 = rest[chunk.count :]
    d = wo.shape[0]
    load_columns(chunk, meta, refs, d // 2, w1.shape[1] // 2, w1)
    load_columns(chunk, meta, refs, 0, d // 2, wo)
    rows = g_ref.shape[0]
    for c in range(0, d, 256):
        dmid_ref[:, c : c + 256] = dot_nt(din_ref[...], w1[c : c + 256, :])
    gains = []
    for r in range(0, rows, tile):
        span = slice(r, r + tile)
        dn = dmid_ref[span, :]
        middle = mid_ref[span, :]
        scale = lax.rsqrt(jnp.mean(middle * middle, axis=-1, keepdims=True) + norm_eps)
        back, gain = norm_back(dn, middle, ext_ref, 6, scale)
        gains.append(gain)
        dmid = g_ref[span, :].astype(F32) + back
        dmid_ref[span, :] = dmid
        datt_ref[span, :] = dmid.astype(BF16)
    for c in range(0, d, 256):
        dctx_ref[:, c : c + 256] = dot_nt(datt_ref[...], wo[c : c + 256, :]).astype(BF16)
    gain_ref[...] = sum(gains)


def mid_back_call(meta, din, middle, g, ext, chunk):
    rows, ff = din.shape
    d = middle.shape[1]
    return call(
        functools.partial(mid_back_kernel, chunk, rows // 4),
        "mid_back",
        (meta, din, middle, g, ext),
        chunk.arrays,
        [
            array((rows, d), F32),
            array((rows, d), BF16),
            array((rows, d), BF16),
            array((1, d), F32),
        ],
        [
            pltpu.VMEM((d, d), BF16),
            pltpu.VMEM((d, ff), BF16),
        ],
        2 * rows * d * (d + ff),
    )


def diagonal_sums(strip):
    for s in (64, 32, 16, 8):
        strip = strip[:s] + pltpu.roll(strip[s:], SPAN - s, 1)
    for s in (4, 2, 1):
        strip = strip + pltpu.roll(pltpu.roll(strip, 8 - s, 0), SPAN - s, 1)
    return strip[:1]


def attend_back_kernel(
    keep,
    todo,
    meta,
    qkv_ref,
    dctx_ref,
    qaug_ref,
    kaug_ref,
    dist_ref,
    lse_ref,
    *rest,
):
    grad_ref, table_ref, strip_acc = rest[-3:]
    side = meta[0] if keep else 1 - meta[0]
    count = H // 4
    rows = qkv_ref.shape[0]
    lane = lax.broadcasted_iota(jnp.int32, (PAIR, 128), 1)
    for pair in todo:
        strip_acc[...] = jnp.zeros_like(strip_acc)
        strips = [
            bias_strip(dist_ref[pl.ds(side * 6 + 2 * pair + hh, 1), :]) for hh in range(2)
        ]
        for base in range(0, rows, PAIR):
            block = slice(base, base + PAIR)

            def part(t):
                col = pl.multiple_of(side * 1152 + (t * 3 + pair) * 128, 128)
                return qkv_ref[block, pl.ds(col, 128)]

            q, k, v = part(0), part(1), part(2)
            do = dctx_ref[block, pl.ds(pl.multiple_of(side * 384 + pair * 128, 128), 128)]
            lse = [lse_ref[pl.ds(side * 6 + 2 * pair + hh, 1), block] for hh in range(2)]
            qaug, kaug = qaug_ref[block, :], kaug_ref[block, :]
            k_turned = k.T
            heads = []
            for hh in range(2):
                mine = (lane // 64) == hh
                heads.append(
                    (
                        jnp.where(mine, q, qaug),
                        jnp.where(mine, k, kaug),
                        jnp.where(mine, v, jnp.zeros_like(v)),
                        k_turned[hh * 64 : (hh + 1) * 64, :],
                        strips[hh],
                    )
                )
            cols = [slice((t * count + pair) * 128, (t * count + pair + 1) * 128) for t in range(3)]
            for off, size in GROUPS:
                step = size
                low = lax.broadcasted_iota(jnp.int32, (size, 128), 1) < 64
                dks, dvs = [None, None], [None, None]
                for i0 in range(0, size, step):
                    lo, hi = off + i0, off + i0 + step
                    dqs = []
                    for hh in range(2):
                        qa, ka, va, kt, strip = heads[hh]
                        scores = dot_nt(ka[off : off + size], qa[lo:hi])
                        scores = scores + strip_bias(strip, size, i0, step)
                        probs = jnp.exp(scores - lse[hh][:, lo:hi])
                        d_probs = dot_nt(va[off : off + size], do[lo:hi])
                        dv = dot(probs.astype(BF16), do[lo:hi])
                        center = jnp.sum(probs * d_probs, axis=0, keepdims=True)
                        d_scores = probs * (d_probs - center)
                        for t in range(size // 128):
                            at = (3 - t) * 128 + i0
                            strip_acc[hh, :, at : at + step] += d_scores[t * 128 : (t + 1) * 128]
                        ds_low = d_scores.astype(BF16)
                        dk = dot(ds_low, q[lo:hi])
                        dqs.append(dot(kt[:, off : off + size], ds_low))
                        dks[hh] = dk if dks[hh] is None else dks[hh] + dk
                        dvs[hh] = dv if dvs[hh] is None else dvs[hh] + dv
                    dq = jnp.concatenate(dqs, axis=0).T.astype(BF16)
                    grad_ref[base + lo : base + hi, cols[0]] = dq
                out = slice(base + off, base + off + size)
                grad_ref[out, cols[1]] = jnp.where(low, dks[0], dks[1]).astype(BF16)
                grad_ref[out, cols[2]] = jnp.where(low, dvs[0], dvs[1]).astype(BF16)
        for hh in range(2):
            table_ref[2 * pair + hh : 2 * pair + hh + 1, :] = diagonal_sums(strip_acc[hh])
    if todo[0] == 0:
        table_ref[2 * count :, :] = jnp.zeros((8 - 2 * count, SPAN), F32)


def attend_back_call(meta, qkv, dctx, qaug, kaug, dist, lse, keep, todo, done=()):
    rows, d = dctx.shape
    pairs = rows // PAIR
    count = H // 4
    return call(
        functools.partial(attend_back_kernel, keep, todo),
        "attend_back",
        (meta, qkv, dctx, qaug, kaug, dist, lse),
        done,
        [array((rows, 3 * count * 128), BF16), array((8, SPAN), F32)],
        [pltpu.VMEM((2, 128, SPAN), F32)],
        20 * pairs * len(todo) * 350000 * 128,
        trans=2 * pairs * len(todo) * 350000,
        aliases={7: 0, 8: 1} if done else None,
    )


def in_back_kernel(chunk, tile, meta, own_ref, rec_ref, x_ref, dmid_ref, ext_ref, *rest):
    stay_ref, away_ref, gain_ref, *rest = rest
    refs = rest[: chunk.count]
    dx_ref, extra_ref, w = rest[chunk.count :]
    load_columns(chunk, meta, refs, 0, w.shape[1] // 2, w, own_first=True)
    place = (lax.broadcasted_iota(jnp.int32, (128, SPAN), 1) + 127) % SPAN
    row = lax.broadcasted_iota(jnp.int32, (128, SPAN), 0)
    chosen = (bucket_of(BLOCK - 1 - place) == row).astype(F32)
    found = [
        lax.dot_general(
            r[...],
            chosen,
            (((1,), (1,)), ((), ())),
            precision=lax.Precision.HIGHEST,
            preferred_element_type=F32,
        )[: H // 2]
        for r in (stay_ref, away_ref)
    ]
    first = meta[0] == 0
    extra_ref[...] = jnp.zeros_like(extra_ref)
    extra_ref[16 : 16 + H // 2, :] = jnp.where(first, found[0], found[1])
    extra_ref[16 + H // 2 : 16 + H, :] = jnp.where(first, found[1], found[0])
    rows, d = x_ref.shape
    both = jnp.concatenate([own_ref[...], rec_ref[...]], axis=1)
    for c in range(0, d, 256):
        dx_ref[:, c : c + 256] = dot_nt(both, w[c : c + 256, :])
    gains = []
    for r in range(0, rows, tile):
        span = slice(r, r + tile)
        dn = dx_ref[span, :]
        x = x_ref[span, :].astype(F32)
        scale = lax.rsqrt(jnp.mean(x * x, axis=-1, keepdims=True) + norm_eps)
        back, gain = norm_back(dn, x, ext_ref, 0, scale)
        gains.append(gain)
        dx_ref[span, :] = dmid_ref[span, :] + back
    total = sum(gains)
    for c in range(d // 128):
        extra_ref[c : c + 1, :] = total[:, c * 128 : (c + 1) * 128]
        extra_ref[6 + c : 7 + c, :] = gain_ref[:, c * 128 : (c + 1) * 128]


def in_back_call(meta, own, rec, x, dmid, ext, found, gain, chunk):
    rows, d = x.shape
    return call(
        functools.partial(in_back_kernel, chunk, rows // 4),
        "in_back",
        (meta, own, rec, x, dmid, ext, *found, gain),
        chunk.arrays,
        [array((rows, d), F32), array((32, 128), F32)],
        [pltpu.VMEM((d, 3 * d), BF16)],
        6 * rows * d * d,
    )


def mask_lanes(lengths, rows):
    spot = jnp.arange(rows, dtype=jnp.int32)
    within = spot % PAIR
    first = jnp.array([0, 512, 768, 896, 960], jnp.int32)
    slot = jnp.sum((within[:, None] >= first[None, 1:]).astype(jnp.int32), axis=1)
    start = jnp.sum(jnp.where(slot[:, None] == jnp.arange(5)[None], first[None], 0), axis=1)
    docs = jnp.arange(lengths.shape[0], dtype=jnp.int32)
    document = spot // PAIR * 5 + slot
    own = jnp.sum(jnp.where(document[:, None] == docs[None], lengths[None], 0), axis=1)
    live = within - start < own
    late = slot == 4
    lane = jnp.arange(128, dtype=jnp.int32) % 64
    shown = [live & ~late, live & late]
    kaug = jnp.where(
        lane[None] == 0,
        jnp.where(shown[0], 0.0, MASKED)[:, None],
        jnp.where(lane[None] == 1, jnp.where(shown[1], 0.0, MASKED)[:, None], 0.0),
    ).astype(BF16)
    qaug = jnp.where(
        lane[None] == 0,
        jnp.where(late, 0.0, 1.0)[:, None],
        jnp.where(lane[None] == 1, jnp.where(late, 1.0, 0.0)[:, None], 0.0),
    ).astype(BF16)
    return qaug, kaug, live


def placed_rows(vector, me, rows):
    count = vector.shape[0]
    spot = jnp.arange(rows * 128, dtype=jnp.int32)[None] - me * count
    hit = spot == jnp.arange(count, dtype=jnp.int32)[:, None]
    flat = jnp.sum(jnp.where(hit, vector.astype(F32)[:, None], 0.0), axis=0)
    return flat.reshape(rows, 128)


def placed_table(vector, me):
    count = vector.shape[0]
    head = jnp.arange(16, dtype=jnp.int32)[:, None]
    bucket = jnp.arange(128, dtype=jnp.int32)[None]
    entry = jnp.where((head < H) & (bucket < BUCKETS), bucket * H + head, -1) - me * count
    hit = entry[None] == jnp.arange(count, dtype=jnp.int32)[:, None, None]
    return jnp.sum(jnp.where(hit, vector.astype(F32)[:, None, None], 0.0), axis=0)


def local(
    ring,
    ring_c,
    hidden,
    gain_attn,
    rel_table,
    query_weight,
    key_weight,
    value_weight,
    output_weight,
    gain_ffn,
    inner_weight,
    outer_weight,
    lengths,
    cotangent,
):
    rows, d = hidden.shape
    ff = inner_weight.shape[1]
    n = ring.n
    shard_rows = query_weight.shape[0]
    outer_rows = outer_weight.shape[0]
    direct = shard_rows % 16 == 0 and shard_rows >= 32 and outer_rows % 32 == 0
    me = lax.axis_index("fsdp")
    core = lax.axis_index("dp")
    meta = ring.meta()
    meta_c = ring_c.meta()
    h = d // 2

    def half(w, which):
        width = w.shape[1] // 2
        return lax.dynamic_slice_in_dim(w, which * width, width, 1)

    small = jnp.concatenate(
        [
            placed_rows(gain_attn, me, d // 128),
            placed_rows(gain_ffn, me, d // 128),
            jnp.zeros((16 - 2 * (d // 128), 128), F32),
            placed_table(rel_table, me),
        ],
        axis=0,
    ).astype(BF16)
    pack_a = [half(w, core) for w in (query_weight, key_weight, value_weight)]
    if direct:
        pack_a.append(jnp.pad(small, ((0, shard_rows - 32), (0, 0))))
    pack_a = jnp.concatenate(pack_a, axis=1)
    pack_b = jnp.concatenate([half(output_weight, core), half(inner_weight, core)], axis=1)
    pack_c = lax.dynamic_slice_in_dim(
        outer_weight, core * (outer_rows // 2), outer_rows // 2, 0
    )

    def whole_columns(own, rec):
        both = []
        for parts, first in ((own, core == 0), (rec, core == 1)):
            pieces = ring.to_origin(jnp.concatenate(parts, axis=0), first)
            both.append(pieces.reshape(-1, pieces.shape[2]))
        first = jnp.where(core == 0, both[0], both[1])
        second = jnp.where(core == 0, both[1], both[0])
        return jnp.stack([first, second])

    qaug, kaug, live = mask_lanes(lengths, rows)
    g = jnp.where(live[:, None], cotangent, jnp.zeros_like(cotangent))
    if direct:
        move_a, move_b = Gather(ring, pack_a), Gather(ring, pack_b)
        move_c = Gather(ring_c, pack_c)
        move_a.go()
        move_c.go()
        move_a.got, move_c.got = lax.optimization_barrier((move_a.got, move_c.got))
        move_c.join()
        for _ in range(ring.bits - 3):
            move_a.join(meta, meta_c, qaug, kaug, g)
            move_a.go()
        move_a.join()
        for _ in range(ring.bits - 3):
            ready(move_a, move_b)
            move_a.go()
            move_b.go()
            move_a.join()
            move_b.join()
        ready(move_a, move_b)
        move_a.go()
        move_b.go()
        move_a.last, move_b.got = lax.optimization_barrier((move_a.last, move_b.got))
        move_b.join()
        final = move_a.last
        move_b.held, final = lax.optimization_barrier((move_b.held, final))
        move_b.go()
        chunk_a = Pieces(*move_a.finish(), n)
        move_c.held, final = lax.optimization_barrier((move_c.held, final))
        move_c.go()
        ext = None
    else:
        got_c = gather_pieces(ring, pack_c)
        chunk_a = Whole(whole_columns(*gather_pieces(ring, pack_a)))
        chunk_b = Whole(whole_columns(*gather_pieces(ring, pack_b)))
        both = [
            ring.to_origin(jnp.concatenate(parts, axis=0), first)
            for parts, first in zip(got_c, (core == 0, core == 1))
        ]
        first = jnp.where(core == 0, both[0], both[1])
        second = jnp.where(core == 0, both[1], both[0])
        chunk_c = Whole(jnp.stack([first, second], axis=1).reshape(ff, d))
        ext = lax.psum(small.astype(F32), "fsdp")

    qkv, normed, dist, ext = qkv_call(meta, hidden, ext, chunk_a)
    if direct:
        (qkv,) = gather_on((qkv,), move_b, move_c)
    ctx0, lse0 = attend_call(meta, qkv, qaug, kaug, dist, 0, H // 4)
    if direct:
        dist, ctx0 = lax.optimization_barrier((dist, ctx0))
    ctx1, lse1 = attend_call(meta, qkv, qaug, kaug, dist, H // 4, H // 4)
    if direct:
        (ctx1,) = gather_on((ctx1,), move_b, move_c)
        chunk_b = Pieces(*move_b.finish(), n)
    ctxs = (ctx0, ctx1)
    middle, normed2, act, slope = mid_call(meta, ctxs, hidden, ext, chunk_b, ff)
    if direct:
        chunk_c = Pieces(*move_c.finish(act), n)

    def split_columns(pairs, which):
        full = [jnp.einsum("td,tf->df", a, b, preferred_element_type=F32) for a, b in pairs]
        part = jnp.concatenate(full, axis=1).astype(BF16)
        part = part.reshape(n, d // n, part.shape[1])
        return ring.from_origin(part, which == 0)

    if direct:
        grad_c = outer_grad_call(meta, act, g, n)
    else:
        full = jnp.einsum("tf,td->fd", act, g, preferred_element_type=F32).astype(BF16)
        full = full.reshape(n, 2, outer_rows // 2, d)
        grad_c = [
            ring.from_origin(
                lax.dynamic_index_in_dim(full, which, 1, keepdims=False), which == 0
            )
            for which in (core, 1 - core)
        ]
    red_c = Reduce(ring, *grad_c)
    (act,) = tick((act,), fresh=(red_c,))
    result, d_inner = out_call(meta_c, act, middle, g, slope, chunk_c)
    (d_inner,) = tick((d_inner,), (red_c,))
    d_middle, d_att, d_ctx, grad_gain_f = mid_back_call(meta, d_inner, middle, g, ext, chunk_b)
    (d_att,) = tick((d_att,), (red_c,))
    if direct:
        grad_b = mid_grad_call(meta, normed2, ctxs, d_inner, d_att, n)
    else:
        both = jnp.concatenate(ctxs, axis=1)
        grad_b = [
            split_columns([(both, half(d_att, w)), (normed2, half(d_inner, w))], w)
            for w in (core, 1 - core)
        ]
    red_b = Reduce(ring, *grad_b)
    (d_ctx,) = tick((after(d_ctx, *grad_b),), (red_c,), (red_b,))
    lse = jnp.concatenate([lse0, lse1], axis=0)
    back = functools.partial(attend_back_call, meta, qkv)
    masks = (qaug, kaug, dist, lse)
    away, found_away = tick(back(d_ctx, *masks, False, (0, 1, 2)), (red_c, red_b))
    if direct:
        send_a = qkv_grad_call(meta, normed, away, n, 3)
    else:
        send_a = split_columns([(normed, away)], 1 - core)
    d_ctx, send_a = lax.optimization_barrier((d_ctx, send_a))
    red_a = Reduce(ring, None, send_a)
    red_a.go()
    stay, found_stay = tick(back(d_ctx, *masks, True, (0, 1, 2)), (red_b,))
    if direct:
        keep_a = qkv_grad_call(meta, normed, stay, n, 2)
    else:
        keep_a = split_columns([(normed, stay)], core)
    red_a.keep = keep_a
    (stay,) = tick((after(stay, keep_a),), (red_a,))
    grad_hidden, extra = in_back_call(
        meta,
        stay,
        away,
        hidden,
        d_middle,
        ext,
        (found_stay, found_away),
        grad_gain_f,
        chunk_a,
    )
    extra, red_b.got = lax.optimization_barrier((extra, red_b.got))
    steps = [ring.swap_phase(k) for k in range(ring.bits)] + [ring.swap_core()]
    extra = extra + shift(extra, steps.pop(0))
    extra, red_a.got = lax.optimization_barrier((extra, red_a.got))
    while red_a.phase > 0:
        red_a.step()
        flat = (extra, red_a.keep, red_a.away)
        extra, red_a.keep, red_a.away = lax.optimization_barrier(flat)
        red_a.go()
        for _ in range(2 if len(steps) > red_a.phase + 1 else 1):
            moved = shift(extra, steps.pop(0))
            extra = extra + moved
        extra, red_a.got = lax.optimization_barrier((extra, red_a.got))
    assert not steps
    sum_c = red_c.finish()
    sum_b = red_b.finish()
    sum_o, sum_b = sum_b[:, :h], sum_b[:, h:]
    sum_a = red_a.finish()

    own = [sum_a, sum_o, sum_b, sum_c]
    other = [shift(s, ring.swap_core()) for s in own]
    low = [jnp.where(core == 0, a, b) for a, b in zip(own, other)]
    high = [jnp.where(core == 0, b, a) for a, b in zip(own, other)]
    grads = [
        jnp.concatenate([low[0][:, t * h : (t + 1) * h], high[0][:, t * h : (t + 1) * h]], axis=1)
        for t in range(3)
    ]
    grad_output = jnp.concatenate([low[1], high[1]], axis=1)
    grad_inner = jnp.concatenate([low[2], high[2]], axis=1)
    grad_outer = jnp.concatenate([low[3], high[3]], axis=0)
    per = d // n
    gain_a = lax.dynamic_slice_in_dim(extra[: d // 128].reshape(-1), me * per, per, 0)
    gain_f = lax.dynamic_slice_in_dim(
        extra[d // 128 : 2 * (d // 128)].reshape(-1), me * per, per, 0
    )
    table = extra[16 : 16 + H, :BUCKETS].T.reshape(-1)
    table = lax.dynamic_slice_in_dim(table, me * rel_table.shape[0], rel_table.shape[0], 0)
    return (
        result,
        grad_hidden,
        gain_a,
        table,
        grads[0],
        grads[1],
        grads[2],
        grad_output,
        gain_f,
        grad_inner,
        grad_outer,
    )


def solution(mesh):
    both = P(("dp", "fsdp"), None)
    line = P("fsdp")
    wide = P("fsdp", None)
    in_specs = (both, line, line, wide, wide, wide, wide, line, wide, wide, P(("dp", "fsdp")), both)
    out_specs = (both, both, line, line, wide, wide, wide, wide, line, wide, wide)
    return jax.shard_map(
        functools.partial(local, Ring(mesh), Ring(mesh, split=True)),
        mesh=mesh,
        in_specs=in_specs,
        out_specs=out_specs,
        check_vma=False,
    )
```

```python
import functools

import jax
import jax.numpy as jnp
import numpy as np
from jax import lax
from jax.experimental import pallas as pl
from jax.experimental.pallas import tpu as pltpu
from jax.sharding import PartitionSpec as P

H = 12
DK = 64
BUCKETS = 32
BLOCK = 512
norm_eps = 1e-06
bucket_edges = (12, 16, 23, 32, 46, 64, 91)
MASKED = -1e30
F32 = jnp.float32
BF16 = jnp.bfloat16
PAIR = 2 * BLOCK
GROUPS = ((0, 512), (512, 256), (768, 128), (896, 128))
SPAN = 1024
SCOPED = {
    "qkv": 10,
    "attend": 8,
    "mid": 8,
    "outer_grad": 4,
    "out": 10,
    "mid_back": 12,
    "mid_grad": 3,
    "attend_back": 8,
    "qkv_grad": 3,
    "in_back": 18,
}


def bucket_of(relative):
    distance = jnp.abs(relative)
    passed = sum(((distance >= edge_value).astype(jnp.int32) for edge_value in bucket_edges))
    return jnp.where(relative > 0, BUCKETS // 2, 0) + jnp.where(
        distance < BUCKETS // 4, distance, BUCKETS // 4 + passed
    )


class Ring:
    def __init__(self, mesh, split=False):
        self.n = mesh.shape["fsdp"]
        self.bits = self.n.bit_length() - 1
        high = list(range(self.bits - 1, 1, -1))
        if split:
            self.order = ([0] + high + [1], [1] + high + [0])
        else:
            self.order = (high + [1, 0], high + [0, 1])

    def swap_phase(self, k):
        n = self.n
        return [
            (c * n + f, c * n + (f ^ (1 << self.order[c][k])))
            for c in range(2)
            for f in range(n)
        ]

    def swap_core(self):
        n = self.n
        return [(c * n + f, (1 - c) * n + f) for c in range(2) for f in range(n)]

    def meta(self):
        me = lax.axis_index("fsdp").astype(jnp.int32)
        core = lax.axis_index("dp").astype(jnp.int32)
        spots = jnp.arange(self.n, dtype=jnp.int32)

        def off(which):
            out = jnp.zeros_like(spots)
            for k, b in enumerate(self.order[which]):
                out = out | (((spots >> k) & 1) << b)
            return out

        def inv(which, m):
            out = jnp.zeros_like(spots)
            for k, b in enumerate(self.order[which]):
                out = out | (((m >> b) & 1) << k)
            return out

        first = core == 0
        mixed = me ^ spots
        return jnp.concatenate(
            [
                core[None],
                me ^ jnp.where(first, off(0), off(1)),
                me ^ jnp.where(first, off(1), off(0)),
                jnp.where(first, inv(0, mixed), inv(1, mixed)),
                jnp.where(first, inv(1, mixed), inv(0, mixed)),
            ]
        )


    def flip_origin(self, pieces):
        me = lax.axis_index("fsdp")
        shape = pieces.shape
        pieces = pieces.reshape((2,) * self.bits + shape[1:])
        for b in range(self.bits):
            axis = self.bits - 1 - b
            pieces = jnp.where((me >> b) & 1 == 1, jnp.flip(pieces, axis), pieces)
        return pieces.reshape(shape)

    def reorder(self, pieces, first, back):
        shape = pieces.shape
        split = pieces.reshape((2,) * self.bits + shape[1:])
        tail = list(range(self.bits, self.bits + len(shape) - 1))
        found = []
        for order in self.order:
            axes = [self.bits - 1 - order.index(self.bits - 1 - a) for a in range(self.bits)]
            if back:
                axes = list(np.argsort(axes))
            found.append(jnp.transpose(split, [int(a) for a in axes] + tail).reshape(shape))
        return jnp.where(first, found[0], found[1])

    def to_origin(self, pieces, first):
        return self.flip_origin(self.reorder(pieces, first, False))

    def from_origin(self, pieces, first):
        return self.reorder(self.flip_origin(pieces), first, True)


def shift(value, pairs):
    return lax.ppermute(value, ("dp", "fsdp"), pairs)


def after(value, *others):
    return lax.optimization_barrier((value, *others))[0]


class Gather:
    def __init__(self, ring, shard):
        self.ring = ring
        self.held = shard[None]
        self.phase = 0
        self.last = None
        self.got = None

    def join(self, *others):
        if self.got is not None:
            got = after(self.got, *others) if others else self.got
            self.held = jnp.concatenate([self.held, got], axis=0)
            self.got = None

    def go(self):
        got = shift(self.held, self.ring.swap_phase(self.phase))
        self.phase += 1
        if self.phase == self.ring.bits:
            self.last = got
        else:
            self.got = got
        return got

    def step(self, *others):
        self.join()
        if others:
            self.held = after(self.held, *others)
        got = self.go()
        return got

    def near(self):
        self.join()
        return self.held

    def finish(self, *others):
        own = (self.held, after(self.last, *others) if others else self.last)
        return own, tuple(shift(p, self.ring.swap_core()) for p in own)


def ready(*moves):
    for move, held in zip(moves, lax.optimization_barrier(tuple(m.held for m in moves))):
        move.held = held


def gather_on(values, *moves):
    values = tuple(values)
    flat = list(values)
    for move in moves:
        move.join(*values)
        flat.append(move.held)
        if move.last is not None:
            flat.append(move.last)
    flat = list(lax.optimization_barrier(tuple(flat)))
    values = [flat.pop(0) for _ in values]
    for move in moves:
        move.held = flat.pop(0)
        if move.last is not None:
            move.last = flat.pop(0)
        else:
            move.go()
    return values


def gather_pieces(ring, shard):
    move = Gather(ring, shard)
    for _ in range(ring.bits):
        move.step()
    return move.finish()


class Reduce:
    def __init__(self, ring, keep, send):
        self.ring = ring
        self.keep = keep
        self.away = send
        self.got = None
        self.phase = ring.bits + 1

    def step(self, *others):
        got = after(self.got, *others) if others else self.got
        self.got = None
        if self.phase == 0:
            return self.keep[0].astype(F32) + got[0].astype(F32)
        half = self.keep.shape[0] // 2

        def add(part):
            return self.keep[part].astype(F32) + got[part].astype(F32)

        self.away = add(slice(half, None)).astype(BF16)
        self.keep = add(slice(0, half))
        if self.phase > 1:
            self.keep = self.keep.astype(BF16)

    def go(self):
        self.phase -= 1
        if self.phase == self.ring.bits:
            pairs = self.ring.swap_core()
        else:
            pairs = self.ring.swap_phase(self.phase)
        self.got = shift(self.away, pairs)

    def finish(self):
        while self.phase > 0:
            if self.got is not None:
                self.step()
            self.go()
        return self.step()


def tick(values, steps=(), fresh=()):
    values = tuple(values)
    for red in steps:
        red.step(*values)
    reds = [*steps, *fresh]
    flat = list(values)
    for red in reds:
        flat += [red.keep, red.away]
    flat = lax.optimization_barrier(tuple(flat))
    for i, red in enumerate(reds):
        red.keep, red.away = flat[len(values) + 2 * i : len(values) + 2 * i + 2]
        red.go()
    return flat[: len(values)]


def params(vmem):
    return pltpu.CompilerParams(vmem_limit_bytes=vmem)


def cost(flops, bytes_accessed, trans=0):
    return pl.CostEstimate(flops=flops, bytes_accessed=bytes_accessed, transcendentals=trans)


def dot(a, b):
    return jnp.dot(a, b, preferred_element_type=F32)


def dot_nt(a, b):
    return lax.dot_general(a, b, (((1,), (1,)), ((), ())), preferred_element_type=F32)


def dot_tn(a, b):
    return lax.dot_general(a, b, (((0,), (0,)), ((), ())), preferred_element_type=F32)


class Pieces:
    def __init__(self, own, rec, n, placed=False):
        self.arrays = [*own, *rec]
        self.n = n
        self.count = len(self.arrays)
        self.part = n // len(own)
        self.whole = False
        self.placed = placed

    def spot(self, meta, h, j):
        place = j if self.placed else meta[1 + h * self.n + j]
        return place, h * (self.count // 2) + j // self.part, j % self.part


class Whole:
    def __init__(self, array):
        self.arrays = [array]
        self.count = 1
        self.whole = True
        self.n = 0


def load_columns(chunk, meta, refs, lo, width, dst, own_first=False):
    core = meta[0]
    if chunk.whole:
        for h in range(2):
            side = (core if h == 0 else 1 - core) if own_first else h
            dst[:, h * width : (h + 1) * width] = refs[0][side, :, lo : lo + width]
        return
    rows = refs[0].shape[1]
    for h in range(2):
        side = h if own_first else (core if h == 0 else 1 - core)
        col = pl.multiple_of(side * width, 128)
        for j in range(chunk.n):
            place, which, index = chunk.spot(meta, h, j)
            row = pl.multiple_of(place * rows, 16)
            dst[pl.ds(row, rows), pl.ds(col, width)] = refs[which][index, :, lo : lo + width]


def load_rows(chunk, meta, refs, dst):
    if chunk.whole:
        dst[...] = refs[0][...]
        return
    rows = refs[0].shape[1]
    core = meta[0]
    for h in range(2):
        for j in range(chunk.n):
            place, which, index = chunk.spot(meta, h, j)
            row = pl.multiple_of(place * (2 * rows) + (core if h == 0 else 1 - core) * rows, 16)
            dst[pl.ds(row, rows), :] = refs[which][index]


def norm_tile(x, ext_ref, first):
    d = x.shape[1]
    scale = lax.rsqrt(jnp.mean(x * x, axis=-1, keepdims=True) + norm_eps)
    out = []
    for c in range(d // 128):
        out.append(
            (x[:, c * 128 : (c + 1) * 128] * scale * ext_ref[first + c : first + c + 1, :]).astype(
                BF16
            )
        )
    return jnp.concatenate(out, axis=1), scale


def call(body, name, inputs, parts, outs, scratch, flops, trans=0, aliases=None):
    meta, *arrays = inputs
    moved = sum(a.size * a.dtype.itemsize for a in [*arrays, *parts])
    moved += sum(int(np.prod(o.shape)) * jnp.dtype(o.dtype).itemsize for o in outs)
    vmem_spec = pl.BlockSpec(memory_space=pltpu.VMEM)
    return pl.pallas_call(
        body,
        in_specs=[pl.BlockSpec(memory_space=pltpu.SMEM)]
        + [vmem_spec] * (len(arrays) + len(parts)),
        out_specs=[vmem_spec] * len(outs),
        out_shape=outs,
        scratch_shapes=scratch,
        input_output_aliases=aliases or {},
        compiler_params=params(SCOPED[name] * 1024 * 1024),
        cost_estimate=cost(flops, moved, trans),
        name=name,
    )(meta, *arrays, *parts)


def array(shape, dtype):
    return jax.ShapeDtypeStruct(shape, dtype)


def qkv_kernel(chunk, tile, meta, x_ref, *rest):
    refs = rest[: chunk.count]
    *given, qkv_ref, n_ref, dist_ref, ext_ref, w = rest[chunk.count :]
    if given:
        ext_ref[...] = given[0][...]
    else:
        lo = w.shape[1] // 2
        ext_ref[...] = sum(
            ref[j, 0:32, lo : lo + 128].astype(F32)
            for ref in refs[: chunk.count // 2]
            for j in range(chunk.part)
        )
    load_columns(chunk, meta, refs, 0, w.shape[1] // 2, w)
    place = lax.broadcasted_iota(jnp.int32, (BUCKETS, SPAN), 1)
    row = lax.broadcasted_iota(jnp.int32, (BUCKETS, SPAN), 0)
    chosen = (bucket_of(BLOCK - 1 - place) == row).astype(F32).astype(BF16)
    dist_ref[...] = dot(ext_ref[16:32, 0:BUCKETS].astype(BF16), chosen)
    rows = x_ref.shape[0]
    for r in range(0, rows, tile):
        n_ref[r : r + tile, :] = norm_tile(x_ref[r : r + tile, :].astype(F32), ext_ref, 0)[0]
    for c in range(0, w.shape[1], 256):
        qkv_ref[:, c : c + 256] = dot(n_ref[...], w[:, c : c + 256]).astype(BF16)


def qkv_call(meta, x, ext, chunk):
    rows, d = x.shape
    return call(
        functools.partial(qkv_kernel, chunk, rows // 4),
        "qkv",
        (meta, x),
        chunk.arrays + ([] if ext is None else [ext]),
        [
            array((rows, 3 * d), BF16),
            array((rows, d), BF16),
            array((16, SPAN), F32),
            array((32, 128), F32),
        ],
        [pltpu.VMEM((d, 3 * d), BF16)],
        6 * rows * d * d,
    )


def bias_strip(dist_row):
    spread = jnp.broadcast_to(dist_row, (128, SPAN))
    return pltpu.roll(spread, SPAN - 127, 1, stride=1, stride_axis=0)


def strip_bias(strip, size, i0, step):
    return jnp.concatenate(
        [
            strip[:, (3 - t) * 128 + i0 : (3 - t) * 128 + i0 + step]
            for t in range(size // 128)
        ],
        axis=0,
    )


def attend_kernel(meta, qkv_ref, qaug_ref, kaug_ref, dist_ref, ctx_ref, lse_ref):
    rows = qkv_ref.shape[0]
    for base in range(0, rows, PAIR):
        lane = lax.broadcasted_iota(jnp.int32, (PAIR, 128), 1)
        qaug, kaug = qaug_ref[base : base + PAIR, :], kaug_ref[base : base + PAIR, :]
        for at in range(H // 2):
            col = (at // 3) * 9 * 128 + (at % 3) * 128
            q = qkv_ref[base : base + PAIR, col : col + 128]
            k = qkv_ref[base : base + PAIR, col + 384 : col + 512]
            v_turned = qkv_ref[base : base + PAIR, col + 768 : col + 896].T
            heads = []
            for hh in range(2):
                mine = (lane // 64) == hh
                heads.append(
                    (
                        jnp.where(mine, q, qaug),
                        jnp.where(mine, k, kaug),
                        v_turned[hh * 64 : (hh + 1) * 64, :],
                        bias_strip(dist_ref[2 * at + hh : 2 * at + hh + 1, :]),
                    )
                )
            for off, size in GROUPS:
                step = size
                for i0 in range(0, size, step):
                    lo, hi = off + i0, off + i0 + step
                    parts = []
                    for hh in range(2):
                        qa, ka, vt, strip = heads[hh]
                        scores = dot_nt(ka[off : off + size], qa[lo:hi])
                        scores = scores + strip_bias(strip, size, i0, step)
                        top = jnp.max(scores, axis=0, keepdims=True)
                        expo = jnp.exp(scores - top)
                        total = jnp.sum(expo, axis=0, keepdims=True)
                        mixed = dot(vt[:, off : off + size], expo.astype(BF16))
                        parts.append(mixed * (1.0 / total))
                        lse_ref[2 * at + hh : 2 * at + hh + 1, base + lo : base + hi] = (
                            top + jnp.log(total)
                        )
                    both = jnp.concatenate(parts, axis=0)
                    ctx_ref[base + lo : base + hi, at * 128 : (at + 1) * 128] = both.T.astype(
                        BF16
                    )


def attend_call(meta, qkv, qaug, kaug, dist):
    rows = qkv.shape[0]
    pairs = rows // PAIR
    return call(
        attend_kernel,
        "attend",
        (meta, qkv, qaug, kaug, dist),
        (),
        [array((rows, H * DK), BF16), array((H, rows), F32)],
        [],
        4 * pairs * H * 350000 * 128,
        trans=pairs * H * 350000,
    )


def mid_kernel(chunk, tile, meta, ctx_ref, x_ref, ext_ref, *rest):
    refs = rest[: chunk.count]
    mid_ref, n2_ref, act_ref, slope_ref, wo, w1 = rest[chunk.count :]
    d = wo.shape[0]
    load_columns(chunk, meta, refs, 0, d // 2, wo)
    load_columns(chunk, meta, refs, d // 2, w1.shape[1] // 2, w1)
    rows = x_ref.shape[0]
    for r in range(0, rows, tile):
        span = slice(r, r + tile)
        middle = x_ref[span, :].astype(F32) + dot(ctx_ref[span, :], wo[...])
        mid_ref[span, :] = middle
        n2_ref[span, :] = norm_tile(middle, ext_ref, 6)[0]
    c0 = 0.7978845608028654
    c1 = c0 * 0.044715
    step = 256
    for f in range(0, w1.shape[1], step):
        for r in range(0, rows, tile):
            span = slice(r, r + tile)
            v = dot(n2_ref[span, :], w1[:, f : f + step])
            v2 = v * v
            half = 0.5 + 0.5 * jnp.tanh(v * (c0 + c1 * v2))
            active = v * half
            act_ref[span, f : f + step] = active.astype(BF16)
            slope_ref[span, f : f + step] = (
                half + (active - active * half) * (2.0 * c0 + (6.0 * c1) * v2)
            ).astype(BF16)


def mid_call(meta, ctx, x, ext, chunk, ff):
    rows, d = x.shape
    return call(
        functools.partial(mid_kernel, chunk, rows),
        "mid",
        (meta, ctx, x, ext),
        chunk.arrays,
        [
            array((rows, d), F32),
            array((rows, d), BF16),
            array((rows, ff), BF16),
            array((rows, ff), BF16),
        ],
        [
            pltpu.VMEM((d, d), BF16),
            pltpu.VMEM((d, ff), BF16),
        ],
        2 * rows * d * (d + ff),
        trans=rows * ff,
    )


def outer_grad_kernel(n, meta, act_ref, g_ref, keep_ref, send_ref):
    per = keep_ref.shape[1]
    first = meta[0] == 0
    width = 4 * per * 2
    for b in range(act_ref.shape[1] // width):
        total = dot_tn(act_ref[:, b * width : (b + 1) * width], g_ref[...]).astype(BF16)
        for f in range(4):
            low = total[2 * f * per : (2 * f + 1) * per]
            high = total[(2 * f + 1) * per : (2 * f + 2) * per]
            spot = b * 4 + f
            keep_ref[meta[1 + 2 * n + spot]] = jnp.where(first, low, high)
            send_ref[meta[1 + 3 * n + spot]] = jnp.where(first, high, low)


def outer_grad_call(meta, act, g, n):
    rows, ff = act.shape
    d = g.shape[1]
    shape = array((n, ff // n // 2, d), BF16)
    return call(
        functools.partial(outer_grad_kernel, n),
        "outer_grad",
        (meta, act, g),
        (),
        [shape, shape],
        [],
        2 * rows * d * ff,
    )


def out_kernel(chunk, tile, meta, act_ref, mid_ref, g_ref, slope_ref, *rest):
    refs = rest[: chunk.count]
    result_ref, din_ref, w2 = rest[chunk.count :]
    load_rows(chunk, meta, refs, w2)
    rows = g_ref.shape[0]
    step = 256
    for f in range(0, w2.shape[0], step):
        for r in range(0, rows, tile):
            span = slice(r, r + tile)
            d_act = dot_nt(g_ref[span, :], w2[f : f + step, :])
            slope = slope_ref[span, f : f + step].astype(F32)
            din_ref[span, f : f + step] = (d_act * slope).astype(BF16)
    for c in range(0, w2.shape[1], step):
        result_ref[:, c : c + step] = mid_ref[:, c : c + step] + dot(
            act_ref[...], w2[:, c : c + step]
        )


def out_call(meta, act, middle, g, slope, chunk):
    rows, ff = act.shape
    d = middle.shape[1]
    return call(
        functools.partial(out_kernel, chunk, rows // 4),
        "out",
        (meta, act, middle, g, slope),
        chunk.arrays,
        [array((rows, d), F32), array((rows, ff), BF16)],
        [pltpu.VMEM((ff, d), BF16)],
        4 * rows * d * ff,
        aliases={4: 1},
    )


def store_pieces(out, spots, base, total, rows, cols):
    for f in range(total.shape[0] // rows):
        out[spots[base + f], :, cols] = total[f * rows : (f + 1) * rows]


def mid_grad_kernel(n, meta, n2_ref, ctx_ref, din_ref, datt_ref, keep_ref, send_ref):
    per = keep_ref.shape[1]
    h = datt_ref.shape[1] // 2
    ffh = din_ref.shape[1] // 2
    step = 512
    for out, side, table in ((send_ref, 1 - meta[0], 3), (keep_ref, meta[0], 2)):
        base = 1 + table * n
        col = pl.multiple_of(side * h, 128)
        datt = datt_ref[:, pl.ds(col, h)]
        total = dot_tn(ctx_ref[...], datt).astype(BF16)
        store_pieces(out, meta, base, total, per, slice(0, h))
        for c in range(0, ffh, step):
            col = pl.multiple_of(side * ffh + c, 128)
            total = dot_tn(n2_ref[...], din_ref[:, pl.ds(col, step)]).astype(BF16)
            store_pieces(out, meta, base, total, per, slice(h + c, h + c + step))


def mid_grad_call(meta, n2, ctx, d_inner, d_att, n):
    rows, d = n2.shape
    ff = d_inner.shape[1]
    shape = array((n, d // n, (d + ff) // 2), BF16)
    return call(
        functools.partial(mid_grad_kernel, n),
        "mid_grad",
        (meta, n2, ctx, d_inner, d_att),
        (),
        [shape, shape],
        [],
        2 * rows * d * (d + ff),
    )


def qkv_grad_kernel(n, table, meta, n_ref, d_ref, out_ref):
    width = d_ref.shape[1]
    for c in range(0, width, 256):
        cols = slice(c, min(c + 256, width))
        total = dot_tn(n_ref[...], d_ref[:, cols]).astype(BF16)
        store_pieces(out_ref, meta, 1 + table * n, total, out_ref.shape[1], cols)


def qkv_grad_call(meta, normed, dqkv, n, table):
    rows, d = normed.shape
    h = dqkv.shape[1] // 3
    return call(
        functools.partial(qkv_grad_kernel, n, table),
        "qkv_grad",
        (meta, normed, dqkv),
        (),
        [array((n, d // n, 3 * h), BF16)],
        [],
        6 * rows * d * h,
    )[0]


def norm_back(dn, x, gain_ref, first, scale):
    d = x.shape[1]
    z = jnp.concatenate(
        [
            dn[:, c * 128 : (c + 1) * 128] * gain_ref[first + c : first + c + 1, :]
            for c in range(d // 128)
        ],
        axis=1,
    )
    inner = jnp.mean(z * x, axis=-1, keepdims=True)
    back = scale * z - x * (scale * scale * scale * inner)
    return back, jnp.sum(dn * (x * scale), axis=0, keepdims=True)


def mid_back_kernel(chunk, tile, meta, din_ref, mid_ref, g_ref, ext_ref, *rest):
    refs = rest[: chunk.count]
    dmid_ref, datt_ref, dctx_ref, gain_ref, wo, w1 = rest[chunk.count :]
    d = wo.shape[0]
    load_columns(chunk, meta, refs, d // 2, w1.shape[1] // 2, w1)
    load_columns(chunk, meta, refs, 0, d // 2, wo)
    rows = g_ref.shape[0]
    for c in range(0, d, 256):
        dmid_ref[:, c : c + 256] = dot_nt(din_ref[...], w1[c : c + 256, :])
    gains = []
    for r in range(0, rows, tile):
        span = slice(r, r + tile)
        dn = dmid_ref[span, :]
        middle = mid_ref[span, :]
        scale = lax.rsqrt(jnp.mean(middle * middle, axis=-1, keepdims=True) + norm_eps)
        back, gain = norm_back(dn, middle, ext_ref, 6, scale)
        gains.append(gain)
        dmid = g_ref[span, :].astype(F32) + back
        dmid_ref[span, :] = dmid
        datt_ref[span, :] = dmid.astype(BF16)
    for c in range(0, d, 256):
        dctx_ref[:, c : c + 256] = dot_nt(datt_ref[...], wo[c : c + 256, :]).astype(BF16)
    gain_ref[...] = sum(gains)


def mid_back_call(meta, din, middle, g, ext, chunk):
    rows, ff = din.shape
    d = middle.shape[1]
    return call(
        functools.partial(mid_back_kernel, chunk, rows // 4),
        "mid_back",
        (meta, din, middle, g, ext),
        chunk.arrays,
        [
            array((rows, d), F32),
            array((rows, d), BF16),
            array((rows, d), BF16),
            array((1, d), F32),
        ],
        [
            pltpu.VMEM((d, d), BF16),
            pltpu.VMEM((d, ff), BF16),
        ],
        2 * rows * d * (d + ff),
    )


def diagonal_sums(strip):
    for s in (64, 32, 16, 8):
        strip = strip[:s] + pltpu.roll(strip[s:], SPAN - s, 1)
    for s in (4, 2, 1):
        strip = strip + pltpu.roll(pltpu.roll(strip, 8 - s, 0), SPAN - s, 1)
    return strip[:1]


def attend_back_kernel(
    keep,
    todo,
    meta,
    qkv_ref,
    dctx_ref,
    qaug_ref,
    kaug_ref,
    dist_ref,
    lse_ref,
    *rest,
):
    grad_ref, table_ref, strip_acc = rest[-3:]
    side = meta[0] if keep else 1 - meta[0]
    count = H // 4
    rows = qkv_ref.shape[0]
    lane = lax.broadcasted_iota(jnp.int32, (PAIR, 128), 1)
    for pair in todo:
        strip_acc[...] = jnp.zeros_like(strip_acc)
        strips = [
            bias_strip(dist_ref[pl.ds(side * 6 + 2 * pair + hh, 1), :]) for hh in range(2)
        ]
        for base in range(0, rows, PAIR):
            block = slice(base, base + PAIR)

            def part(t):
                col = pl.multiple_of(side * 1152 + (t * 3 + pair) * 128, 128)
                return qkv_ref[block, pl.ds(col, 128)]

            q, k, v = part(0), part(1), part(2)
            do = dctx_ref[block, pl.ds(pl.multiple_of(side * 384 + pair * 128, 128), 128)]
            lse = [lse_ref[pl.ds(side * 6 + 2 * pair + hh, 1), block] for hh in range(2)]
            qaug, kaug = qaug_ref[block, :], kaug_ref[block, :]
            k_turned = k.T
            heads = []
            for hh in range(2):
                mine = (lane // 64) == hh
                heads.append(
                    (
                        jnp.where(mine, q, qaug),
                        jnp.where(mine, k, kaug),
                        jnp.where(mine, v, jnp.zeros_like(v)),
                        k_turned[hh * 64 : (hh + 1) * 64, :],
                        strips[hh],
                    )
                )
            cols = [slice((t * count + pair) * 128, (t * count + pair + 1) * 128) for t in range(3)]
            for off, size in GROUPS:
                step = size
                low = lax.broadcasted_iota(jnp.int32, (size, 128), 1) < 64
                dks, dvs = [None, None], [None, None]
                for i0 in range(0, size, step):
                    lo, hi = off + i0, off + i0 + step
                    dqs = []
                    for hh in range(2):
                        qa, ka, va, kt, strip = heads[hh]
                        scores = dot_nt(ka[off : off + size], qa[lo:hi])
                        scores = scores + strip_bias(strip, size, i0, step)
                        probs = jnp.exp(scores - lse[hh][:, lo:hi])
                        d_probs = dot_nt(va[off : off + size], do[lo:hi])
                        dv = dot(probs.astype(BF16), do[lo:hi])
                        center = jnp.sum(probs * d_probs, axis=0, keepdims=True)
                        d_scores = probs * (d_probs - center)
                        for t in range(size // 128):
                            at = (3 - t) * 128 + i0
                            strip_acc[hh, :, at : at + step] += d_scores[t * 128 : (t + 1) * 128]
                        ds_low = d_scores.astype(BF16)
                        dk = dot(ds_low, q[lo:hi])
                        dqs.append(dot(kt[:, off : off + size], ds_low))
                        dks[hh] = dk if dks[hh] is None else dks[hh] + dk
                        dvs[hh] = dv if dvs[hh] is None else dvs[hh] + dv
                    dq = jnp.concatenate(dqs, axis=0).T.astype(BF16)
                    grad_ref[base + lo : base + hi, cols[0]] = dq
                out = slice(base + off, base + off + size)
                grad_ref[out, cols[1]] = jnp.where(low, dks[0], dks[1]).astype(BF16)
                grad_ref[out, cols[2]] = jnp.where(low, dvs[0], dvs[1]).astype(BF16)
        for hh in range(2):
            table_ref[2 * pair + hh : 2 * pair + hh + 1, :] = diagonal_sums(strip_acc[hh])
    if todo[0] == 0:
        table_ref[2 * count :, :] = jnp.zeros((8 - 2 * count, SPAN), F32)


def attend_back_call(meta, qkv, dctx, qaug, kaug, dist, lse, keep, todo, done=()):
    rows, d = dctx.shape
    pairs = rows // PAIR
    count = H // 4
    return call(
        functools.partial(attend_back_kernel, keep, todo),
        "attend_back",
        (meta, qkv, dctx, qaug, kaug, dist, lse),
        done,
        [array((rows, 3 * count * 128), BF16), array((8, SPAN), F32)],
        [pltpu.VMEM((2, 128, SPAN), F32)],
        20 * pairs * len(todo) * 350000 * 128,
        trans=2 * pairs * len(todo) * 350000,
        aliases={7: 0, 8: 1} if done else None,
    )


def in_back_kernel(chunk, tile, meta, own_ref, rec_ref, x_ref, dmid_ref, ext_ref, *rest):
    stay_ref, away_ref, gain_ref, *rest = rest
    refs = rest[: chunk.count]
    dx_ref, extra_ref, w = rest[chunk.count :]
    load_columns(chunk, meta, refs, 0, w.shape[1] // 2, w, own_first=True)
    place = (lax.broadcasted_iota(jnp.int32, (128, SPAN), 1) + 127) % SPAN
    row = lax.broadcasted_iota(jnp.int32, (128, SPAN), 0)
    chosen = (bucket_of(BLOCK - 1 - place) == row).astype(F32)
    found = [
        lax.dot_general(
            r[...],
            chosen,
            (((1,), (1,)), ((), ())),
            precision=lax.Precision.HIGHEST,
            preferred_element_type=F32,
        )[: H // 2]
        for r in (stay_ref, away_ref)
    ]
    first = meta[0] == 0
    extra_ref[...] = jnp.zeros_like(extra_ref)
    extra_ref[16 : 16 + H // 2, :] = jnp.where(first, found[0], found[1])
    extra_ref[16 + H // 2 : 16 + H, :] = jnp.where(first, found[1], found[0])
    rows, d = x_ref.shape
    both = jnp.concatenate([own_ref[...], rec_ref[...]], axis=1)
    for c in range(0, d, 256):
        dx_ref[:, c : c + 256] = dot_nt(both, w[c : c + 256, :])
    gains = []
    for r in range(0, rows, tile):
        span = slice(r, r + tile)
        dn = dx_ref[span, :]
        x = x_ref[span, :].astype(F32)
        scale = lax.rsqrt(jnp.mean(x * x, axis=-1, keepdims=True) + norm_eps)
        back, gain = norm_back(dn, x, ext_ref, 0, scale)
        gains.append(gain)
        dx_ref[span, :] = dmid_ref[span, :] + back
    total = sum(gains)
    for c in range(d // 128):
        extra_ref[c : c + 1, :] = total[:, c * 128 : (c + 1) * 128]
        extra_ref[6 + c : 7 + c, :] = gain_ref[:, c * 128 : (c + 1) * 128]


def in_back_call(meta, own, rec, x, dmid, ext, found, gain, chunk):
    rows, d = x.shape
    return call(
        functools.partial(in_back_kernel, chunk, rows // 4),
        "in_back",
        (meta, own, rec, x, dmid, ext, *found, gain),
        chunk.arrays,
        [array((rows, d), F32), array((32, 128), F32)],
        [pltpu.VMEM((d, 3 * d), BF16)],
        6 * rows * d * d,
    )


def mask_lanes(lengths, rows):
    spot = jnp.arange(rows, dtype=jnp.int32)
    within = spot % PAIR
    first = jnp.array([0, 512, 768, 896, 960], jnp.int32)
    slot = jnp.sum((within[:, None] >= first[None, 1:]).astype(jnp.int32), axis=1)
    start = jnp.sum(jnp.where(slot[:, None] == jnp.arange(5)[None], first[None], 0), axis=1)
    docs = jnp.arange(lengths.shape[0], dtype=jnp.int32)
    document = spot // PAIR * 5 + slot
    own = jnp.sum(jnp.where(document[:, None] == docs[None], lengths[None], 0), axis=1)
    live = within - start < own
    late = slot == 4
    lane = jnp.arange(128, dtype=jnp.int32) % 64
    shown = [live & ~late, live & late]
    kaug = jnp.where(
        lane[None] == 0,
        jnp.where(shown[0], 0.0, MASKED)[:, None],
        jnp.where(lane[None] == 1, jnp.where(shown[1], 0.0, MASKED)[:, None], 0.0),
    ).astype(BF16)
    qaug = jnp.where(
        lane[None] == 0,
        jnp.where(late, 0.0, 1.0)[:, None],
        jnp.where(lane[None] == 1, jnp.where(late, 1.0, 0.0)[:, None], 0.0),
    ).astype(BF16)
    return qaug, kaug, live


def placed_rows(vector, me, rows):
    count = vector.shape[0]
    spot = jnp.arange(rows * 128, dtype=jnp.int32)[None] - me * count
    hit = spot == jnp.arange(count, dtype=jnp.int32)[:, None]
    flat = jnp.sum(jnp.where(hit, vector.astype(F32)[:, None], 0.0), axis=0)
    return flat.reshape(rows, 128)


def placed_table(vector, me):
    count = vector.shape[0]
    head = jnp.arange(16, dtype=jnp.int32)[:, None]
    bucket = jnp.arange(128, dtype=jnp.int32)[None]
    entry = jnp.where((head < H) & (bucket < BUCKETS), bucket * H + head, -1) - me * count
    hit = entry[None] == jnp.arange(count, dtype=jnp.int32)[:, None, None]
    return jnp.sum(jnp.where(hit, vector.astype(F32)[:, None, None], 0.0), axis=0)


def local(
    ring,
    ring_c,
    hidden,
    gain_attn,
    rel_table,
    query_weight,
    key_weight,
    value_weight,
    output_weight,
    gain_ffn,
    inner_weight,
    outer_weight,
    lengths,
    cotangent,
):
    rows, d = hidden.shape
    ff = inner_weight.shape[1]
    n = ring.n
    shard_rows = query_weight.shape[0]
    outer_rows = outer_weight.shape[0]
    direct = shard_rows % 16 == 0 and shard_rows >= 32 and outer_rows % 32 == 0
    me = lax.axis_index("fsdp")
    core = lax.axis_index("dp")
    meta = ring.meta()
    meta_c = ring_c.meta()
    h = d // 2

    def half(w, which):
        width = w.shape[1] // 2
        return lax.dynamic_slice_in_dim(w, which * width, width, 1)

    small = jnp.concatenate(
        [
            placed_rows(gain_attn, me, d // 128),
            placed_rows(gain_ffn, me, d // 128),
            jnp.zeros((16 - 2 * (d // 128), 128), F32),
            placed_table(rel_table, me),
        ],
        axis=0,
    ).astype(BF16)
    pack_a = [half(w, core) for w in (query_weight, key_weight, value_weight)]
    if direct:
        pack_a.append(jnp.pad(small, ((0, shard_rows - 32), (0, 0))))
    pack_a = jnp.concatenate(pack_a, axis=1)
    pack_b = jnp.concatenate([half(output_weight, core), half(inner_weight, core)], axis=1)
    pack_c = lax.dynamic_slice_in_dim(
        outer_weight, core * (outer_rows // 2), outer_rows // 2, 0
    )

    def whole_columns(own, rec):
        both = []
        for parts, first in ((own, core == 0), (rec, core == 1)):
            pieces = ring.to_origin(jnp.concatenate(parts, axis=0), first)
            both.append(pieces.reshape(-1, pieces.shape[2]))
        first = jnp.where(core == 0, both[0], both[1])
        second = jnp.where(core == 0, both[1], both[0])
        return jnp.stack([first, second])

    qaug, kaug, live = mask_lanes(lengths, rows)
    g = jnp.where(live[:, None], cotangent, jnp.zeros_like(cotangent))
    if direct:
        move_a, move_b = Gather(ring, pack_a), Gather(ring, pack_b)
        move_c = Gather(ring_c, pack_c)
        move_a.go()
        move_c.go()
        move_a.got, move_c.got = lax.optimization_barrier((move_a.got, move_c.got))
        move_c.join()
        for _ in range(ring.bits - 3):
            move_a.join(meta, meta_c, qaug, kaug, g)
            move_a.go()
        move_a.join()
        for _ in range(ring.bits - 3):
            ready(move_a, move_b)
            move_a.go()
            move_b.go()
            move_a.join()
            move_b.join()
        ready(move_a, move_b)
        move_a.go()
        move_b.go()
        move_a.last, move_b.got = lax.optimization_barrier((move_a.last, move_b.got))
        move_b.join()
        final = move_a.last
        move_b.held, final = lax.optimization_barrier((move_b.held, final))
        move_b.go()
        chunk_a = Pieces(*move_a.finish(), n)
        move_c.held, final = lax.optimization_barrier((move_c.held, final))
        move_c.go()
        ext = None
    else:
        got_c = gather_pieces(ring, pack_c)
        chunk_a = Whole(whole_columns(*gather_pieces(ring, pack_a)))
        chunk_b = Whole(whole_columns(*gather_pieces(ring, pack_b)))
        both = [
            ring.to_origin(jnp.concatenate(parts, axis=0), first)
            for parts, first in zip(got_c, (core == 0, core == 1))
        ]
        first = jnp.where(core == 0, both[0], both[1])
        second = jnp.where(core == 0, both[1], both[0])
        chunk_c = Whole(jnp.stack([first, second], axis=1).reshape(ff, d))
        ext = lax.psum(small.astype(F32), "fsdp")

    qkv, normed, dist, ext = qkv_call(meta, hidden, ext, chunk_a)
    if direct:
        (qkv,) = gather_on((qkv,), move_b, move_c)
        near_b = shift(move_b.held, ring.swap_core())
    ctx, lse = attend_call(meta, qkv, qaug, kaug, dist)
    if direct:
        held_b = move_b.held
        ctx, near_b = gather_on((ctx, near_b), move_b, move_c)
        far_b = shift(move_b.last, ring.swap_core())
        near_c = shift(move_c.held, ring.swap_core())
        chunk_b = Pieces((held_b, move_b.last), (near_b, far_b), n)
    middle, normed2, act, slope = mid_call(meta, ctx, hidden, ext, chunk_b, ff)
    if direct:
        act, near_c, move_c.last = lax.optimization_barrier((act, near_c, move_c.last))
        far_c = shift(move_c.last, ring.swap_core())

    def split_columns(pairs, which):
        full = [jnp.einsum("td,tf->df", a, b, preferred_element_type=F32) for a, b in pairs]
        part = jnp.concatenate(full, axis=1).astype(BF16)
        part = part.reshape(n, d // n, part.shape[1])
        return ring.from_origin(part, which == 0)

    if direct:
        grad_c = outer_grad_call(meta, act, g, n)
        far_c, *grad_c = lax.optimization_barrier((far_c, *grad_c))
        chunk_c = Pieces((move_c.held, move_c.last), (near_c, far_c), n)
    else:
        full = jnp.einsum("tf,td->fd", act, g, preferred_element_type=F32).astype(BF16)
        full = full.reshape(n, 2, outer_rows // 2, d)
        grad_c = [
            ring.from_origin(
                lax.dynamic_index_in_dim(full, which, 1, keepdims=False), which == 0
            )
            for which in (core, 1 - core)
        ]
    red_c = Reduce(ring, *grad_c)
    (act,) = tick((act,), fresh=(red_c,))
    result, d_inner = out_call(meta_c, act, middle, g, slope, chunk_c)
    (d_inner,) = tick((d_inner,), (red_c,))
    d_middle, d_att, d_ctx, grad_gain_f = mid_back_call(meta, d_inner, middle, g, ext, chunk_b)
    (d_att,) = tick((d_att,), (red_c,))
    if direct:
        grad_b = mid_grad_call(meta, normed2, ctx, d_inner, d_att, n)
    else:
        grad_b = [
            split_columns([(ctx, half(d_att, w)), (normed2, half(d_inner, w))], w)
            for w in (core, 1 - core)
        ]
    red_b = Reduce(ring, *grad_b)
    (d_ctx,) = tick((after(d_ctx, *grad_b),), (red_c,), (red_b,))
    back = functools.partial(attend_back_call, meta, qkv)
    masks = (qaug, kaug, dist, lse)
    away, found_away = tick(back(d_ctx, *masks, False, (0, 1, 2)), (red_c, red_b))
    if direct:
        send_a = qkv_grad_call(meta, normed, away, n, 3)
    else:
        send_a = split_columns([(normed, away)], 1 - core)
    d_ctx, send_a = lax.optimization_barrier((d_ctx, send_a))
    red_a = Reduce(ring, None, send_a)
    red_a.go()
    stay, found_stay = tick(back(d_ctx, *masks, True, (0, 1, 2)), (red_b,))
    if direct:
        keep_a = qkv_grad_call(meta, normed, stay, n, 2)
    else:
        keep_a = split_columns([(normed, stay)], core)
    red_a.keep = keep_a
    (stay,) = tick((after(stay, keep_a),), (red_a,))
    grad_hidden, extra = in_back_call(
        meta,
        stay,
        away,
        hidden,
        d_middle,
        ext,
        (found_stay, found_away),
        grad_gain_f,
        chunk_a,
    )
    extra, red_b.got = lax.optimization_barrier((extra, red_b.got))
    steps = [ring.swap_phase(k) for k in range(ring.bits)] + [ring.swap_core()]
    extra = extra + shift(extra, steps.pop(0))
    extra, red_a.got = lax.optimization_barrier((extra, red_a.got))
    while red_a.phase > 0:
        red_a.step()
        flat = (extra, red_a.keep, red_a.away)
        extra, red_a.keep, red_a.away = lax.optimization_barrier(flat)
        red_a.go()
        for _ in range(2 if len(steps) > red_a.phase + 1 else 1):
            moved = shift(extra, steps.pop(0))
            extra = extra + moved
        extra, red_a.got = lax.optimization_barrier((extra, red_a.got))
    assert not steps
    sum_c = red_c.finish()
    sum_b = red_b.finish()
    sum_o, sum_b = sum_b[:, :h], sum_b[:, h:]
    sum_a = red_a.finish()

    own = [sum_a, sum_o, sum_b, sum_c]
    other = [shift(s, ring.swap_core()) for s in own]
    low = [jnp.where(core == 0, a, b) for a, b in zip(own, other)]
    high = [jnp.where(core == 0, b, a) for a, b in zip(own, other)]
    grads = [
        jnp.concatenate([low[0][:, t * h : (t + 1) * h], high[0][:, t * h : (t + 1) * h]], axis=1)
        for t in range(3)
    ]
    grad_output = jnp.concatenate([low[1], high[1]], axis=1)
    grad_inner = jnp.concatenate([low[2], high[2]], axis=1)
    grad_outer = jnp.concatenate([low[3], high[3]], axis=0)
    per = d // n
    gain_a = lax.dynamic_slice_in_dim(extra[: d // 128].reshape(-1), me * per, per, 0)
    gain_f = lax.dynamic_slice_in_dim(
        extra[d // 128 : 2 * (d // 128)].reshape(-1), me * per, per, 0
    )
    table = extra[16 : 16 + H, :BUCKETS].T.reshape(-1)
    table = lax.dynamic_slice_in_dim(table, me * rel_table.shape[0], rel_table.shape[0], 0)
    return (
        result,
        grad_hidden,
        gain_a,
        table,
        grads[0],
        grads[1],
        grads[2],
        grad_output,
        gain_f,
        grad_inner,
        grad_outer,
    )


def solution(mesh):
    both = P(("dp", "fsdp"), None)
    line = P("fsdp")
    wide = P("fsdp", None)
    in_specs = (both, line, line, wide, wide, wide, wide, line, wide, wide, P(("dp", "fsdp")), both)
    out_specs = (both, both, line, line, wide, wide, wide, wide, line, wide, wide)
    return jax.shard_map(
        functools.partial(local, Ring(mesh), Ring(mesh, split=True)),
        mesh=mesh,
        in_specs=in_specs,
        out_specs=out_specs,
        check_vma=False,
    )
```

```python
import functools

import jax
import jax.numpy as jnp
import numpy as np
from jax import lax
from jax.experimental import pallas as pl
from jax.experimental.pallas import tpu as pltpu
from jax.sharding import PartitionSpec as P

H = 12
DK = 64
BUCKETS = 32
BLOCK = 512
norm_eps = 1e-06
bucket_edges = (12, 16, 23, 32, 46, 64, 91)
MASKED = -1e30
F32 = jnp.float32
BF16 = jnp.bfloat16
PAIR = 2 * BLOCK
GROUPS = ((0, 512), (512, 256), (768, 128), (896, 128))
SPAN = 1024
SCOPED = {
    "qkv": 9,
    "attend": 8,
    "mid": 8,
    "outer_grad": 9,
    "out": 9,
    "mid_back": 11,
    "mid_grad": 3,
    "attend_back": 7,
    "qkv_grad": 3,
    "in_back": 22,
}


def bucket_of(relative):
    distance = jnp.abs(relative)
    passed = sum(((distance >= edge_value).astype(jnp.int32) for edge_value in bucket_edges))
    return jnp.where(relative > 0, BUCKETS // 2, 0) + jnp.where(
        distance < BUCKETS // 4, distance, BUCKETS // 4 + passed
    )


class Ring:
    def __init__(self, mesh, split=False):
        self.n = mesh.shape["fsdp"]
        self.bits = self.n.bit_length() - 1
        high = list(range(self.bits - 1, 1, -1))
        if split:
            self.order = ([0] + high + [1], [1] + high + [0])
        else:
            self.order = (high + [1, 0], high + [0, 1])

    def swap_phase(self, k):
        n = self.n
        return [
            (c * n + f, c * n + (f ^ (1 << self.order[c][k])))
            for c in range(2)
            for f in range(n)
        ]

    def swap_core(self):
        n = self.n
        return [(c * n + f, (1 - c) * n + f) for c in range(2) for f in range(n)]

    def meta(self):
        me = lax.axis_index("fsdp").astype(jnp.int32)
        core = lax.axis_index("dp").astype(jnp.int32)
        spots = jnp.arange(self.n, dtype=jnp.int32)

        def off(which):
            out = jnp.zeros_like(spots)
            for k, b in enumerate(self.order[which]):
                out = out | (((spots >> k) & 1) << b)
            return out

        def inv(which, m):
            out = jnp.zeros_like(spots)
            for k, b in enumerate(self.order[which]):
                out = out | (((m >> b) & 1) << k)
            return out

        first = core == 0
        mixed = me ^ spots
        return jnp.concatenate(
            [
                core[None],
                me ^ jnp.where(first, off(0), off(1)),
                me ^ jnp.where(first, off(1), off(0)),
                jnp.where(first, inv(0, mixed), inv(1, mixed)),
                jnp.where(first, inv(1, mixed), inv(0, mixed)),
            ]
        )


    def flip_origin(self, pieces):
        me = lax.axis_index("fsdp")
        shape = pieces.shape
        pieces = pieces.reshape((2,) * self.bits + shape[1:])
        for b in range(self.bits):
            axis = self.bits - 1 - b
            pieces = jnp.where((me >> b) & 1 == 1, jnp.flip(pieces, axis), pieces)
        return pieces.reshape(shape)

    def reorder(self, pieces, first, back):
        shape = pieces.shape
        split = pieces.reshape((2,) * self.bits + shape[1:])
        tail = list(range(self.bits, self.bits + len(shape) - 1))
        found = []
        for order in self.order:
            axes = [self.bits - 1 - order.index(self.bits - 1 - a) for a in range(self.bits)]
            if back:
                axes = list(np.argsort(axes))
            found.append(jnp.transpose(split, [int(a) for a in axes] + tail).reshape(shape))
        return jnp.where(first, found[0], found[1])

    def to_origin(self, pieces, first):
        return self.flip_origin(self.reorder(pieces, first, False))

    def from_origin(self, pieces, first):
        return self.reorder(self.flip_origin(pieces), first, True)


def shift(value, pairs):
    return lax.ppermute(value, ("dp", "fsdp"), pairs)


def after(value, *others):
    return lax.optimization_barrier((value, *others))[0]


class Gather:
    def __init__(self, ring, shard):
        self.ring = ring
        self.held = shard[None]
        self.phase = 0
        self.last = None
        self.got = None

    def join(self, *others):
        if self.got is not None:
            got = after(self.got, *others) if others else self.got
            self.held = jnp.concatenate([self.held, got], axis=0)
            self.got = None

    def go(self):
        got = shift(self.held, self.ring.swap_phase(self.phase))
        self.phase += 1
        if self.phase == self.ring.bits:
            self.last = got
        else:
            self.got = got
        return got

    def step(self, *others):
        self.join()
        if others:
            self.held = after(self.held, *others)
        got = self.go()
        return got

    def near(self):
        self.join()
        return self.held

    def finish(self, *others):
        own = (self.held, after(self.last, *others) if others else self.last)
        return own, tuple(shift(p, self.ring.swap_core()) for p in own)


def ready(*moves):
    for move, held in zip(moves, lax.optimization_barrier(tuple(m.held for m in moves))):
        move.held = held


def gather_on(values, *moves):
    values = tuple(values)
    flat = list(values)
    for move in moves:
        move.join(*values)
        flat.append(move.held)
        if move.last is not None:
            flat.append(move.last)
    flat = list(lax.optimization_barrier(tuple(flat)))
    values = [flat.pop(0) for _ in values]
    for move in moves:
        move.held = flat.pop(0)
        if move.last is not None:
            move.last = flat.pop(0)
        else:
            move.go()
    return values


def gather_pieces(ring, shard):
    move = Gather(ring, shard)
    for _ in range(ring.bits):
        move.step()
    return move.finish()


class Reduce:
    def __init__(self, ring, keep, send):
        self.ring = ring
        self.keep = keep
        self.away = send
        self.got = None
        self.phase = ring.bits + 1

    def step(self, *others):
        got = after(self.got, *others) if others else self.got
        self.got = None
        if self.phase == 0:
            return self.keep[0].astype(F32) + got[0].astype(F32)
        half = self.keep.shape[0] // 2

        def add(part):
            return self.keep[part].astype(F32) + got[part].astype(F32)

        self.away = add(slice(half, None)).astype(BF16)
        self.keep = add(slice(0, half))
        if self.phase > 1:
            self.keep = self.keep.astype(BF16)

    def go(self):
        self.phase -= 1
        if self.phase == self.ring.bits:
            pairs = self.ring.swap_core()
        else:
            pairs = self.ring.swap_phase(self.phase)
        self.got = shift(self.away, pairs)

    def finish(self):
        while self.phase > 0:
            if self.got is not None:
                self.step()
            self.go()
        return self.step()


def tick(values, steps=(), fresh=()):
    values = tuple(values)
    for red in steps:
        red.step(*values)
    reds = [*steps, *fresh]
    flat = list(values)
    for red in reds:
        flat += [red.keep, red.away]
    flat = lax.optimization_barrier(tuple(flat))
    for i, red in enumerate(reds):
        red.keep, red.away = flat[len(values) + 2 * i : len(values) + 2 * i + 2]
        red.go()
    return flat[: len(values)]


def params(vmem):
    return pltpu.CompilerParams(vmem_limit_bytes=vmem)


def cost(flops, bytes_accessed, trans=0):
    return pl.CostEstimate(flops=flops, bytes_accessed=bytes_accessed, transcendentals=trans)


def dot(a, b):
    return jnp.dot(a, b, preferred_element_type=F32)


def dot_nt(a, b):
    return lax.dot_general(a, b, (((1,), (1,)), ((), ())), preferred_element_type=F32)


def dot_tn(a, b):
    return lax.dot_general(a, b, (((0,), (0,)), ((), ())), preferred_element_type=F32)


class Pieces:
    def __init__(self, own, rec, n, placed=False):
        self.arrays = [*own, *rec]
        self.n = n
        self.count = len(self.arrays)
        self.part = n // len(own)
        self.whole = False
        self.placed = placed

    def spot(self, meta, h, j):
        place = j if self.placed else meta[1 + h * self.n + j]
        return place, h * (self.count // 2) + j // self.part, j % self.part


class Whole:
    def __init__(self, array):
        self.arrays = [array]
        self.count = 1
        self.whole = True
        self.n = 0


def load_columns(chunk, meta, refs, lo, width, dst, own_first=False):
    core = meta[0]
    if chunk.whole:
        for h in range(2):
            side = (core if h == 0 else 1 - core) if own_first else h
            dst[:, h * width : (h + 1) * width] = refs[0][side, :, lo : lo + width]
        return
    rows = refs[0].shape[1]
    for h in range(2):
        side = h if own_first else (core if h == 0 else 1 - core)
        col = pl.multiple_of(side * width, 128)
        for j in range(chunk.n):
            place, which, index = chunk.spot(meta, h, j)
            row = pl.multiple_of(place * rows, 16)
            dst[pl.ds(row, rows), pl.ds(col, width)] = refs[which][index, :, lo : lo + width]


def load_rows(chunk, meta, refs, dst):
    if chunk.whole:
        dst[...] = refs[0][...]
        return
    rows = refs[0].shape[1]
    core = meta[0]
    for h in range(2):
        for j in range(chunk.n):
            place, which, index = chunk.spot(meta, h, j)
            row = pl.multiple_of(place * (2 * rows) + (core if h == 0 else 1 - core) * rows, 16)
            dst[pl.ds(row, rows), :] = refs[which][index]


def norm_tile(x, ext_ref, first):
    d = x.shape[1]
    scale = lax.rsqrt(jnp.mean(x * x, axis=-1, keepdims=True) + norm_eps)
    out = []
    for c in range(d // 128):
        out.append(
            (x[:, c * 128 : (c + 1) * 128] * scale * ext_ref[first + c : first + c + 1, :]).astype(
                BF16
            )
        )
    return jnp.concatenate(out, axis=1), scale


def call(body, name, inputs, parts, outs, scratch, flops, trans=0, aliases=None):
    meta, *arrays = inputs
    moved = sum(a.size * a.dtype.itemsize for a in [*arrays, *parts])
    moved += sum(int(np.prod(o.shape)) * jnp.dtype(o.dtype).itemsize for o in outs)
    vmem_spec = pl.BlockSpec(memory_space=pltpu.VMEM)
    return pl.pallas_call(
        body,
        in_specs=[pl.BlockSpec(memory_space=pltpu.SMEM)]
        + [vmem_spec] * (len(arrays) + len(parts)),
        out_specs=[vmem_spec] * len(outs),
        out_shape=outs,
        scratch_shapes=scratch,
        input_output_aliases=aliases or {},
        compiler_params=params(SCOPED[name] * 1024 * 1024),
        cost_estimate=cost(flops, moved, trans),
        name=name,
    )(meta, *arrays, *parts)


def away(values):
    return [pltpu.with_memory_space_constraint(v, pltpu.HBM) for v in values]


def array(shape, dtype):
    return jax.ShapeDtypeStruct(shape, dtype)


def qkv_kernel(chunk, tile, meta, x_ref, *rest):
    refs = rest[: chunk.count]
    *given, qkv_ref, n_ref, dist_ref, ext_ref, w = rest[chunk.count :]
    if given:
        ext_ref[...] = given[0][...]
    else:
        lo = w.shape[1] // 2
        ext_ref[...] = sum(
            ref[j, 0:32, lo : lo + 128].astype(F32)
            for ref in refs[: chunk.count // 2]
            for j in range(chunk.part)
        )
    load_columns(chunk, meta, refs, 0, w.shape[1] // 2, w)
    place = lax.broadcasted_iota(jnp.int32, (BUCKETS, SPAN), 1)
    row = lax.broadcasted_iota(jnp.int32, (BUCKETS, SPAN), 0)
    chosen = (bucket_of(BLOCK - 1 - place) == row).astype(F32).astype(BF16)
    dist_ref[...] = dot(ext_ref[16:32, 0:BUCKETS].astype(BF16), chosen)
    rows = x_ref.shape[0]
    for r in range(0, rows, tile):
        n_ref[r : r + tile, :] = norm_tile(x_ref[r : r + tile, :].astype(F32), ext_ref, 0)[0]
    for c in range(0, w.shape[1], 256):
        qkv_ref[:, c : c + 256] = dot(n_ref[...], w[:, c : c + 256]).astype(BF16)


def qkv_call(meta, x, ext, chunk):
    rows, d = x.shape
    return call(
        functools.partial(qkv_kernel, chunk, rows // 4),
        "qkv",
        (meta, x),
        chunk.arrays + ([] if ext is None else [ext]),
        [
            array((rows, 3 * d), BF16),
            array((rows, d), BF16),
            array((16, SPAN), F32),
            array((32, 128), F32),
        ],
        [pltpu.VMEM((d, 3 * d), BF16)],
        6 * rows * d * d,
    )


def bias_strip(dist_row):
    spread = jnp.broadcast_to(dist_row, (128, SPAN))
    return pltpu.roll(spread, SPAN - 127, 1, stride=1, stride_axis=0)


def strip_bias(strip, size, i0, step):
    return jnp.concatenate(
        [
            strip[:, (3 - t) * 128 + i0 : (3 - t) * 128 + i0 + step]
            for t in range(size // 128)
        ],
        axis=0,
    )


def attend_kernel(meta, qkv_ref, qaug_ref, kaug_ref, dist_ref, ctx_ref, lse_ref):
    rows = qkv_ref.shape[0]
    for base in range(0, rows, PAIR):
        lane = lax.broadcasted_iota(jnp.int32, (PAIR, 128), 1)
        qaug, kaug = qaug_ref[base : base + PAIR, :], kaug_ref[base : base + PAIR, :]
        for at in range(H // 2):
            col = (at // 3) * 9 * 128 + (at % 3) * 128
            q = qkv_ref[base : base + PAIR, col : col + 128]
            k = qkv_ref[base : base + PAIR, col + 384 : col + 512]
            v_turned = qkv_ref[base : base + PAIR, col + 768 : col + 896].T
            heads = []
            for hh in range(2):
                mine = (lane // 64) == hh
                heads.append(
                    (
                        jnp.where(mine, q, qaug),
                        jnp.where(mine, k, kaug),
                        v_turned[hh * 64 : (hh + 1) * 64, :],
                        bias_strip(dist_ref[2 * at + hh : 2 * at + hh + 1, :]),
                    )
                )
            for off, size in GROUPS:
                step = size
                for i0 in range(0, size, step):
                    lo, hi = off + i0, off + i0 + step
                    parts = []
                    for hh in range(2):
                        qa, ka, vt, strip = heads[hh]
                        scores = dot_nt(ka[off : off + size], qa[lo:hi])
                        scores = scores + strip_bias(strip, size, i0, step)
                        top = jnp.max(scores, axis=0, keepdims=True)
                        expo = jnp.exp(scores - top)
                        total = jnp.sum(expo, axis=0, keepdims=True)
                        mixed = dot(vt[:, off : off + size], expo.astype(BF16))
                        parts.append(mixed * (1.0 / total))
                        lse_ref[2 * at + hh : 2 * at + hh + 1, base + lo : base + hi] = (
                            top + jnp.log(total)
                        )
                    both = jnp.concatenate(parts, axis=0)
                    ctx_ref[base + lo : base + hi, at * 128 : (at + 1) * 128] = both.T.astype(
                        BF16
                    )


def attend_call(meta, qkv, qaug, kaug, dist):
    rows = qkv.shape[0]
    pairs = rows // PAIR
    return call(
        attend_kernel,
        "attend",
        (meta, qkv, qaug, kaug, dist),
        (),
        [array((rows, H * DK), BF16), array((H, rows), F32)],
        [],
        4 * pairs * H * 350000 * 128,
        trans=pairs * H * 350000,
    )


def mid_kernel(chunk, tile, meta, ctx_ref, x_ref, ext_ref, *rest):
    refs = rest[: chunk.count]
    mid_ref, n2_ref, act_ref, slope_ref, wo, w1 = rest[chunk.count :]
    d = wo.shape[0]
    load_columns(chunk, meta, refs, 0, d // 2, wo)
    load_columns(chunk, meta, refs, d // 2, w1.shape[1] // 2, w1)
    rows = x_ref.shape[0]
    for r in range(0, rows, tile):
        span = slice(r, r + tile)
        middle = x_ref[span, :].astype(F32) + dot(ctx_ref[span, :], wo[...])
        mid_ref[span, :] = middle
        n2_ref[span, :] = norm_tile(middle, ext_ref, 6)[0]
    c0 = 0.7978845608028654
    c1 = c0 * 0.044715
    step = 256
    for f in range(0, w1.shape[1], step):
        for r in range(0, rows, tile):
            span = slice(r, r + tile)
            v = dot(n2_ref[span, :], w1[:, f : f + step])
            v2 = v * v
            half = 0.5 + 0.5 * jnp.tanh(v * (c0 + c1 * v2))
            active = v * half
            act_ref[span, f : f + step] = active.astype(BF16)
            slope_ref[span, f : f + step] = (
                half + (active - active * half) * (2.0 * c0 + (6.0 * c1) * v2)
            ).astype(BF16)


def mid_call(meta, ctx, x, ext, chunk, ff):
    rows, d = x.shape
    return call(
        functools.partial(mid_kernel, chunk, rows),
        "mid",
        (meta, ctx, x, ext),
        chunk.arrays,
        [
            array((rows, d), F32),
            array((rows, d), BF16),
            array((rows, ff), BF16),
            array((rows, ff), BF16),
        ],
        [
            pltpu.VMEM((d, d), BF16),
            pltpu.VMEM((d, ff), BF16),
        ],
        2 * rows * d * (d + ff),
        trans=rows * ff,
    )


def outer_grad_kernel(n, meta, act_ref, g_ref, keep_ref, send_ref):
    per = keep_ref.shape[1]
    first = meta[0] == 0
    width = 4 * per * 2
    for b in range(act_ref.shape[1] // width):
        total = dot_tn(act_ref[:, b * width : (b + 1) * width], g_ref[...]).astype(BF16)
        for f in range(4):
            low = total[2 * f * per : (2 * f + 1) * per]
            high = total[(2 * f + 1) * per : (2 * f + 2) * per]
            spot = b * 4 + f
            keep_ref[meta[1 + 2 * n + spot]] = jnp.where(first, low, high)
            send_ref[meta[1 + 3 * n + spot]] = jnp.where(first, high, low)


def outer_grad_call(meta, act, g, n):
    rows, ff = act.shape
    d = g.shape[1]
    shape = pltpu.HBM((n, ff // n // 2, d), BF16)
    return call(
        functools.partial(outer_grad_kernel, n),
        "outer_grad",
        (meta, act, g),
        (),
        [shape, shape],
        [],
        2 * rows * d * ff,
    )


def out_kernel(chunk, tile, meta, act_ref, mid_ref, g_ref, slope_ref, *rest):
    refs = rest[: chunk.count]
    result_ref, din_ref, w2 = rest[chunk.count :]
    load_rows(chunk, meta, refs, w2)
    rows = g_ref.shape[0]
    step = 256
    for f in range(0, w2.shape[0], step):
        for r in range(0, rows, tile):
            span = slice(r, r + tile)
            d_act = dot_nt(g_ref[span, :], w2[f : f + step, :])
            slope = slope_ref[span, f : f + step].astype(F32)
            din_ref[span, f : f + step] = (d_act * slope).astype(BF16)
    for c in range(0, w2.shape[1], step):
        result_ref[:, c : c + step] = mid_ref[:, c : c + step] + dot(
            act_ref[...], w2[:, c : c + step]
        )


def out_call(meta, act, middle, g, slope, chunk):
    rows, ff = act.shape
    d = middle.shape[1]
    return call(
        functools.partial(out_kernel, chunk, rows // 4),
        "out",
        (meta, act, middle, g, slope),
        chunk.arrays,
        [array((rows, d), F32), array((rows, ff), BF16)],
        [pltpu.VMEM((ff, d), BF16)],
        4 * rows * d * ff,
        aliases={4: 1},
    )


def store_pieces(out, spots, base, total, rows, cols):
    for f in range(total.shape[0] // rows):
        out[spots[base + f], :, cols] = total[f * rows : (f + 1) * rows]


def mid_grad_kernel(n, meta, n2_ref, ctx_ref, din_ref, datt_ref, keep_ref, send_ref):
    per = keep_ref.shape[1]
    h = datt_ref.shape[1] // 2
    ffh = din_ref.shape[1] // 2
    step = 512
    for out, side, table in ((send_ref, 1 - meta[0], 3), (keep_ref, meta[0], 2)):
        base = 1 + table * n
        col = pl.multiple_of(side * h, 128)
        datt = datt_ref[:, pl.ds(col, h)]
        total = dot_tn(ctx_ref[...], datt).astype(BF16)
        store_pieces(out, meta, base, total, per, slice(0, h))
        for c in range(0, ffh, step):
            col = pl.multiple_of(side * ffh + c, 128)
            total = dot_tn(n2_ref[...], din_ref[:, pl.ds(col, step)]).astype(BF16)
            store_pieces(out, meta, base, total, per, slice(h + c, h + c + step))


def mid_grad_call(meta, n2, ctx, d_inner, d_att, n):
    rows, d = n2.shape
    ff = d_inner.shape[1]
    shape = array((n, d // n, (d + ff) // 2), BF16)
    return call(
        functools.partial(mid_grad_kernel, n),
        "mid_grad",
        (meta, n2, ctx, d_inner, d_att),
        (),
        [shape, shape],
        [],
        2 * rows * d * (d + ff),
    )


def qkv_grad_kernel(n, table, meta, n_ref, d_ref, out_ref):
    width = d_ref.shape[1]
    for c in range(0, width, 256):
        cols = slice(c, min(c + 256, width))
        total = dot_tn(n_ref[...], d_ref[:, cols]).astype(BF16)
        store_pieces(out_ref, meta, 1 + table * n, total, out_ref.shape[1], cols)


def qkv_grad_call(meta, normed, dqkv, n, table):
    rows, d = normed.shape
    h = dqkv.shape[1] // 3
    return call(
        functools.partial(qkv_grad_kernel, n, table),
        "qkv_grad",
        (meta, normed, dqkv),
        (),
        [array((n, d // n, 3 * h), BF16)],
        [],
        6 * rows * d * h,
    )[0]


def norm_back(dn, x, gain_ref, first, scale):
    d = x.shape[1]
    z = jnp.concatenate(
        [
            dn[:, c * 128 : (c + 1) * 128] * gain_ref[first + c : first + c + 1, :]
            for c in range(d // 128)
        ],
        axis=1,
    )
    inner = jnp.mean(z * x, axis=-1, keepdims=True)
    back = scale * z - x * (scale * scale * scale * inner)
    return back, jnp.sum(dn * (x * scale), axis=0, keepdims=True)


def mid_back_kernel(chunk, tile, meta, din_ref, mid_ref, g_ref, ext_ref, *rest):
    refs = rest[: chunk.count]
    dmid_ref, datt_ref, dctx_ref, gain_ref, wo, w1 = rest[chunk.count :]
    d = wo.shape[0]
    load_columns(chunk, meta, refs, d // 2, w1.shape[1] // 2, w1)
    load_columns(chunk, meta, refs, 0, d // 2, wo)
    rows = g_ref.shape[0]
    for c in range(0, d, 256):
        dmid_ref[:, c : c + 256] = dot_nt(din_ref[...], w1[c : c + 256, :])
    gains = []
    for r in range(0, rows, tile):
        span = slice(r, r + tile)
        dn = dmid_ref[span, :]
        middle = mid_ref[span, :]
        scale = lax.rsqrt(jnp.mean(middle * middle, axis=-1, keepdims=True) + norm_eps)
        back, gain = norm_back(dn, middle, ext_ref, 6, scale)
        gains.append(gain)
        dmid = g_ref[span, :].astype(F32) + back
        dmid_ref[span, :] = dmid
        datt_ref[span, :] = dmid.astype(BF16)
    for c in range(0, d, 256):
        dctx_ref[:, c : c + 256] = dot_nt(datt_ref[...], wo[c : c + 256, :]).astype(BF16)
    gain_ref[...] = sum(gains)


def mid_back_call(meta, din, middle, g, ext, chunk):
    rows, ff = din.shape
    d = middle.shape[1]
    return call(
        functools.partial(mid_back_kernel, chunk, rows // 4),
        "mid_back",
        (meta, din, middle, g, ext),
        chunk.arrays,
        [
            array((rows, d), F32),
            array((rows, d), BF16),
            array((rows, d), BF16),
            array((1, d), F32),
        ],
        [
            pltpu.VMEM((d, d), BF16),
            pltpu.VMEM((d, ff), BF16),
        ],
        2 * rows * d * (d + ff),
    )


def diagonal_sums(strip):
    for s in (64, 32, 16, 8):
        strip = strip[:s] + pltpu.roll(strip[s:], SPAN - s, 1)
    for s in (4, 2, 1):
        strip = strip + pltpu.roll(pltpu.roll(strip, 8 - s, 0), SPAN - s, 1)
    return strip[:1]


def attend_back_kernel(
    keep,
    todo,
    meta,
    qkv_ref,
    dctx_ref,
    qaug_ref,
    kaug_ref,
    dist_ref,
    lse_ref,
    *rest,
):
    grad_ref, table_ref, strip_acc = rest[-3:]
    side = meta[0] if keep else 1 - meta[0]
    count = H // 4
    rows = qkv_ref.shape[0]
    lane = lax.broadcasted_iota(jnp.int32, (PAIR, 128), 1)
    for pair in todo:
        strip_acc[...] = jnp.zeros_like(strip_acc)
        strips = [
            bias_strip(dist_ref[pl.ds(side * 6 + 2 * pair + hh, 1), :]) for hh in range(2)
        ]
        for base in range(0, rows, PAIR):
            block = slice(base, base + PAIR)

            def part(t):
                col = pl.multiple_of(side * 1152 + (t * 3 + pair) * 128, 128)
                return qkv_ref[block, pl.ds(col, 128)]

            q, k, v = part(0), part(1), part(2)
            do = dctx_ref[block, pl.ds(pl.multiple_of(side * 384 + pair * 128, 128), 128)]
            lse = [lse_ref[pl.ds(side * 6 + 2 * pair + hh, 1), block] for hh in range(2)]
            qaug, kaug = qaug_ref[block, :], kaug_ref[block, :]
            k_turned = k.T
            heads = []
            for hh in range(2):
                mine = (lane // 64) == hh
                heads.append(
                    (
                        jnp.where(mine, q, qaug),
                        jnp.where(mine, k, kaug),
                        jnp.where(mine, v, jnp.zeros_like(v)),
                        k_turned[hh * 64 : (hh + 1) * 64, :],
                        strips[hh],
                    )
                )
            cols = [slice((t * count + pair) * 128, (t * count + pair + 1) * 128) for t in range(3)]
            for off, size in GROUPS:
                step = size
                low = lax.broadcasted_iota(jnp.int32, (size, 128), 1) < 64
                dks, dvs = [None, None], [None, None]
                for i0 in range(0, size, step):
                    lo, hi = off + i0, off + i0 + step
                    dqs = []
                    for hh in range(2):
                        qa, ka, va, kt, strip = heads[hh]
                        scores = dot_nt(ka[off : off + size], qa[lo:hi])
                        scores = scores + strip_bias(strip, size, i0, step)
                        probs = jnp.exp(scores - lse[hh][:, lo:hi])
                        d_probs = dot_nt(va[off : off + size], do[lo:hi])
                        dv = dot(probs.astype(BF16), do[lo:hi])
                        center = jnp.sum(probs * d_probs, axis=0, keepdims=True)
                        d_scores = probs * (d_probs - center)
                        for t in range(size // 128):
                            at = (3 - t) * 128 + i0
                            strip_acc[hh, :, at : at + step] += d_scores[t * 128 : (t + 1) * 128]
                        ds_low = d_scores.astype(BF16)
                        dk = dot(ds_low, q[lo:hi])
                        dqs.append(dot(kt[:, off : off + size], ds_low))
                        dks[hh] = dk if dks[hh] is None else dks[hh] + dk
                        dvs[hh] = dv if dvs[hh] is None else dvs[hh] + dv
                    dq = jnp.concatenate(dqs, axis=0).T.astype(BF16)
                    grad_ref[base + lo : base + hi, cols[0]] = dq
                out = slice(base + off, base + off + size)
                grad_ref[out, cols[1]] = jnp.where(low, dks[0], dks[1]).astype(BF16)
                grad_ref[out, cols[2]] = jnp.where(low, dvs[0], dvs[1]).astype(BF16)
        for hh in range(2):
            table_ref[2 * pair + hh : 2 * pair + hh + 1, :] = diagonal_sums(strip_acc[hh])
    if todo[0] == 0:
        table_ref[2 * count :, :] = jnp.zeros((8 - 2 * count, SPAN), F32)


def attend_back_call(meta, qkv, dctx, qaug, kaug, dist, lse, keep, todo, done=()):
    rows, d = dctx.shape
    pairs = rows // PAIR
    count = H // 4
    return call(
        functools.partial(attend_back_kernel, keep, todo),
        "attend_back",
        (meta, qkv, dctx, qaug, kaug, dist, lse),
        done,
        [array((rows, 3 * count * 128), BF16), array((8, SPAN), F32)],
        [pltpu.VMEM((2, 128, SPAN), F32)],
        20 * pairs * len(todo) * 350000 * 128,
        trans=2 * pairs * len(todo) * 350000,
        aliases={7: 0, 8: 1} if done else None,
    )


def in_back_kernel(chunk, tile, meta, own_ref, rec_ref, x_ref, dmid_ref, ext_ref, *rest):
    stay_ref, away_ref, gain_ref, *rest = rest
    refs = rest[: chunk.count]
    dx_ref, extra_ref, w = rest[chunk.count :]
    load_columns(chunk, meta, refs, 0, w.shape[1] // 2, w, own_first=True)
    place = (lax.broadcasted_iota(jnp.int32, (128, SPAN), 1) + 127) % SPAN
    row = lax.broadcasted_iota(jnp.int32, (128, SPAN), 0)
    chosen = (bucket_of(BLOCK - 1 - place) == row).astype(F32)
    found = [
        lax.dot_general(
            r[...],
            chosen,
            (((1,), (1,)), ((), ())),
            precision=lax.Precision.HIGHEST,
            preferred_element_type=F32,
        )[: H // 2]
        for r in (stay_ref, away_ref)
    ]
    first = meta[0] == 0
    extra_ref[...] = jnp.zeros_like(extra_ref)
    extra_ref[16 : 16 + H // 2, :] = jnp.where(first, found[0], found[1])
    extra_ref[16 + H // 2 : 16 + H, :] = jnp.where(first, found[1], found[0])
    rows, d = x_ref.shape
    both = jnp.concatenate([own_ref[...], rec_ref[...]], axis=1)
    for c in range(0, d, 256):
        dx_ref[:, c : c + 256] = dot_nt(both, w[c : c + 256, :])
    gains = []
    for r in range(0, rows, tile):
        span = slice(r, r + tile)
        dn = dx_ref[span, :]
        x = x_ref[span, :].astype(F32)
        scale = lax.rsqrt(jnp.mean(x * x, axis=-1, keepdims=True) + norm_eps)
        back, gain = norm_back(dn, x, ext_ref, 0, scale)
        gains.append(gain)
        dx_ref[span, :] = dmid_ref[span, :] + back
    total = sum(gains)
    for c in range(d // 128):
        extra_ref[c : c + 1, :] = total[:, c * 128 : (c + 1) * 128]
        extra_ref[6 + c : 7 + c, :] = gain_ref[:, c * 128 : (c + 1) * 128]


def in_back_call(meta, own, rec, x, dmid, ext, found, gain, chunk):
    rows, d = x.shape
    return call(
        functools.partial(in_back_kernel, chunk, rows // 4),
        "in_back",
        (meta, own, rec, x, dmid, ext, *found, gain),
        away(chunk.arrays),
        [array((rows, d), F32), array((32, 128), F32)],
        [pltpu.VMEM((d, 3 * d), BF16)],
        6 * rows * d * d,
    )


def mask_lanes(lengths, rows):
    spot = jnp.arange(rows, dtype=jnp.int32)
    within = spot % PAIR
    first = jnp.array([0, 512, 768, 896, 960], jnp.int32)
    slot = jnp.sum((within[:, None] >= first[None, 1:]).astype(jnp.int32), axis=1)
    start = jnp.sum(jnp.where(slot[:, None] == jnp.arange(5)[None], first[None], 0), axis=1)
    docs = jnp.arange(lengths.shape[0], dtype=jnp.int32)
    document = spot // PAIR * 5 + slot
    own = jnp.sum(jnp.where(document[:, None] == docs[None], lengths[None], 0), axis=1)
    live = within - start < own
    late = slot == 4
    lane = jnp.arange(128, dtype=jnp.int32) % 64
    shown = [live & ~late, live & late]
    kaug = jnp.where(
        lane[None] == 0,
        jnp.where(shown[0], 0.0, MASKED)[:, None],
        jnp.where(lane[None] == 1, jnp.where(shown[1], 0.0, MASKED)[:, None], 0.0),
    ).astype(BF16)
    qaug = jnp.where(
        lane[None] == 0,
        jnp.where(late, 0.0, 1.0)[:, None],
        jnp.where(lane[None] == 1, jnp.where(late, 1.0, 0.0)[:, None], 0.0),
    ).astype(BF16)
    return qaug, kaug, live


def placed_rows(vector, me, rows):
    count = vector.shape[0]
    spot = jnp.arange(rows * 128, dtype=jnp.int32)[None] - me * count
    hit = spot == jnp.arange(count, dtype=jnp.int32)[:, None]
    flat = jnp.sum(jnp.where(hit, vector.astype(F32)[:, None], 0.0), axis=0)
    return flat.reshape(rows, 128)


def placed_table(vector, me):
    count = vector.shape[0]
    head = jnp.arange(16, dtype=jnp.int32)[:, None]
    bucket = jnp.arange(128, dtype=jnp.int32)[None]
    entry = jnp.where((head < H) & (bucket < BUCKETS), bucket * H + head, -1) - me * count
    hit = entry[None] == jnp.arange(count, dtype=jnp.int32)[:, None, None]
    return jnp.sum(jnp.where(hit, vector.astype(F32)[:, None, None], 0.0), axis=0)


def local(
    ring,
    ring_c,
    hidden,
    gain_attn,
    rel_table,
    query_weight,
    key_weight,
    value_weight,
    output_weight,
    gain_ffn,
    inner_weight,
    outer_weight,
    lengths,
    cotangent,
):
    rows, d = hidden.shape
    ff = inner_weight.shape[1]
    n = ring.n
    shard_rows = query_weight.shape[0]
    outer_rows = outer_weight.shape[0]
    direct = shard_rows % 16 == 0 and shard_rows >= 32 and outer_rows % 32 == 0
    me = lax.axis_index("fsdp")
    core = lax.axis_index("dp")
    meta = ring.meta()
    meta_c = ring_c.meta()
    h = d // 2

    def half(w, which):
        width = w.shape[1] // 2
        return lax.dynamic_slice_in_dim(w, which * width, width, 1)

    small = jnp.concatenate(
        [
            placed_rows(gain_attn, me, d // 128),
            placed_rows(gain_ffn, me, d // 128),
            jnp.zeros((16 - 2 * (d // 128), 128), F32),
            placed_table(rel_table, me),
        ],
        axis=0,
    ).astype(BF16)
    pack_a = [half(w, core) for w in (query_weight, key_weight, value_weight)]
    if direct:
        pack_a.append(jnp.pad(small, ((0, shard_rows - 32), (0, 0))))
    pack_a = jnp.concatenate(pack_a, axis=1)
    pack_b = jnp.concatenate([half(output_weight, core), half(inner_weight, core)], axis=1)
    pack_c = lax.dynamic_slice_in_dim(
        outer_weight, core * (outer_rows // 2), outer_rows // 2, 0
    )

    def whole_columns(own, rec):
        both = []
        for parts, first in ((own, core == 0), (rec, core == 1)):
            pieces = ring.to_origin(jnp.concatenate(parts, axis=0), first)
            both.append(pieces.reshape(-1, pieces.shape[2]))
        first = jnp.where(core == 0, both[0], both[1])
        second = jnp.where(core == 0, both[1], both[0])
        return jnp.stack([first, second])

    qaug, kaug, live = mask_lanes(lengths, rows)
    g = jnp.where(live[:, None], cotangent, jnp.zeros_like(cotangent))
    if direct:
        move_a, move_b = Gather(ring, pack_a), Gather(ring, pack_b)
        move_c = Gather(ring_c, pack_c)
        move_a.go()
        move_c.go()
        move_a.got, move_c.got = lax.optimization_barrier((move_a.got, move_c.got))
        move_c.join()
        for _ in range(ring.bits - 3):
            move_a.join(meta, meta_c, qaug, kaug, g)
            move_a.go()
        move_a.join()
        for _ in range(ring.bits - 3):
            ready(move_a, move_b)
            move_a.go()
            move_b.go()
            move_a.join()
            move_b.join()
        ready(move_a, move_b)
        move_a.go()
        move_b.go()
        move_a.last, move_b.got = lax.optimization_barrier((move_a.last, move_b.got))
        move_b.join()
        final = move_a.last
        move_b.held, final = lax.optimization_barrier((move_b.held, final))
        move_b.go()
        chunk_a = Pieces(*move_a.finish(), n)
        move_c.held, final = lax.optimization_barrier((move_c.held, final))
        move_c.go()
        ext = None
    else:
        got_c = gather_pieces(ring, pack_c)
        chunk_a = Whole(whole_columns(*gather_pieces(ring, pack_a)))
        chunk_b = Whole(whole_columns(*gather_pieces(ring, pack_b)))
        both = [
            ring.to_origin(jnp.concatenate(parts, axis=0), first)
            for parts, first in zip(got_c, (core == 0, core == 1))
        ]
        first = jnp.where(core == 0, both[0], both[1])
        second = jnp.where(core == 0, both[1], both[0])
        chunk_c = Whole(jnp.stack([first, second], axis=1).reshape(ff, d))
        ext = lax.psum(small.astype(F32), "fsdp")

    qkv, normed, dist, ext = qkv_call(meta, hidden, ext, chunk_a)
    if direct:
        (qkv,) = gather_on((qkv,), move_b, move_c)
        near_b = shift(move_b.held, ring.swap_core())
    ctx, lse = attend_call(meta, qkv, qaug, kaug, dist)
    if direct:
        held_b = move_b.held
        ctx, near_b = gather_on((ctx, near_b), move_b, move_c)
        far_b = shift(move_b.last, ring.swap_core())
        near_c = shift(move_c.held, ring.swap_core())
        chunk_b = Pieces((held_b, move_b.last), (near_b, far_b), n)
    middle, normed2, act, slope = mid_call(meta, ctx, hidden, ext, chunk_b, ff)
    if direct:
        act, near_c, move_c.last = lax.optimization_barrier((act, near_c, move_c.last))
        far_c = shift(move_c.last, ring.swap_core())

    def split_columns(pairs, which):
        full = [jnp.einsum("td,tf->df", a, b, preferred_element_type=F32) for a, b in pairs]
        part = jnp.concatenate(full, axis=1).astype(BF16)
        part = part.reshape(n, d // n, part.shape[1])
        return ring.from_origin(part, which == 0)

    if direct:
        grad_c = outer_grad_call(meta, act, g, n)
        far_c, *grad_c = lax.optimization_barrier((far_c, *grad_c))
        chunk_c = Pieces((move_c.held, move_c.last), (near_c, far_c), n)
    else:
        full = jnp.einsum("tf,td->fd", act, g, preferred_element_type=F32).astype(BF16)
        full = full.reshape(n, 2, outer_rows // 2, d)
        grad_c = [
            ring.from_origin(
                lax.dynamic_index_in_dim(full, which, 1, keepdims=False), which == 0
            )
            for which in (core, 1 - core)
        ]
    red_c = Reduce(ring, *grad_c)
    (act,) = tick((act,), fresh=(red_c,))
    result, d_inner = out_call(meta_c, act, middle, g, slope, chunk_c)
    (d_inner,) = tick((d_inner,), (red_c,))
    d_middle, d_att, d_ctx, grad_gain_f = mid_back_call(meta, d_inner, middle, g, ext, chunk_b)
    (d_att,) = tick((d_att,), (red_c,))
    if direct:
        grad_b = mid_grad_call(meta, normed2, ctx, d_inner, d_att, n)
    else:
        grad_b = [
            split_columns([(ctx, half(d_att, w)), (normed2, half(d_inner, w))], w)
            for w in (core, 1 - core)
        ]
    red_b = Reduce(ring, *grad_b)
    (d_ctx,) = tick((after(d_ctx, *grad_b),), (red_c,), (red_b,))
    back = functools.partial(attend_back_call, meta, qkv)
    masks = (qaug, kaug, dist, lse)
    away, found_away = tick(back(d_ctx, *masks, False, (0, 1, 2)), (red_c, red_b))
    if direct:
        send_a = qkv_grad_call(meta, normed, away, n, 3)
    else:
        send_a = split_columns([(normed, away)], 1 - core)
    d_ctx, send_a = lax.optimization_barrier((d_ctx, send_a))
    red_a = Reduce(ring, None, send_a)
    red_a.go()
    stay, found_stay = tick(back(d_ctx, *masks, True, (0, 1, 2)), (red_b,))
    if direct:
        keep_a = qkv_grad_call(meta, normed, stay, n, 2)
    else:
        keep_a = split_columns([(normed, stay)], core)
    red_a.keep = keep_a
    (stay,) = tick((after(stay, keep_a),), (red_a,))
    grad_hidden, extra = in_back_call(
        meta,
        stay,
        away,
        hidden,
        d_middle,
        ext,
        (found_stay, found_away),
        grad_gain_f,
        chunk_a,
    )
    extra, red_b.got = lax.optimization_barrier((extra, red_b.got))
    steps = [ring.swap_phase(k) for k in range(ring.bits)] + [ring.swap_core()]
    extra = extra + shift(extra, steps.pop(0))
    extra, red_a.got = lax.optimization_barrier((extra, red_a.got))
    while red_a.phase > 0:
        red_a.step()
        flat = (extra, red_a.keep, red_a.away)
        extra, red_a.keep, red_a.away = lax.optimization_barrier(flat)
        red_a.go()
        for _ in range(2 if len(steps) > red_a.phase + 1 else 1):
            moved = shift(extra, steps.pop(0))
            extra = extra + moved
        extra, red_a.got = lax.optimization_barrier((extra, red_a.got))
    assert not steps
    sum_c = red_c.finish()
    sum_b = red_b.finish()
    sum_o, sum_b = sum_b[:, :h], sum_b[:, h:]
    sum_a = red_a.finish()

    own = [sum_a, sum_o, sum_b, sum_c]
    other = [shift(s, ring.swap_core()) for s in own]
    low = [jnp.where(core == 0, a, b) for a, b in zip(own, other)]
    high = [jnp.where(core == 0, b, a) for a, b in zip(own, other)]
    grads = [
        jnp.concatenate([low[0][:, t * h : (t + 1) * h], high[0][:, t * h : (t + 1) * h]], axis=1)
        for t in range(3)
    ]
    grad_output = jnp.concatenate([low[1], high[1]], axis=1)
    grad_inner = jnp.concatenate([low[2], high[2]], axis=1)
    grad_outer = jnp.concatenate([low[3], high[3]], axis=0)
    per = d // n
    gain_a = lax.dynamic_slice_in_dim(extra[: d // 128].reshape(-1), me * per, per, 0)
    gain_f = lax.dynamic_slice_in_dim(
        extra[d // 128 : 2 * (d // 128)].reshape(-1), me * per, per, 0
    )
    table = extra[16 : 16 + H, :BUCKETS].T.reshape(-1)
    table = lax.dynamic_slice_in_dim(table, me * rel_table.shape[0], rel_table.shape[0], 0)
    return (
        result,
        grad_hidden,
        gain_a,
        table,
        grads[0],
        grads[1],
        grads[2],
        grad_output,
        gain_f,
        grad_inner,
        grad_outer,
    )


def solution(mesh):
    both = P(("dp", "fsdp"), None)
    line = P("fsdp")
    wide = P("fsdp", None)
    in_specs = (both, line, line, wide, wide, wide, wide, line, wide, wide, P(("dp", "fsdp")), both)
    out_specs = (both, both, line, line, wide, wide, wide, wide, line, wide, wide)
    return jax.shard_map(
        functools.partial(local, Ring(mesh), Ring(mesh, split=True)),
        mesh=mesh,
        in_specs=in_specs,
        out_specs=out_specs,
        check_vma=False,
    )
```

```python
import functools

import jax
import jax.numpy as jnp
import numpy as np
from jax import lax
from jax.experimental import pallas as pl
from jax.experimental.pallas import tpu as pltpu
from jax.sharding import PartitionSpec as P

H = 12
DK = 64
BUCKETS = 32
BLOCK = 512
norm_eps = 1e-06
bucket_edges = (12, 16, 23, 32, 46, 64, 91)
MASKED = -1e30
F32 = jnp.float32
BF16 = jnp.bfloat16
PAIR = 2 * BLOCK
GROUPS = ((0, 512), (512, 256), (768, 128), (896, 128))
SPAN = 1024
SCOPED = {
    "qkv": 9,
    "attend": 8,
    "mid": 8,
    "outer_grad": 9,
    "out": 9,
    "mid_back": 11,
    "mid_grad": 3,
    "attend_back": 7,
    "qkv_grad": 3,
    "in_back": 22,
}


def bucket_of(relative):
    distance = jnp.abs(relative)
    passed = sum(((distance >= edge_value).astype(jnp.int32) for edge_value in bucket_edges))
    return jnp.where(relative > 0, BUCKETS // 2, 0) + jnp.where(
        distance < BUCKETS // 4, distance, BUCKETS // 4 + passed
    )


class Ring:
    def __init__(self, mesh, split=False):
        self.n = mesh.shape["fsdp"]
        self.bits = self.n.bit_length() - 1
        high = list(range(self.bits - 1, 1, -1))
        if split:
            self.order = ([0] + high + [1], [1] + high + [0])
        else:
            self.order = (high + [1, 0], high + [0, 1])

    def swap_phase(self, k):
        n = self.n
        return [
            (c * n + f, c * n + (f ^ (1 << self.order[c][k])))
            for c in range(2)
            for f in range(n)
        ]

    def swap_core(self):
        n = self.n
        return [(c * n + f, (1 - c) * n + f) for c in range(2) for f in range(n)]

    def meta(self):
        me = lax.axis_index("fsdp").astype(jnp.int32)
        core = lax.axis_index("dp").astype(jnp.int32)
        spots = jnp.arange(self.n, dtype=jnp.int32)

        def off(which):
            out = jnp.zeros_like(spots)
            for k, b in enumerate(self.order[which]):
                out = out | (((spots >> k) & 1) << b)
            return out

        def inv(which, m):
            out = jnp.zeros_like(spots)
            for k, b in enumerate(self.order[which]):
                out = out | (((m >> b) & 1) << k)
            return out

        first = core == 0
        mixed = me ^ spots
        return jnp.concatenate(
            [
                core[None],
                me ^ jnp.where(first, off(0), off(1)),
                me ^ jnp.where(first, off(1), off(0)),
                jnp.where(first, inv(0, mixed), inv(1, mixed)),
                jnp.where(first, inv(1, mixed), inv(0, mixed)),
            ]
        )


    def flip_origin(self, pieces):
        me = lax.axis_index("fsdp")
        shape = pieces.shape
        pieces = pieces.reshape((2,) * self.bits + shape[1:])
        for b in range(self.bits):
            axis = self.bits - 1 - b
            pieces = jnp.where((me >> b) & 1 == 1, jnp.flip(pieces, axis), pieces)
        return pieces.reshape(shape)

    def reorder(self, pieces, first, back):
        shape = pieces.shape
        split = pieces.reshape((2,) * self.bits + shape[1:])
        tail = list(range(self.bits, self.bits + len(shape) - 1))
        found = []
        for order in self.order:
            axes = [self.bits - 1 - order.index(self.bits - 1 - a) for a in range(self.bits)]
            if back:
                axes = list(np.argsort(axes))
            found.append(jnp.transpose(split, [int(a) for a in axes] + tail).reshape(shape))
        return jnp.where(first, found[0], found[1])

    def to_origin(self, pieces, first):
        return self.flip_origin(self.reorder(pieces, first, False))

    def from_origin(self, pieces, first):
        return self.reorder(self.flip_origin(pieces), first, True)


def shift(value, pairs):
    return lax.ppermute(value, ("dp", "fsdp"), pairs)


def after(value, *others):
    return lax.optimization_barrier((value, *others))[0]


class Gather:
    def __init__(self, ring, shard):
        self.ring = ring
        self.held = shard[None]
        self.phase = 0
        self.last = None
        self.got = None

    def join(self, *others):
        if self.got is not None:
            got = after(self.got, *others) if others else self.got
            self.held = jnp.concatenate([self.held, got], axis=0)
            self.got = None

    def go(self):
        got = shift(self.held, self.ring.swap_phase(self.phase))
        self.phase += 1
        if self.phase == self.ring.bits:
            self.last = got
        else:
            self.got = got
        return got

    def step(self, *others):
        self.join()
        if others:
            self.held = after(self.held, *others)
        got = self.go()
        return got

    def near(self):
        self.join()
        return self.held

    def finish(self, *others):
        own = (self.held, after(self.last, *others) if others else self.last)
        return own, tuple(shift(p, self.ring.swap_core()) for p in own)


def ready(*moves):
    for move, held in zip(moves, lax.optimization_barrier(tuple(m.held for m in moves))):
        move.held = held


def gather_on(values, *moves):
    values = tuple(values)
    flat = list(values)
    for move in moves:
        move.join(*values)
        flat.append(move.held)
        if move.last is not None:
            flat.append(move.last)
    flat = list(lax.optimization_barrier(tuple(flat)))
    values = [flat.pop(0) for _ in values]
    for move in moves:
        move.held = flat.pop(0)
        if move.last is not None:
            move.last = flat.pop(0)
        else:
            move.go()
    return values


def gather_pieces(ring, shard):
    move = Gather(ring, shard)
    for _ in range(ring.bits):
        move.step()
    return move.finish()


class Reduce:
    def __init__(self, ring, keep, send):
        self.ring = ring
        self.keep = keep
        self.away = send
        self.got = None
        self.phase = ring.bits + 1

    def step(self, *others):
        got = after(self.got, *others) if others else self.got
        self.got = None
        if self.phase == 0:
            return self.keep[0].astype(F32) + got[0].astype(F32)
        half = self.keep.shape[0] // 2

        def add(part):
            return self.keep[part].astype(F32) + got[part].astype(F32)

        self.away = add(slice(half, None)).astype(BF16)
        self.keep = add(slice(0, half))
        if self.phase > 1:
            self.keep = self.keep.astype(BF16)

    def go(self):
        self.phase -= 1
        if self.phase == self.ring.bits:
            pairs = self.ring.swap_core()
        else:
            pairs = self.ring.swap_phase(self.phase)
        self.got = shift(self.away, pairs)

    def finish(self):
        while self.phase > 0:
            if self.got is not None:
                self.step()
            self.go()
        return self.step()


def tick(values, steps=(), fresh=()):
    values = tuple(values)
    for red in steps:
        red.step(*values)
    reds = [*steps, *fresh]
    flat = list(values)
    for red in reds:
        flat += [red.keep, red.away]
    flat = lax.optimization_barrier(tuple(flat))
    for i, red in enumerate(reds):
        red.keep, red.away = flat[len(values) + 2 * i : len(values) + 2 * i + 2]
        red.go()
    return flat[: len(values)]


def params(vmem):
    return pltpu.CompilerParams(vmem_limit_bytes=vmem)


def cost(flops, bytes_accessed, trans=0):
    return pl.CostEstimate(flops=flops, bytes_accessed=bytes_accessed, transcendentals=trans)


def dot(a, b):
    return jnp.dot(a, b, preferred_element_type=F32)


def dot_nt(a, b):
    return lax.dot_general(a, b, (((1,), (1,)), ((), ())), preferred_element_type=F32)


def dot_tn(a, b):
    return lax.dot_general(a, b, (((0,), (0,)), ((), ())), preferred_element_type=F32)


class Pieces:
    def __init__(self, own, rec, n, placed=False):
        self.arrays = [*own, *rec]
        self.n = n
        self.count = len(self.arrays)
        self.part = n // len(own)
        self.whole = False
        self.placed = placed

    def spot(self, meta, h, j):
        place = j if self.placed else meta[1 + h * self.n + j]
        return place, h * (self.count // 2) + j // self.part, j % self.part


class Whole:
    def __init__(self, array):
        self.arrays = [array]
        self.count = 1
        self.whole = True
        self.n = 0


def load_columns(chunk, meta, refs, lo, width, dst, own_first=False):
    core = meta[0]
    if chunk.whole:
        for h in range(2):
            side = (core if h == 0 else 1 - core) if own_first else h
            dst[:, h * width : (h + 1) * width] = refs[0][side, :, lo : lo + width]
        return
    rows = refs[0].shape[1]
    for h in range(2):
        side = h if own_first else (core if h == 0 else 1 - core)
        col = pl.multiple_of(side * width, 128)
        for j in range(chunk.n):
            place, which, index = chunk.spot(meta, h, j)
            row = pl.multiple_of(place * rows, 16)
            dst[pl.ds(row, rows), pl.ds(col, width)] = refs[which][index, :, lo : lo + width]


def load_rows(chunk, meta, refs, dst):
    if chunk.whole:
        dst[...] = refs[0][...]
        return
    rows = refs[0].shape[1]
    core = meta[0]
    for h in range(2):
        for j in range(chunk.n):
            place, which, index = chunk.spot(meta, h, j)
            row = pl.multiple_of(place * (2 * rows) + (core if h == 0 else 1 - core) * rows, 16)
            dst[pl.ds(row, rows), :] = refs[which][index]


def norm_tile(x, ext_ref, first):
    d = x.shape[1]
    scale = lax.rsqrt(jnp.mean(x * x, axis=-1, keepdims=True) + norm_eps)
    out = []
    for c in range(d // 128):
        out.append(
            (x[:, c * 128 : (c + 1) * 128] * scale * ext_ref[first + c : first + c + 1, :]).astype(
                BF16
            )
        )
    return jnp.concatenate(out, axis=1), scale


def call(body, name, inputs, parts, outs, scratch, flops, trans=0, aliases=None):
    meta, *arrays = inputs
    moved = sum(a.size * a.dtype.itemsize for a in [*arrays, *parts])
    moved += sum(int(np.prod(o.shape)) * jnp.dtype(o.dtype).itemsize for o in outs)
    vmem_spec = pl.BlockSpec(memory_space=pltpu.VMEM)
    return pl.pallas_call(
        body,
        in_specs=[pl.BlockSpec(memory_space=pltpu.SMEM)]
        + [vmem_spec] * (len(arrays) + len(parts)),
        out_specs=[vmem_spec] * len(outs),
        out_shape=outs,
        scratch_shapes=scratch,
        input_output_aliases=aliases or {},
        compiler_params=params(SCOPED[name] * 1024 * 1024),
        cost_estimate=cost(flops, moved, trans),
        name=name,
    )(meta, *arrays, *parts)


def away(values):
    return [pltpu.with_memory_space_constraint(v, pltpu.HBM) for v in values]


def array(shape, dtype):
    return jax.ShapeDtypeStruct(shape, dtype)


def qkv_kernel(chunk, tile, meta, x_ref, *rest):
    refs = rest[: chunk.count]
    *given, qkv_ref, n_ref, dist_ref, ext_ref, w = rest[chunk.count :]
    if given:
        ext_ref[...] = given[0][...]
    else:
        lo = w.shape[1] // 2
        ext_ref[...] = sum(
            ref[j, 0:32, lo : lo + 128].astype(F32)
            for ref in refs[: chunk.count // 2]
            for j in range(chunk.part)
        )
    load_columns(chunk, meta, refs, 0, w.shape[1] // 2, w)
    place = lax.broadcasted_iota(jnp.int32, (BUCKETS, SPAN), 1)
    row = lax.broadcasted_iota(jnp.int32, (BUCKETS, SPAN), 0)
    chosen = (bucket_of(BLOCK - 1 - place) == row).astype(F32).astype(BF16)
    dist_ref[...] = dot(ext_ref[16:32, 0:BUCKETS].astype(BF16), chosen)
    rows = x_ref.shape[0]
    for r in range(0, rows, tile):
        n_ref[r : r + tile, :] = norm_tile(x_ref[r : r + tile, :].astype(F32), ext_ref, 0)[0]
    for c in range(0, w.shape[1], 256):
        qkv_ref[:, c : c + 256] = dot(n_ref[...], w[:, c : c + 256]).astype(BF16)


def qkv_call(meta, x, ext, chunk):
    rows, d = x.shape
    return call(
        functools.partial(qkv_kernel, chunk, rows // 4),
        "qkv",
        (meta, x),
        chunk.arrays + ([] if ext is None else [ext]),
        [
            array((rows, 3 * d), BF16),
            array((rows, d), BF16),
            array((16, SPAN), F32),
            array((32, 128), F32),
        ],
        [pltpu.VMEM((d, 3 * d), BF16)],
        6 * rows * d * d,
    )


def bias_strip(dist_row):
    spread = jnp.broadcast_to(dist_row, (128, SPAN))
    return pltpu.roll(spread, SPAN - 127, 1, stride=1, stride_axis=0)


def strip_bias(strip, size, i0, step):
    return jnp.concatenate(
        [
            strip[:, (3 - t) * 128 + i0 : (3 - t) * 128 + i0 + step]
            for t in range(size // 128)
        ],
        axis=0,
    )


def attend_kernel(meta, qkv_ref, qaug_ref, kaug_ref, dist_ref, ctx_ref, lse_ref):
    rows = qkv_ref.shape[0]
    for base in range(0, rows, PAIR):
        lane = lax.broadcasted_iota(jnp.int32, (PAIR, 128), 1)
        qaug, kaug = qaug_ref[base : base + PAIR, :], kaug_ref[base : base + PAIR, :]
        for at in range(H // 2):
            col = (at // 3) * 9 * 128 + (at % 3) * 128
            q = qkv_ref[base : base + PAIR, col : col + 128]
            k = qkv_ref[base : base + PAIR, col + 384 : col + 512]
            v_turned = qkv_ref[base : base + PAIR, col + 768 : col + 896].T
            heads = []
            for hh in range(2):
                mine = (lane // 64) == hh
                heads.append(
                    (
                        jnp.where(mine, q, qaug),
                        jnp.where(mine, k, kaug),
                        v_turned[hh * 64 : (hh + 1) * 64, :],
                        bias_strip(dist_ref[2 * at + hh : 2 * at + hh + 1, :]),
                    )
                )
            for off, size in GROUPS:
                step = size
                for i0 in range(0, size, step):
                    lo, hi = off + i0, off + i0 + step
                    parts = []
                    for hh in range(2):
                        qa, ka, vt, strip = heads[hh]
                        scores = dot_nt(ka[off : off + size], qa[lo:hi])
                        scores = scores + strip_bias(strip, size, i0, step)
                        top = jnp.max(scores, axis=0, keepdims=True)
                        expo = jnp.exp(scores - top)
                        total = jnp.sum(expo, axis=0, keepdims=True)
                        mixed = dot(vt[:, off : off + size], expo.astype(BF16))
                        parts.append(mixed * (1.0 / total))
                        lse_ref[2 * at + hh : 2 * at + hh + 1, base + lo : base + hi] = (
                            top + jnp.log(total)
                        )
                    both = jnp.concatenate(parts, axis=0)
                    ctx_ref[base + lo : base + hi, at * 128 : (at + 1) * 128] = both.T.astype(
                        BF16
                    )


def attend_call(meta, qkv, qaug, kaug, dist):
    rows = qkv.shape[0]
    pairs = rows // PAIR
    return call(
        attend_kernel,
        "attend",
        (meta, qkv, qaug, kaug, dist),
        (),
        [array((rows, H * DK), BF16), array((H, rows), F32)],
        [],
        4 * pairs * H * 350000 * 128,
        trans=pairs * H * 350000,
    )


def mid_kernel(chunk, tile, meta, ctx_ref, x_ref, ext_ref, *rest):
    refs = rest[: chunk.count]
    mid_ref, n2_ref, act_ref, slope_ref, wo, w1 = rest[chunk.count :]
    d = wo.shape[0]
    load_columns(chunk, meta, refs, 0, d // 2, wo)
    load_columns(chunk, meta, refs, d // 2, w1.shape[1] // 2, w1)
    rows = x_ref.shape[0]
    for r in range(0, rows, tile):
        span = slice(r, r + tile)
        middle = x_ref[span, :].astype(F32) + dot(ctx_ref[span, :], wo[...])
        mid_ref[span, :] = middle
        n2_ref[span, :] = norm_tile(middle, ext_ref, 6)[0]
    c0 = 0.7978845608028654
    c1 = c0 * 0.044715
    step = 256
    for f in range(0, w1.shape[1], step):
        for r in range(0, rows, tile):
            span = slice(r, r + tile)
            v = dot(n2_ref[span, :], w1[:, f : f + step])
            v2 = v * v
            half = 0.5 + 0.5 * jnp.tanh(v * (c0 + c1 * v2))
            active = v * half
            act_ref[span, f : f + step] = active.astype(BF16)
            slope_ref[span, f : f + step] = (
                half + (active - active * half) * (2.0 * c0 + (6.0 * c1) * v2)
            ).astype(BF16)


def mid_call(meta, ctx, x, ext, chunk, ff):
    rows, d = x.shape
    return call(
        functools.partial(mid_kernel, chunk, rows),
        "mid",
        (meta, ctx, x, ext),
        chunk.arrays,
        [
            array((rows, d), F32),
            array((rows, d), BF16),
            array((rows, ff), BF16),
            array((rows, ff), BF16),
        ],
        [
            pltpu.VMEM((d, d), BF16),
            pltpu.VMEM((d, ff), BF16),
        ],
        2 * rows * d * (d + ff),
        trans=rows * ff,
    )


def outer_grad_kernel(n, meta, act_ref, g_ref, keep_ref, send_ref):
    per = keep_ref.shape[1]
    first = meta[0] == 0
    width = 4 * per * 2
    for b in range(act_ref.shape[1] // width):
        total = dot_tn(act_ref[:, b * width : (b + 1) * width], g_ref[...]).astype(BF16)
        for f in range(4):
            low = total[2 * f * per : (2 * f + 1) * per]
            high = total[(2 * f + 1) * per : (2 * f + 2) * per]
            spot = b * 4 + f
            keep_ref[meta[1 + 2 * n + spot]] = jnp.where(first, low, high)
            send_ref[meta[1 + 3 * n + spot]] = jnp.where(first, high, low)


def outer_grad_call(meta, act, g, n):
    rows, ff = act.shape
    d = g.shape[1]
    shape = pltpu.HBM((n, ff // n // 2, d), BF16)
    return call(
        functools.partial(outer_grad_kernel, n),
        "outer_grad",
        (meta, act, g),
        (),
        [shape, shape],
        [],
        2 * rows * d * ff,
    )


def out_kernel(chunk, tile, meta, act_ref, mid_ref, g_ref, slope_ref, *rest):
    refs = rest[: chunk.count]
    result_ref, din_ref, w2 = rest[chunk.count :]
    load_rows(chunk, meta, refs, w2)
    rows = g_ref.shape[0]
    step = 256
    for f in range(0, w2.shape[0], step):
        for r in range(0, rows, tile):
            span = slice(r, r + tile)
            d_act = dot_nt(g_ref[span, :], w2[f : f + step, :])
            slope = slope_ref[span, f : f + step].astype(F32)
            din_ref[span, f : f + step] = (d_act * slope).astype(BF16)
    for c in range(0, w2.shape[1], step):
        result_ref[:, c : c + step] = mid_ref[:, c : c + step] + dot(
            act_ref[...], w2[:, c : c + step]
        )


def out_call(meta, act, middle, g, slope, chunk):
    rows, ff = act.shape
    d = middle.shape[1]
    return call(
        functools.partial(out_kernel, chunk, rows // 4),
        "out",
        (meta, act, middle, g, slope),
        chunk.arrays,
        [array((rows, d), F32), array((rows, ff), BF16)],
        [pltpu.VMEM((ff, d), BF16)],
        4 * rows * d * ff,
        aliases={4: 1},
    )


def store_pieces(out, spots, base, total, rows, cols):
    for f in range(total.shape[0] // rows):
        out[spots[base + f], :, cols] = total[f * rows : (f + 1) * rows]


def mid_grad_kernel(n, meta, n2_ref, ctx_ref, din_ref, datt_ref, keep_ref, send_ref):
    per = keep_ref.shape[1]
    h = datt_ref.shape[1] // 2
    ffh = din_ref.shape[1] // 2
    step = 512
    for out, side, table in ((send_ref, 1 - meta[0], 3), (keep_ref, meta[0], 2)):
        base = 1 + table * n
        col = pl.multiple_of(side * h, 128)
        datt = datt_ref[:, pl.ds(col, h)]
        total = dot_tn(ctx_ref[...], datt).astype(BF16)
        store_pieces(out, meta, base, total, per, slice(0, h))
        for c in range(0, ffh, step):
            col = pl.multiple_of(side * ffh + c, 128)
            total = dot_tn(n2_ref[...], din_ref[:, pl.ds(col, step)]).astype(BF16)
            store_pieces(out, meta, base, total, per, slice(h + c, h + c + step))


def mid_grad_call(meta, n2, ctx, d_inner, d_att, n):
    rows, d = n2.shape
    ff = d_inner.shape[1]
    shape = array((n, d // n, (d + ff) // 2), BF16)
    return call(
        functools.partial(mid_grad_kernel, n),
        "mid_grad",
        (meta, n2, ctx, d_inner, d_att),
        (),
        [shape, shape],
        [],
        2 * rows * d * (d + ff),
    )


def qkv_grad_kernel(n, table, meta, n_ref, d_ref, out_ref):
    width = d_ref.shape[1]
    for c in range(0, width, 256):
        cols = slice(c, min(c + 256, width))
        total = dot_tn(n_ref[...], d_ref[:, cols]).astype(BF16)
        store_pieces(out_ref, meta, 1 + table * n, total, out_ref.shape[1], cols)


def qkv_grad_call(meta, normed, dqkv, n, table):
    rows, d = normed.shape
    h = dqkv.shape[1] // 3
    return call(
        functools.partial(qkv_grad_kernel, n, table),
        "qkv_grad",
        (meta, normed, dqkv),
        (),
        [array((n, d // n, 3 * h), BF16)],
        [],
        6 * rows * d * h,
    )[0]


def norm_back(dn, x, gain_ref, first, scale):
    d = x.shape[1]
    z = jnp.concatenate(
        [
            dn[:, c * 128 : (c + 1) * 128] * gain_ref[first + c : first + c + 1, :]
            for c in range(d // 128)
        ],
        axis=1,
    )
    inner = jnp.mean(z * x, axis=-1, keepdims=True)
    back = scale * z - x * (scale * scale * scale * inner)
    return back, jnp.sum(dn * (x * scale), axis=0, keepdims=True)


def mid_back_kernel(chunk, tile, meta, din_ref, mid_ref, g_ref, ext_ref, *rest):
    refs = rest[: chunk.count]
    dmid_ref, datt_ref, dctx_ref, gain_ref, wo, w1 = rest[chunk.count :]
    d = wo.shape[0]
    load_columns(chunk, meta, refs, d // 2, w1.shape[1] // 2, w1)
    load_columns(chunk, meta, refs, 0, d // 2, wo)
    rows = g_ref.shape[0]
    for c in range(0, d, 256):
        dmid_ref[:, c : c + 256] = dot_nt(din_ref[...], w1[c : c + 256, :])
    gains = []
    for r in range(0, rows, tile):
        span = slice(r, r + tile)
        dn = dmid_ref[span, :]
        middle = mid_ref[span, :]
        scale = lax.rsqrt(jnp.mean(middle * middle, axis=-1, keepdims=True) + norm_eps)
        back, gain = norm_back(dn, middle, ext_ref, 6, scale)
        gains.append(gain)
        dmid = g_ref[span, :].astype(F32) + back
        dmid_ref[span, :] = dmid
        datt_ref[span, :] = dmid.astype(BF16)
    for c in range(0, d, 256):
        dctx_ref[:, c : c + 256] = dot_nt(datt_ref[...], wo[c : c + 256, :]).astype(BF16)
    gain_ref[...] = sum(gains)


def mid_back_call(meta, din, middle, g, ext, chunk):
    rows, ff = din.shape
    d = middle.shape[1]
    return call(
        functools.partial(mid_back_kernel, chunk, rows // 4),
        "mid_back",
        (meta, din, middle, g, ext),
        chunk.arrays,
        [
            array((rows, d), F32),
            array((rows, d), BF16),
            array((rows, d), BF16),
            array((1, d), F32),
        ],
        [
            pltpu.VMEM((d, d), BF16),
            pltpu.VMEM((d, ff), BF16),
        ],
        2 * rows * d * (d + ff),
    )


def diagonal_sums(strip):
    for s in (64, 32, 16, 8):
        strip = strip[:s] + pltpu.roll(strip[s:], SPAN - s, 1)
    for s in (4, 2, 1):
        strip = strip + pltpu.roll(pltpu.roll(strip, 8 - s, 0), SPAN - s, 1)
    return strip[:1]


def attend_back_kernel(
    keep,
    todo,
    meta,
    qkv_ref,
    dctx_ref,
    qaug_ref,
    kaug_ref,
    dist_ref,
    lse_ref,
    *rest,
):
    grad_ref, table_ref, strip_acc = rest[-3:]
    side = meta[0] if keep else 1 - meta[0]
    count = H // 4
    rows = qkv_ref.shape[0]
    lane = lax.broadcasted_iota(jnp.int32, (PAIR, 128), 1)
    for pair in todo:
        strip_acc[...] = jnp.zeros_like(strip_acc)
        strips = [
            bias_strip(dist_ref[pl.ds(side * 6 + 2 * pair + hh, 1), :]) for hh in range(2)
        ]
        for base in range(0, rows, PAIR):
            block = slice(base, base + PAIR)

            def part(t):
                col = pl.multiple_of(side * 1152 + (t * 3 + pair) * 128, 128)
                return qkv_ref[block, pl.ds(col, 128)]

            q, k, v = part(0), part(1), part(2)
            do = dctx_ref[block, pl.ds(pl.multiple_of(side * 384 + pair * 128, 128), 128)]
            lse = [lse_ref[pl.ds(side * 6 + 2 * pair + hh, 1), block] for hh in range(2)]
            qaug, kaug = qaug_ref[block, :], kaug_ref[block, :]
            k_turned = k.T
            heads = []
            for hh in range(2):
                mine = (lane // 64) == hh
                heads.append(
                    (
                        jnp.where(mine, q, qaug),
                        jnp.where(mine, k, kaug),
                        jnp.where(mine, v, jnp.zeros_like(v)),
                        k_turned[hh * 64 : (hh + 1) * 64, :],
                        strips[hh],
                    )
                )
            cols = [slice((t * count + pair) * 128, (t * count + pair + 1) * 128) for t in range(3)]
            for off, size in GROUPS:
                step = size
                low = lax.broadcasted_iota(jnp.int32, (size, 128), 1) < 64
                dks, dvs = [None, None], [None, None]
                for i0 in range(0, size, step):
                    lo, hi = off + i0, off + i0 + step
                    dqs = []
                    for hh in range(2):
                        qa, ka, va, kt, strip = heads[hh]
                        scores = dot_nt(ka[off : off + size], qa[lo:hi])
                        scores = scores + strip_bias(strip, size, i0, step)
                        probs = jnp.exp(scores - lse[hh][:, lo:hi])
                        d_probs = dot_nt(va[off : off + size], do[lo:hi])
                        dv = dot(probs.astype(BF16), do[lo:hi])
                        center = jnp.sum(probs * d_probs, axis=0, keepdims=True)
                        d_scores = probs * (d_probs - center)
                        for t in range(size // 128):
                            at = (3 - t) * 128 + i0
                            strip_acc[hh, :, at : at + step] += d_scores[t * 128 : (t + 1) * 128]
                        ds_low = d_scores.astype(BF16)
                        dk = dot(ds_low, q[lo:hi])
                        dqs.append(dot(kt[:, off : off + size], ds_low))
                        dks[hh] = dk if dks[hh] is None else dks[hh] + dk
                        dvs[hh] = dv if dvs[hh] is None else dvs[hh] + dv
                    dq = jnp.concatenate(dqs, axis=0).T.astype(BF16)
                    grad_ref[base + lo : base + hi, cols[0]] = dq
                out = slice(base + off, base + off + size)
                grad_ref[out, cols[1]] = jnp.where(low, dks[0], dks[1]).astype(BF16)
                grad_ref[out, cols[2]] = jnp.where(low, dvs[0], dvs[1]).astype(BF16)
        for hh in range(2):
            table_ref[2 * pair + hh : 2 * pair + hh + 1, :] = diagonal_sums(strip_acc[hh])
    if todo[0] == 0:
        table_ref[2 * count :, :] = jnp.zeros((8 - 2 * count, SPAN), F32)


def attend_back_call(meta, qkv, dctx, qaug, kaug, dist, lse, keep, todo, done=()):
    rows, d = dctx.shape
    pairs = rows // PAIR
    count = H // 4
    return call(
        functools.partial(attend_back_kernel, keep, todo),
        "attend_back",
        (meta, qkv, dctx, qaug, kaug, dist, lse),
        done,
        [array((rows, 3 * count * 128), BF16), array((8, SPAN), F32)],
        [pltpu.VMEM((2, 128, SPAN), F32)],
        20 * pairs * len(todo) * 350000 * 128,
        trans=2 * pairs * len(todo) * 350000,
        aliases={7: 0, 8: 1} if done else None,
    )


def in_back_kernel(chunk, tile, meta, own_ref, rec_ref, x_ref, dmid_ref, ext_ref, *rest):
    stay_ref, away_ref, gain_ref, *rest = rest
    refs = rest[: chunk.count]
    dx_ref, extra_ref, w = rest[chunk.count :]
    load_columns(chunk, meta, refs, 0, w.shape[1] // 2, w, own_first=True)
    place = (lax.broadcasted_iota(jnp.int32, (128, SPAN), 1) + 127) % SPAN
    row = lax.broadcasted_iota(jnp.int32, (128, SPAN), 0)
    chosen = (bucket_of(BLOCK - 1 - place) == row).astype(F32)
    found = [
        lax.dot_general(
            r[...],
            chosen,
            (((1,), (1,)), ((), ())),
            precision=lax.Precision.HIGHEST,
            preferred_element_type=F32,
        )[: H // 2]
        for r in (stay_ref, away_ref)
    ]
    first = meta[0] == 0
    extra_ref[...] = jnp.zeros_like(extra_ref)
    extra_ref[16 : 16 + H // 2, :] = jnp.where(first, found[0], found[1])
    extra_ref[16 + H // 2 : 16 + H, :] = jnp.where(first, found[1], found[0])
    rows, d = x_ref.shape
    both = jnp.concatenate([own_ref[...], rec_ref[...]], axis=1)
    for c in range(0, d, 256):
        dx_ref[:, c : c + 256] = dot_nt(both, w[c : c + 256, :])
    gains = []
    for r in range(0, rows, tile):
        span = slice(r, r + tile)
        dn = dx_ref[span, :]
        x = x_ref[span, :].astype(F32)
        scale = lax.rsqrt(jnp.mean(x * x, axis=-1, keepdims=True) + norm_eps)
        back, gain = norm_back(dn, x, ext_ref, 0, scale)
        gains.append(gain)
        dx_ref[span, :] = dmid_ref[span, :] + back
    total = sum(gains)
    for c in range(d // 128):
        extra_ref[c : c + 1, :] = total[:, c * 128 : (c + 1) * 128]
        extra_ref[6 + c : 7 + c, :] = gain_ref[:, c * 128 : (c + 1) * 128]


def in_back_call(meta, own, rec, x, dmid, ext, found, gain, chunk):
    rows, d = x.shape
    return call(
        functools.partial(in_back_kernel, chunk, rows // 4),
        "in_back",
        (meta, own, rec, x, dmid, ext, *found, gain),
        away(chunk.arrays),
        [array((rows, d), F32), array((32, 128), F32)],
        [pltpu.VMEM((d, 3 * d), BF16)],
        6 * rows * d * d,
    )


def mask_lanes(lengths, rows):
    spot = jnp.arange(rows, dtype=jnp.int32)
    within = spot % PAIR
    first = jnp.array([0, 512, 768, 896, 960], jnp.int32)
    slot = jnp.sum((within[:, None] >= first[None, 1:]).astype(jnp.int32), axis=1)
    start = jnp.sum(jnp.where(slot[:, None] == jnp.arange(5)[None], first[None], 0), axis=1)
    docs = jnp.arange(lengths.shape[0], dtype=jnp.int32)
    document = spot // PAIR * 5 + slot
    own = jnp.sum(jnp.where(document[:, None] == docs[None], lengths[None], 0), axis=1)
    live = within - start < own
    late = slot == 4
    lane = jnp.arange(128, dtype=jnp.int32) % 64
    shown = [live & ~late, live & late]
    kaug = jnp.where(
        lane[None] == 0,
        jnp.where(shown[0], 0.0, MASKED)[:, None],
        jnp.where(lane[None] == 1, jnp.where(shown[1], 0.0, MASKED)[:, None], 0.0),
    ).astype(BF16)
    qaug = jnp.where(
        lane[None] == 0,
        jnp.where(late, 0.0, 1.0)[:, None],
        jnp.where(lane[None] == 1, jnp.where(late, 1.0, 0.0)[:, None], 0.0),
    ).astype(BF16)
    return qaug, kaug, live


def placed_rows(vector, me, rows):
    count = vector.shape[0]
    spot = jnp.arange(rows * 128, dtype=jnp.int32)[None] - me * count
    hit = spot == jnp.arange(count, dtype=jnp.int32)[:, None]
    flat = jnp.sum(jnp.where(hit, vector.astype(F32)[:, None], 0.0), axis=0)
    return flat.reshape(rows, 128)


def placed_table(vector, me):
    count = vector.shape[0]
    head = jnp.arange(16, dtype=jnp.int32)[:, None]
    bucket = jnp.arange(128, dtype=jnp.int32)[None]
    entry = jnp.where((head < H) & (bucket < BUCKETS), bucket * H + head, -1) - me * count
    hit = entry[None] == jnp.arange(count, dtype=jnp.int32)[:, None, None]
    return jnp.sum(jnp.where(hit, vector.astype(F32)[:, None, None], 0.0), axis=0)


def local(
    ring,
    ring_c,
    hidden,
    gain_attn,
    rel_table,
    query_weight,
    key_weight,
    value_weight,
    output_weight,
    gain_ffn,
    inner_weight,
    outer_weight,
    lengths,
    cotangent,
):
    rows, d = hidden.shape
    ff = inner_weight.shape[1]
    n = ring.n
    shard_rows = query_weight.shape[0]
    outer_rows = outer_weight.shape[0]
    direct = shard_rows % 16 == 0 and shard_rows >= 32 and outer_rows % 32 == 0
    me = lax.axis_index("fsdp")
    core = lax.axis_index("dp")
    meta = ring.meta()
    meta_c = ring_c.meta()
    h = d // 2

    def half(w, which):
        width = w.shape[1] // 2
        return lax.dynamic_slice_in_dim(w, which * width, width, 1)

    small = jnp.concatenate(
        [
            placed_rows(gain_attn, me, d // 128),
            placed_rows(gain_ffn, me, d // 128),
            jnp.zeros((16 - 2 * (d // 128), 128), F32),
            placed_table(rel_table, me),
        ],
        axis=0,
    ).astype(BF16)
    pack_a = [half(w, core) for w in (query_weight, key_weight, value_weight)]
    if direct:
        pack_a.append(jnp.pad(small, ((0, shard_rows - 32), (0, 0))))
    pack_a = jnp.concatenate(pack_a, axis=1)
    pack_b = jnp.concatenate([half(output_weight, core), half(inner_weight, core)], axis=1)
    pack_c = lax.dynamic_slice_in_dim(
        outer_weight, core * (outer_rows // 2), outer_rows // 2, 0
    )

    def whole_columns(own, rec):
        both = []
        for parts, first in ((own, core == 0), (rec, core == 1)):
            pieces = ring.to_origin(jnp.concatenate(parts, axis=0), first)
            both.append(pieces.reshape(-1, pieces.shape[2]))
        first = jnp.where(core == 0, both[0], both[1])
        second = jnp.where(core == 0, both[1], both[0])
        return jnp.stack([first, second])

    qaug, kaug, live = mask_lanes(lengths, rows)
    g = jnp.where(live[:, None], cotangent, jnp.zeros_like(cotangent))
    if direct:
        move_a, move_b = Gather(ring, pack_a), Gather(ring, pack_b)
        move_c = Gather(ring_c, pack_c)
        move_a.go()
        move_c.go()
        move_a.got, move_c.got = lax.optimization_barrier((move_a.got, move_c.got))
        move_c.join()
        for _ in range(ring.bits - 3):
            move_a.join(meta, meta_c, qaug, kaug, g)
            move_a.go()
        move_a.join()
        for _ in range(ring.bits - 3):
            ready(move_a, move_b)
            move_a.go()
            move_b.go()
            move_a.join()
            move_b.join()
        ready(move_a, move_b)
        move_a.go()
        move_b.go()
        move_a.last, move_b.got = lax.optimization_barrier((move_a.last, move_b.got))
        move_b.join()
        final = move_a.last
        move_b.held, final = lax.optimization_barrier((move_b.held, final))
        move_b.go()
        chunk_a = Pieces(*move_a.finish(), n)
        move_c.held, final = lax.optimization_barrier((move_c.held, final))
        move_c.go()
        ext = None
    else:
        got_c = gather_pieces(ring, pack_c)
        chunk_a = Whole(whole_columns(*gather_pieces(ring, pack_a)))
        chunk_b = Whole(whole_columns(*gather_pieces(ring, pack_b)))
        both = [
            ring.to_origin(jnp.concatenate(parts, axis=0), first)
            for parts, first in zip(got_c, (core == 0, core == 1))
        ]
        first = jnp.where(core == 0, both[0], both[1])
        second = jnp.where(core == 0, both[1], both[0])
        chunk_c = Whole(jnp.stack([first, second], axis=1).reshape(ff, d))
        ext = lax.psum(small.astype(F32), "fsdp")

    qkv, normed, dist, ext = qkv_call(meta, hidden, ext, chunk_a)
    if direct:
        (qkv,) = gather_on((qkv,), move_b, move_c)
        near_b = shift(move_b.held, ring.swap_core())
    ctx, lse = attend_call(meta, qkv, qaug, kaug, dist)
    if direct:
        held_b = move_b.held
        ctx, near_b = gather_on((ctx, near_b), move_b, move_c)
        far_b = shift(move_b.last, ring.swap_core())
        near_c = shift(move_c.held, ring.swap_core())
        chunk_b = Pieces((held_b, move_b.last), (near_b, far_b), n)
    middle, normed2, act, slope = mid_call(meta, ctx, hidden, ext, chunk_b, ff)
    if direct:
        act, near_c, move_c.last = lax.optimization_barrier((act, near_c, move_c.last))
        far_c = shift(move_c.last, ring.swap_core())

    def split_columns(pairs, which):
        full = [jnp.einsum("td,tf->df", a, b, preferred_element_type=F32) for a, b in pairs]
        part = jnp.concatenate(full, axis=1).astype(BF16)
        part = part.reshape(n, d // n, part.shape[1])
        return ring.from_origin(part, which == 0)

    if direct:
        grad_c = outer_grad_call(meta, act, g, n)
        far_c, *grad_c = lax.optimization_barrier((far_c, *grad_c))
        chunk_c = Pieces((move_c.held, move_c.last), (near_c, far_c), n)
    else:
        full = jnp.einsum("tf,td->fd", act, g, preferred_element_type=F32).astype(BF16)
        full = full.reshape(n, 2, outer_rows // 2, d)
        grad_c = [
            ring.from_origin(
                lax.dynamic_index_in_dim(full, which, 1, keepdims=False), which == 0
            )
            for which in (core, 1 - core)
        ]
    red_c = Reduce(ring, *grad_c)
    (act,) = tick((act,), fresh=(red_c,))
    result, d_inner = out_call(meta_c, act, middle, g, slope, chunk_c)
    (d_inner,) = tick((d_inner,), (red_c,))
    d_middle, d_att, d_ctx, grad_gain_f = mid_back_call(meta, d_inner, middle, g, ext, chunk_b)
    (d_att,) = tick((d_att,), (red_c,))
    if direct:
        grad_b = mid_grad_call(meta, normed2, ctx, d_inner, d_att, n)
    else:
        grad_b = [
            split_columns([(ctx, half(d_att, w)), (normed2, half(d_inner, w))], w)
            for w in (core, 1 - core)
        ]
    red_b = Reduce(ring, *grad_b)
    (d_ctx,) = tick((after(d_ctx, *grad_b),), (red_c,), (red_b,))
    back = functools.partial(attend_back_call, meta, qkv)
    masks = (qaug, kaug, dist, lse)
    away, found_away = tick(back(d_ctx, *masks, False, (0, 1, 2)), (red_c, red_b))
    if direct:
        send_a = qkv_grad_call(meta, normed, away, n, 3)
    else:
        send_a = split_columns([(normed, away)], 1 - core)
    d_ctx, send_a = lax.optimization_barrier((d_ctx, send_a))
    red_a = Reduce(ring, None, send_a)
    red_a.go()
    stay, found_stay = tick(back(d_ctx, *masks, True, (0, 1, 2)), (red_b,))
    if red_c.phase == 0:
        stay, sum_c = lax.optimization_barrier((stay, red_c.step(stay)))
    else:
        sum_c = red_c.finish()
    if direct:
        keep_a = qkv_grad_call(meta, normed, stay, n, 2)
    else:
        keep_a = split_columns([(normed, stay)], core)
    red_a.keep = keep_a
    (stay,) = tick((after(stay, keep_a),), (red_a,))
    grad_hidden, extra = in_back_call(
        meta,
        stay,
        away,
        hidden,
        d_middle,
        ext,
        (found_stay, found_away),
        grad_gain_f,
        chunk_a,
    )
    steps = [ring.swap_phase(k) for k in range(ring.bits)] + [ring.swap_core()]
    moved = shift(extra, steps.pop(0))
    while red_a.phase > 0:
        reds = [r for r in (red_a, red_b) if r.phase > 0]
        flat = (extra, moved, *[r.got for r in reds])
        extra, moved, *flat = lax.optimization_barrier(flat)
        for r, got in zip(reds, flat):
            r.got = got
            r.step()
        flat = [extra + moved]
        for r in reds:
            flat += [r.keep, r.away]
        extra, *flat = lax.optimization_barrier(tuple(flat))
        for i, r in enumerate(reds):
            r.keep, r.away = flat[2 * i : 2 * i + 2]
            r.go()
        if len(steps) > red_a.phase + 1:
            extra = extra + shift(extra, steps.pop(0))
        moved = shift(extra, steps.pop(0))
    moved, red_a.got = lax.optimization_barrier((moved, red_a.got))
    extra = extra + moved
    assert not steps
    sum_b = red_b.finish()
    sum_o, sum_b = sum_b[:, :h], sum_b[:, h:]
    sum_a = red_a.finish()

    own = [sum_a, sum_o, sum_b, sum_c]
    other = [shift(s, ring.swap_core()) for s in own]
    low = [jnp.where(core == 0, a, b) for a, b in zip(own, other)]
    high = [jnp.where(core == 0, b, a) for a, b in zip(own, other)]
    grads = [
        jnp.concatenate([low[0][:, t * h : (t + 1) * h], high[0][:, t * h : (t + 1) * h]], axis=1)
        for t in range(3)
    ]
    grad_output = jnp.concatenate([low[1], high[1]], axis=1)
    grad_inner = jnp.concatenate([low[2], high[2]], axis=1)
    grad_outer = jnp.concatenate([low[3], high[3]], axis=0)
    per = d // n
    gain_a = lax.dynamic_slice_in_dim(extra[: d // 128].reshape(-1), me * per, per, 0)
    gain_f = lax.dynamic_slice_in_dim(
        extra[d // 128 : 2 * (d // 128)].reshape(-1), me * per, per, 0
    )
    table = extra[16 : 16 + H, :BUCKETS].T.reshape(-1)
    table = lax.dynamic_slice_in_dim(table, me * rel_table.shape[0], rel_table.shape[0], 0)
    return (
        result,
        grad_hidden,
        gain_a,
        table,
        grads[0],
        grads[1],
        grads[2],
        grad_output,
        gain_f,
        grad_inner,
        grad_outer,
    )


def solution(mesh):
    both = P(("dp", "fsdp"), None)
    line = P("fsdp")
    wide = P("fsdp", None)
    in_specs = (both, line, line, wide, wide, wide, wide, line, wide, wide, P(("dp", "fsdp")), both)
    out_specs = (both, both, line, line, wide, wide, wide, wide, line, wide, wide)
    return jax.shard_map(
        functools.partial(local, Ring(mesh), Ring(mesh, split=True)),
        mesh=mesh,
        in_specs=in_specs,
        out_specs=out_specs,
        check_vma=False,
    )
```
